256 devices in a mesh: segment: 8 (over x, core), expert: 32 (over y, z).
Axes of the slice: x: 4, y: 4, z: 8, core: 2. Of those that a mesh axis runs over, the one named last changes fastest.
Arguments:
- states: bfloat16 [8, 128, 7168], P('segment', 'expert'), may hold values from -6 to 6
- routing: int32 [8, 2, 128, 2], P('segment', None, 'expert'), may hold values from 0 to 7, all different within a row; in each aligned block of 4 rows (0 to 3, 4 to 7, ..., all dimensions but the last counted through in order) at most 2 rows name the same one
- route_weight: bfloat16 [8, 2, 128, 2], P('segment', None, 'expert'), may hold values from 0.19921875 to 1
- norm_gain: float32 [8, 7168], P('segment'), may hold values from 0.1 to 1.9
- gate_proj: bfloat16 [8, 7168, 8192], P('segment', None, 'expert'), may hold values from -0.0625 to 0.0625
- up_proj: bfloat16 [8, 7168, 8192], P('segment', None, 'expert'), may hold values from -0.0625 to 0.0625
- down_proj: bfloat16 [8, 8192, 7168], P('segment', 'expert'), may hold values from -0.1875 to 0.1875
Outputs:
- new_states: bfloat16 [8, 128, 7168], P('segment', 'expert')
The draws below stay inside these ranges and needn't reach their ends.
Inputs may be any that keep to these rules, and one draw needn't show every extreme that they name: `routing`: in each aligned block of 4 rows (the rows of one device for one layer and pass) no expert is named by more than 2 rows, and some block reaches 2; each row names 2 different experts.
All inputs are finite; a program needn't handle non-finite values.
Results may differ from the reference program's by a relative error of at most 0.015.
Values may be sent and summed in bfloat16 or wider, within the bound.
A program may use at most 64 MiB of HBM per device.

```python
import math
import jax
import jax.numpy as jnp
import numpy as np
from jax import lax

D = 7168
HID_DEV = 256
GROUP = 4
TOP = 2
PASSES = 2
RD = 4
EXPERT_HID = 1024
EXPERTS = 8
CAP = 2
ROWS = 128
MB = 8
N_SEGMENT = 8
N_EXPERT = 32


def level_of(rng, extent, cuts, least, top_value):
    def one(dim, blocks):
        steps = jax.random.uniform(jax.random.fold_in(jax.random.fold_in(rng, 6), dim), (blocks,), jnp.float32, least / len(cuts), top_value / len(cuts))
        return jnp.repeat(jnp.exp(steps), extent[dim] // blocks).reshape((-1,) + (1,) * (len(extent) - dim - 1))

    factor_of = one(*cuts[0])
    for cut in cuts[1:]:
        factor_of = factor_of * one(*cut)
    return factor_of


def assign_block(rng, own, number, rows, amount, top, reach, lean):
    ranking = jax.random.permutation(rng, amount)
    packed, usual = load_shares(amount, rows * top, reach, lean, True), load_shares(amount, rows * top, reach, lean, False)
    places = jnp.arange(amount)

    def named(lengths, turn):
        used = int((lengths > 0).sum())
        fixed = max(1, used // 4)
        shifted = fixed + (places - fixed + turn * (used - fixed)) % max(1, amount - fixed)
        return jnp.zeros((amount,), jnp.int32).at[ranking[jnp.where(places < fixed, places, shifted)]].set(jnp.asarray(lengths, jnp.int32))

    lengths = jnp.where(number % 4 == 0, named(packed, number // 4), named(usual, number - number // 4 - 1))
    mixed = jax.random.permutation(jax.random.fold_in(own, 3), amount)
    donor, taker = mixed[0:amount // 2 * 2:2], mixed[1:amount // 2 * 2:2]
    margin = jnp.minimum(lengths[donor] - 1, reach - lengths[taker]) // 2
    margin = jnp.where((donor == ranking[0]) | (taker == ranking[0]) | (lengths[taker] == 0), 0, jnp.maximum(margin, 0))
    shifted = jax.random.randint(jax.random.fold_in(own, 4), (amount // 2,), 0, 1 << 20) % (margin + 1)
    lengths = lengths.at[donor].add(-shifted).at[taker].add(shifted)
    members = jnp.searchsorted(jnp.cumsum(lengths), jnp.arange(rows * top), side="right").astype(jnp.int32)
    table = members.reshape(top, rows).T
    table = table[jax.random.permutation(jax.random.fold_in(own, 1), rows)]
    turn = jax.random.randint(jax.random.fold_in(own, 2), (rows, 1), 0, top)
    return jnp.take_along_axis(table, (jnp.arange(top)[None, :] + turn) % top, axis=1)


def load_shares(count, total, reach, skew, full):
    weights = [(1 << 20) // math.isqrt(standing ** skew) + 1 for standing in range(1, count + 1)]
    largest = reach if full else min(reach, max(-(-total // count), total * weights[0] // sum(weights)))
    least = 1 if total - largest >= count - 1 else 0
    given, surplus = [largest] + [least] * (count - 1), total - largest - least * (count - 1)
    while surplus > 0:
        movable = [i for i in range(1, count) if given[i] < largest] or [i for i in range(1, count) if given[i] < reach]
        whole, left = sum([weights[i] for i in movable]), surplus
        for i in movable:
            addition = min(reach - given[i], max(1, left * weights[i] // whole), surplus)
            given[i] = given[i] + addition
            surplus = surplus - addition
    return np.array(given)


def gaussian(own_key, extent, width, bound, cuts=(), held_as=jnp.bfloat16):
    entries = width * jax.random.normal(own_key, extent, jnp.float32)
    if cuts:
        entries = entries * level_of(own_key, extent, cuts, -0.22, 0.18)
    return jnp.clip(entries, -bound, bound).astype(held_as)


def setup_inputs(seed: int = 0) -> dict:
    keys = jax.random.split(jax.random.key(seed), 8)
    states = gaussian(keys[0], (MB, ROWS, D), 1.0, 6.0, ((0, 8), (1, 32)))
    routing_keys = jax.random.split(jax.random.fold_in(keys[1], 1), MB * PASSES * ROWS // RD)
    routing_turns = jax.random.permutation(jax.random.fold_in(keys[1], 3), MB * PASSES * ROWS // RD)
    routing = jax.vmap(lambda own, number: assign_block(jax.random.fold_in(keys[1], 2), own, number, RD, EXPERTS, TOP, CAP, 2))(routing_keys, routing_turns).reshape((MB, PASSES, ROWS, TOP))
    route_weight = jnp.clip(0.19921875 + 0.80078125 * jax.random.uniform(keys[2], (MB, PASSES, ROWS, TOP), jnp.float32) ** level_of(keys[2], (MB, PASSES, ROWS, TOP), ((0, 8), (2, 32)), -0.2, 0.2), 0.19921875, 1.0).astype(jnp.bfloat16)
    norm_gain = jnp.clip(1.0 + 0.18 * jax.random.normal(keys[3], (MB, D), jnp.float32), 0.1, 1.9)
    gate_proj = gaussian(keys[4], (MB, D, EXPERTS * EXPERT_HID), D ** -0.5, 0.0625, ((0, 8), (2, 32)))
    up_proj = gaussian(keys[5], (MB, D, EXPERTS * EXPERT_HID), D ** -0.5, 0.0625, ((0, 8), (2, 32)))
    down_proj = gaussian(keys[6], (MB, EXPERTS * EXPERT_HID, D), EXPERT_HID ** -0.5, 0.1875, ((0, 8), (1, 32)))
    return {"states": states, "routing": routing, "route_weight": route_weight, "norm_gain": norm_gain, "gate_proj": gate_proj, "up_proj": up_proj, "down_proj": down_proj}


def apply_layer(current, routes, weights_now, gain_row, gate_mat, up_mat, down_mat):
    hidden_f = current.astype(jnp.float32)
    inv_rms = lax.rsqrt(lax.optimization_barrier(jnp.mean(hidden_f * hidden_f, axis=1, keepdims=True)) + 1e-06)
    normed = (hidden_f * inv_rms * gain_row).astype(jnp.bfloat16)
    slot_count = N_EXPERT * CAP
    summed = jnp.zeros(hidden_f.shape, jnp.float32)
    for expert in range(EXPERTS):
        picked = routes == expert
        member = jnp.any(picked, axis=1)
        weight_row = lax.optimization_barrier(jnp.sum(jnp.where(picked, weights_now.astype(jnp.float32), jnp.float32(0.0)), axis=1))
        where_rows = jnp.nonzero(member, size=slot_count, fill_value=0)[0]
        is_valid = jnp.arange(slot_count) < jnp.sum(member.astype(jnp.int32))
        chosen = normed[where_rows]
        first_col = expert * EXPERT_HID
        gate_cols = gate_mat[:, first_col:first_col + EXPERT_HID]
        up_cols = up_mat[:, first_col:first_col + EXPERT_HID]
        down_rows = down_mat[first_col:first_col + EXPERT_HID, :]
        gated = jnp.dot(chosen, gate_cols, preferred_element_type=jnp.float32)
        up_part = jnp.dot(chosen, up_cols, preferred_element_type=jnp.float32)
        inner_act = (jax.nn.silu(gated) * up_part).astype(jnp.bfloat16)
        slice_terms = jnp.einsum('sgh,ghd->sgd', inner_act.reshape(slot_count, GROUP, HID_DEV).astype(jnp.float32), down_rows.reshape(GROUP, HID_DEV, D).astype(jnp.float32))
        slot_weight = jnp.where(is_valid, weight_row[where_rows], jnp.float32(0.0))
        term_vals = (slot_weight[:, None, None] * slice_terms).astype(jnp.bfloat16).astype(jnp.float32)
        summed = summed.at[where_rows].add(lax.optimization_barrier(jnp.sum(term_vals, axis=1)))
    return (hidden_f + summed).astype(jnp.bfloat16)

def reference(states, routing, route_weight, norm_gain, gate_proj, up_proj, down_proj):
    outputs = []
    for micro_idx in range(N_SEGMENT):
        current = states[micro_idx]
        for offset in range(PASSES):
            layer_no = (micro_idx + offset) % N_SEGMENT
            current = apply_layer(current, routing[layer_no, offset], route_weight[layer_no, offset], norm_gain[layer_no], gate_proj[layer_no], up_proj[layer_no], down_proj[layer_no])
        outputs.append(current)
    return jnp.roll(jnp.stack(outputs), PASSES, axis=0)
```

```python
import jax
import jax.numpy as jnp
from jax import lax
from jax.sharding import PartitionSpec as P

GROUP = 4


def shifted(value, axis, steps):
    count = lax.axis_size(axis)
    pairs = [(source, (source + steps) % count) for source in range(count)]
    return lax.ppermute(value, axis, pairs)


def on_device(states, routing, route_weight, norm_gain, gate_proj, up_proj, down_proj):
    owners = lax.axis_size("expert")
    experts = owners // GROUP
    passes_count = routing.shape[1]
    row_dev = states.shape[1]
    capacity = 2
    gain_row = norm_gain[0]
    gate_mat = gate_proj[0]
    up_mat = up_proj[0]
    down_mat = down_proj[0]
    expert_ids = jnp.arange(experts, dtype=jnp.int32)
    slot_ids = jnp.arange(capacity, dtype=jnp.int32)
    owner_expert = jnp.arange(owners, dtype=jnp.int32) // GROUP

    current = states[0]
    for step_no in range(passes_count):
        chosen = routing[0, step_no]
        weights_now = route_weight[0, step_no]
        picked = chosen[:, :, None] == expert_ids[None, None, :]
        member = jnp.any(picked, axis=1)
        dense_weight = jnp.sum(
            jnp.where(picked, weights_now[:, :, None].astype(jnp.float32), jnp.float32(0.0)), axis=1
        )
        slot_rank = jnp.cumsum(member.astype(jnp.int32), axis=0) - 1
        placer = member.T[:, None, :] & (slot_rank.T[:, None, :] == slot_ids[None, :, None])
        placer_f = placer.astype(jnp.bfloat16)

        current_f = current.astype(jnp.float32)
        inv_rms = lax.rsqrt(jnp.mean(current_f * current_f, axis=1, keepdims=True) + 1e-06)
        normed = (current_f * inv_rms * gain_row).astype(jnp.bfloat16)

        packed = jnp.einsum(
            "jcr,rd->jcd", placer_f, normed, preferred_element_type=jnp.float32
        ).astype(jnp.bfloat16)
        packed_weight = jnp.sum(
            jnp.where(placer, dense_weight.T[:, None, :], jnp.float32(0.0)), axis=2
        ).astype(jnp.bfloat16)
        send_rows = packed[owner_expert]
        send_weight = packed_weight[owner_expert]
        got_rows = lax.all_to_all(send_rows, "expert", 0, 0, tiled=True)
        got_weight = lax.all_to_all(send_weight, "expert", 0, 0, tiled=True)

        flat_rows = got_rows.reshape(owners * capacity, -1)
        gated = jnp.dot(flat_rows, gate_mat, preferred_element_type=jnp.float32)
        up_part = jnp.dot(flat_rows, up_mat, preferred_element_type=jnp.float32)
        inner_act = (jax.nn.silu(gated) * up_part).astype(jnp.bfloat16)
        partial_out = jnp.dot(inner_act, down_mat, preferred_element_type=jnp.float32)
        scaled = got_weight.reshape(-1, 1).astype(jnp.float32) * partial_out
        terms = scaled.astype(jnp.bfloat16).reshape(owners, capacity, -1)

        back = lax.all_to_all(terms, "expert", 0, 0, tiled=True)
        back_placer = placer_f[owner_expert]
        summed = jnp.einsum(
            "ocr,ocd->rd", back_placer, back, preferred_element_type=jnp.float32
        )
        updated = (current_f + summed).astype(jnp.bfloat16)
        current = shifted(updated, "segment", 1)
    return current[None]


def solution(mesh):
    return jax.shard_map(
        on_device,
        mesh=mesh,
        in_specs=(
            P("segment", "expert", None),
            P("segment", None, "expert", None),
            P("segment", None, "expert", None),
            P("segment", None),
            P("segment", None, "expert"),
            P("segment", None, "expert"),
            P("segment", "expert", None),
        ),
        out_specs=P("segment", "expert", None),
        check_vma=False,
    )
```

```python
import functools

import jax
import jax.numpy as jnp
from jax import lax
from jax.experimental import pallas as pl
from jax.experimental.pallas import tpu as pltpu
from jax.sharding import PartitionSpec as P

GROUP = 4
LANES = 128


def exchange_kernel(count, x_ref, y_ref, send_sem, recv_sem, own_sem):
    me = lax.axis_index("expert")
    seg = lax.axis_index("segment")

    barrier = pltpu.get_barrier_semaphore()

    def greet(d, carry):
        peer = lax.rem(me + d, count)
        pl.semaphore_signal(
            barrier, inc=1, device_id=(seg, peer), device_id_type=pl.DeviceIdType.MESH
        )
        return carry

    lax.fori_loop(1, count, greet, 0)
    pl.semaphore_wait(barrier, count - 1)

    own = pltpu.make_async_copy(x_ref.at[me], y_ref.at[me], own_sem)
    own.start()

    def outgoing(peer):
        return pltpu.make_async_remote_copy(
            src_ref=x_ref.at[peer],
            dst_ref=y_ref.at[me],
            send_sem=send_sem.at[peer],
            recv_sem=recv_sem.at[me],
            device_id=(seg, peer),
            device_id_type=pl.DeviceIdType.MESH,
        )

    def incoming(peer):
        return pltpu.make_async_remote_copy(
            src_ref=x_ref.at[me],
            dst_ref=y_ref.at[peer],
            send_sem=send_sem.at[peer],
            recv_sem=recv_sem.at[peer],
            device_id=(seg, peer),
            device_id_type=pl.DeviceIdType.MESH,
        )

    def send(d, carry):
        outgoing(lax.rem(me + d, count)).start()
        return carry

    lax.fori_loop(1, count, send, 0)

    def finish(d, carry):
        outgoing(lax.rem(me + d, count)).wait_send()
        incoming(lax.rem(me + count - d, count)).wait_recv()
        return carry

    lax.fori_loop(1, count, finish, 0)
    own.wait()


def exchange(x, collective_id):
    count = x.shape[0]
    return pl.pallas_call(
        functools.partial(exchange_kernel, count),
        out_shape=jax.ShapeDtypeStruct(x.shape, x.dtype),
        in_specs=[pl.BlockSpec(memory_space=pl.ANY)],
        out_specs=pl.BlockSpec(memory_space=pl.ANY),
        scratch_shapes=[
            pltpu.SemaphoreType.DMA((count,)),
            pltpu.SemaphoreType.DMA((count,)),
            pltpu.SemaphoreType.DMA,
        ],
        compiler_params=pltpu.CompilerParams(collective_id=collective_id, has_side_effects=True),
    )(x)


def shifted(value, axis, steps):
    count = lax.axis_size(axis)
    pairs = [(source, (source + steps) % count) for source in range(count)]
    return lax.ppermute(value, axis, pairs)


def on_device(states, routing, route_weight, norm_gain, gate_proj, up_proj, down_proj):
    owners = lax.axis_size("expert")
    experts = owners // GROUP
    passes_count = routing.shape[1]
    row_dev = states.shape[1]
    capacity = 2
    gain_row = norm_gain[0]
    gate_mat = gate_proj[0]
    up_mat = up_proj[0]
    down_mat = down_proj[0]
    expert_ids = jnp.arange(experts, dtype=jnp.int32)
    slot_ids = jnp.arange(capacity, dtype=jnp.int32)
    owner_expert = jnp.arange(owners, dtype=jnp.int32) // GROUP

    current = states[0]
    for step_no in range(passes_count):
        chosen = routing[0, step_no]
        weights_now = route_weight[0, step_no]
        picked = chosen[:, :, None] == expert_ids[None, None, :]
        member = jnp.any(picked, axis=1)
        dense_weight = jnp.sum(
            jnp.where(picked, weights_now[:, :, None].astype(jnp.float32), jnp.float32(0.0)), axis=1
        )
        slot_rank = jnp.cumsum(member.astype(jnp.int32), axis=0) - 1
        placer = member.T[:, None, :] & (slot_rank.T[:, None, :] == slot_ids[None, :, None])
        placer_f = placer.astype(jnp.bfloat16)

        current_f = current.astype(jnp.float32)
        inv_rms = lax.rsqrt(jnp.mean(current_f * current_f, axis=1, keepdims=True) + 1e-06)
        normed = (current_f * inv_rms * gain_row).astype(jnp.bfloat16)

        packed = jnp.einsum(
            "jcr,rd->jcd", placer_f, normed, preferred_element_type=jnp.float32
        ).astype(jnp.bfloat16)
        packed_weight = jnp.sum(
            jnp.where(placer, dense_weight.T[:, None, :], jnp.float32(0.0)), axis=2
        ).astype(jnp.bfloat16)
        weight_block = jnp.broadcast_to(packed_weight[:, :, None], packed_weight.shape + (LANES,))
        with_weight = jnp.concatenate([packed, weight_block], axis=2)
        send_rows = jnp.broadcast_to(
            with_weight[:, None], (experts, GROUP) + with_weight.shape[1:]
        ).reshape((owners,) + with_weight.shape[1:])
        got = exchange(send_rows, 0)
        model_dim = normed.shape[1]
        flat_rows = got[:, :, :model_dim].reshape(owners * capacity, model_dim)
        got_weight = got[:, :, model_dim]
        gated = jnp.dot(flat_rows, gate_mat, preferred_element_type=jnp.float32)
        up_part = jnp.dot(flat_rows, up_mat, preferred_element_type=jnp.float32)
        inner_act = (jax.nn.silu(gated) * up_part).astype(jnp.bfloat16)
        partial_out = jnp.dot(inner_act, down_mat, preferred_element_type=jnp.float32)
        scaled = got_weight.reshape(-1, 1).astype(jnp.float32) * partial_out
        terms = scaled.astype(jnp.bfloat16).reshape(owners, capacity, -1)

        back = exchange(terms, 1)
        back_placer = placer_f[owner_expert]
        summed = jnp.einsum(
            "ocr,ocd->rd", back_placer, back, preferred_element_type=jnp.float32
        )
        updated = (current_f + summed).astype(jnp.bfloat16)
        current = shifted(updated, "segment", 1)
    return current[None]


def solution(mesh):
    return jax.shard_map(
        on_device,
        mesh=mesh,
        in_specs=(
            P("segment", "expert", None),
            P("segment", None, "expert", None),
            P("segment", None, "expert", None),
            P("segment", None),
            P("segment", None, "expert"),
            P("segment", None, "expert"),
            P("segment", "expert", None),
        ),
        out_specs=P("segment", "expert", None),
        check_vma=False,
    )
```

```python
import functools

import jax
import jax.numpy as jnp
from jax import lax
from jax.experimental import pallas as pl
from jax.experimental.pallas import tpu as pltpu
from jax.sharding import PartitionSpec as P

GROUP = 4


def exchange_kernel(count, spread, x_ref, y_ref, send_sem, recv_sem, own_sem):
    me = lax.axis_index("expert")
    seg = lax.axis_index("segment")

    barrier = pltpu.get_barrier_semaphore()

    def greet(d, carry):
        peer = lax.rem(me + d, count)
        pl.semaphore_signal(
            barrier, inc=1, device_id=(seg, peer), device_id_type=pl.DeviceIdType.MESH
        )
        return carry

    lax.fori_loop(1, count, greet, 0)
    pl.semaphore_wait(barrier, count - 1)

    own = pltpu.make_async_copy(x_ref.at[me // spread], y_ref.at[me], own_sem)
    own.start()

    def outgoing(peer):
        return pltpu.make_async_remote_copy(
            src_ref=x_ref.at[peer // spread],
            dst_ref=y_ref.at[me],
            send_sem=send_sem.at[peer],
            recv_sem=recv_sem.at[me],
            device_id=(seg, peer),
            device_id_type=pl.DeviceIdType.MESH,
        )

    def incoming(peer):
        return pltpu.make_async_remote_copy(
            src_ref=x_ref.at[me // spread],
            dst_ref=y_ref.at[peer],
            send_sem=send_sem.at[peer],
            recv_sem=recv_sem.at[peer],
            device_id=(seg, peer),
            device_id_type=pl.DeviceIdType.MESH,
        )

    def send(d, carry):
        outgoing(lax.rem(me + d, count)).start()
        return carry

    lax.fori_loop(1, count, send, 0)

    def finish(d, carry):
        outgoing(lax.rem(me + d, count)).wait_send()
        incoming(lax.rem(me + count - d, count)).wait_recv()
        return carry

    lax.fori_loop(1, count, finish, 0)
    own.wait()


def exchange(x, count, collective_id):
    spread = count // x.shape[0]
    return pl.pallas_call(
        functools.partial(exchange_kernel, count, spread),
        out_shape=jax.ShapeDtypeStruct((count,) + x.shape[1:], x.dtype),
        in_specs=[pl.BlockSpec(memory_space=pl.ANY)],
        out_specs=pl.BlockSpec(memory_space=pl.ANY),
        scratch_shapes=[
            pltpu.SemaphoreType.DMA((count,)),
            pltpu.SemaphoreType.DMA((count,)),
            pltpu.SemaphoreType.DMA,
        ],
        compiler_params=pltpu.CompilerParams(collective_id=collective_id, has_side_effects=True),
    )(x)


def shifted(value, axis, steps):
    count = lax.axis_size(axis)
    pairs = [(source, (source + steps) % count) for source in range(count)]
    return lax.ppermute(value, axis, pairs)


def on_device(states, routing, route_weight, norm_gain, gate_proj, up_proj, down_proj):
    owners = lax.axis_size("expert")
    experts = owners // GROUP
    passes_count = routing.shape[1]
    row_dev = states.shape[1]
    capacity = 2
    gain_row = norm_gain[0]
    gate_mat = gate_proj[0]
    up_mat = up_proj[0]
    down_mat = down_proj[0]
    expert_ids = jnp.arange(experts, dtype=jnp.int32)
    slot_ids = jnp.arange(capacity, dtype=jnp.int32)
    owner_expert = jnp.arange(owners, dtype=jnp.int32) // GROUP

    current = states[0]
    for step_no in range(passes_count):
        chosen = routing[0, step_no]
        weights_now = route_weight[0, step_no]
        picked = chosen[:, :, None] == expert_ids[None, None, :]
        member = jnp.any(picked, axis=1)
        dense_weight = jnp.sum(
            jnp.where(picked, weights_now[:, :, None].astype(jnp.float32), jnp.float32(0.0)), axis=1
        )
        slot_rank = jnp.cumsum(member.astype(jnp.int32), axis=0) - 1
        placer = member.T[:, None, :] & (slot_rank.T[:, None, :] == slot_ids[None, :, None])
        placer_f = placer.astype(jnp.bfloat16)

        current_f = current.astype(jnp.float32)
        inv_rms = lax.rsqrt(jnp.mean(current_f * current_f, axis=1, keepdims=True) + 1e-06)
        normed = (current_f * inv_rms * gain_row).astype(jnp.bfloat16)

        packed = jnp.einsum(
            "jcr,rd->jcd", placer_f, normed, preferred_element_type=jnp.float32
        ).astype(jnp.bfloat16)
        packed_weight = jnp.sum(
            jnp.where(placer, dense_weight.T[:, None, :], jnp.float32(0.0)), axis=2
        )
        got = exchange(packed, owners, 0)
        flat_rows = got.reshape(owners * capacity, -1)
        gated = jnp.dot(flat_rows, gate_mat, preferred_element_type=jnp.float32)
        up_part = jnp.dot(flat_rows, up_mat, preferred_element_type=jnp.float32)
        inner_act = (jax.nn.silu(gated) * up_part).astype(jnp.bfloat16)
        partial_out = jnp.dot(inner_act, down_mat, preferred_element_type=jnp.float32)
        terms = partial_out.astype(jnp.bfloat16).reshape(owners, capacity, -1)

        back = exchange(terms, owners, 1)
        slot_weight = jnp.where(placer, packed_weight[:, :, None], jnp.float32(0.0))
        back_weight = slot_weight[owner_expert].astype(jnp.bfloat16)
        summed = jnp.einsum(
            "ocr,ocd->rd", back_weight, back, preferred_element_type=jnp.float32
        )
        updated = (current_f + summed).astype(jnp.bfloat16)
        current = shifted(updated, "segment", 1)
    return current[None]


def solution(mesh):
    return jax.shard_map(
        on_device,
        mesh=mesh,
        in_specs=(
            P("segment", "expert", None),
            P("segment", None, "expert", None),
            P("segment", None, "expert", None),
            P("segment", None),
            P("segment", None, "expert"),
            P("segment", None, "expert"),
            P("segment", "expert", None),
        ),
        out_specs=P("segment", "expert", None),
        check_vma=False,
    )
```

```python
import functools

import jax
import jax.numpy as jnp
from jax import lax
from jax.experimental import pallas as pl
from jax.experimental.pallas import tpu as pltpu
from jax.sharding import PartitionSpec as P

GROUP = 4


def exchange_kernel(count, spread, shift, x_ref, y_ref, send_sem, recv_sem, own_sem):
    me = lax.axis_index("expert")
    seg = lax.axis_index("segment")
    sections = lax.axis_size("segment")
    ahead = lax.rem(seg + shift, sections)
    behind = lax.rem(seg + sections - shift, sections)
    first = 1 if shift == 0 else 0

    barrier = pltpu.get_barrier_semaphore()

    def greet(d, carry):
        peer = lax.rem(me + d, count)
        pl.semaphore_signal(
            barrier, inc=1, device_id=(ahead, peer), device_id_type=pl.DeviceIdType.MESH
        )
        if shift != 0:
            pl.semaphore_signal(
                barrier, inc=1, device_id=(behind, peer), device_id_type=pl.DeviceIdType.MESH
            )
        return carry

    lax.fori_loop(first, count, greet, 0)
    pl.semaphore_wait(barrier, (count - first) * (1 if shift == 0 else 2))

    if shift == 0:
        own = pltpu.make_async_copy(x_ref.at[me // spread], y_ref.at[me], own_sem)
        own.start()

    def outgoing(peer):
        return pltpu.make_async_remote_copy(
            src_ref=x_ref.at[peer // spread],
            dst_ref=y_ref.at[me],
            send_sem=send_sem.at[peer],
            recv_sem=recv_sem.at[me],
            device_id=(ahead, peer),
            device_id_type=pl.DeviceIdType.MESH,
        )

    def incoming(peer):
        return pltpu.make_async_remote_copy(
            src_ref=x_ref.at[me // spread],
            dst_ref=y_ref.at[peer],
            send_sem=send_sem.at[peer],
            recv_sem=recv_sem.at[peer],
            device_id=(behind, peer),
            device_id_type=pl.DeviceIdType.MESH,
        )

    def send(d, carry):
        outgoing(lax.rem(me + d, count)).start()
        return carry

    lax.fori_loop(first, count, send, 0)

    def finish(d, carry):
        outgoing(lax.rem(me + d, count)).wait_send()
        incoming(lax.rem(me + count - d, count)).wait_recv()
        return carry

    lax.fori_loop(first, count, finish, 0)
    if shift == 0:
        own.wait()


def exchange(x, count, shift, collective_id):
    spread = count // x.shape[0]
    return pl.pallas_call(
        functools.partial(exchange_kernel, count, spread, shift),
        out_shape=jax.ShapeDtypeStruct((count,) + x.shape[1:], x.dtype),
        in_specs=[pl.BlockSpec(memory_space=pl.ANY)],
        out_specs=pl.BlockSpec(memory_space=pl.ANY),
        scratch_shapes=[
            pltpu.SemaphoreType.DMA((count,)),
            pltpu.SemaphoreType.DMA((count,)),
            pltpu.SemaphoreType.DMA,
        ],
        compiler_params=pltpu.CompilerParams(collective_id=collective_id, has_side_effects=True),
    )(x)


def shifted(value, axis, steps):
    count = lax.axis_size(axis)
    pairs = [(source, (source + steps) % count) for source in range(count)]
    return lax.ppermute(value, axis, pairs)


def on_device(states, routing, route_weight, norm_gain, gate_proj, up_proj, down_proj):
    owners = lax.axis_size("expert")
    experts = owners // GROUP
    passes_count = routing.shape[1]
    row_dev = states.shape[1]
    capacity = 2
    gain_row = norm_gain[0]
    gate_mat = gate_proj[0]
    up_mat = up_proj[0]
    down_mat = down_proj[0]
    expert_ids = jnp.arange(experts, dtype=jnp.int32)
    slot_ids = jnp.arange(capacity, dtype=jnp.int32)
    owner_expert = jnp.arange(owners, dtype=jnp.int32) // GROUP

    current = states[0]
    for step_no in range(passes_count):
        chosen = routing[0, step_no]
        weights_now = route_weight[0, step_no]
        picked = chosen[:, :, None] == expert_ids[None, None, :]
        member = jnp.any(picked, axis=1)
        dense_weight = jnp.sum(
            jnp.where(picked, weights_now[:, :, None].astype(jnp.float32), jnp.float32(0.0)), axis=1
        )
        slot_rank = jnp.cumsum(member.astype(jnp.int32), axis=0) - 1
        placer = member.T[:, None, :] & (slot_rank.T[:, None, :] == slot_ids[None, :, None])
        placer_f = placer.astype(jnp.bfloat16)

        current_f = current.astype(jnp.float32)
        inv_rms = lax.rsqrt(jnp.mean(current_f * current_f, axis=1, keepdims=True) + 1e-06)
        normed = (current_f * inv_rms * gain_row).astype(jnp.bfloat16)

        packed = jnp.einsum(
            "jcr,rd->jcd", placer_f, normed, preferred_element_type=jnp.float32
        ).astype(jnp.bfloat16)
        packed_weight = jnp.sum(
            jnp.where(placer, dense_weight.T[:, None, :], jnp.float32(0.0)), axis=2
        )
        got = exchange(packed, owners, 0, 0)
        flat_rows = got.reshape(owners * capacity, -1)
        gated = jnp.dot(flat_rows, gate_mat, preferred_element_type=jnp.float32)
        up_part = jnp.dot(flat_rows, up_mat, preferred_element_type=jnp.float32)
        inner_act = (jax.nn.silu(gated) * up_part).astype(jnp.bfloat16)
        partial_out = jnp.dot(inner_act, down_mat, preferred_element_type=jnp.float32)
        terms = partial_out.astype(jnp.bfloat16).reshape(owners, capacity, -1)

        back = exchange(terms, owners, 1, 1 + step_no)
        slot_weight = jnp.where(placer, packed_weight[:, :, None], jnp.float32(0.0))
        back_weight = shifted(slot_weight[owner_expert].astype(jnp.bfloat16), "segment", 1)
        moved = shifted(current, "segment", 1)
        summed = jnp.einsum(
            "ocr,ocd->rd", back_weight, back, preferred_element_type=jnp.float32
        )
        current = (moved.astype(jnp.float32) + summed).astype(jnp.bfloat16)
    return current[None]


def solution(mesh):
    return jax.shard_map(
        on_device,
        mesh=mesh,
        in_specs=(
            P("segment", "expert", None),
            P("segment", None, "expert", None),
            P("segment", None, "expert", None),
            P("segment", None),
            P("segment", None, "expert"),
            P("segment", None, "expert"),
            P("segment", "expert", None),
        ),
        out_specs=P("segment", "expert", None),
        check_vma=False,
    )
```

```python
import functools

import jax
import jax.numpy as jnp
from jax import lax
from jax.experimental import pallas as pl
from jax.experimental.pallas import tpu as pltpu
from jax.sharding import PartitionSpec as P

GROUP = 4


def exchange_kernel(count, spread, x_ref, y_ref, send_sem, recv_sem, own_sem):
    me = lax.axis_index("expert")
    seg = lax.axis_index("segment")

    barrier = pltpu.get_barrier_semaphore()

    def greet(d, carry):
        peer = lax.rem(me + d, count)
        pl.semaphore_signal(
            barrier, inc=1, device_id=(seg, peer), device_id_type=pl.DeviceIdType.MESH
        )
        return carry

    lax.fori_loop(1, count, greet, 0)
    pl.semaphore_wait(barrier, count - 1)

    own = pltpu.make_async_copy(x_ref.at[me // spread], y_ref.at[me], own_sem)
    own.start()

    def outgoing(peer):
        return pltpu.make_async_remote_copy(
            src_ref=x_ref.at[peer // spread],
            dst_ref=y_ref.at[me],
            send_sem=send_sem.at[peer],
            recv_sem=recv_sem.at[me],
            device_id=(seg, peer),
            device_id_type=pl.DeviceIdType.MESH,
        )

    def incoming(peer):
        return pltpu.make_async_remote_copy(
            src_ref=x_ref.at[me // spread],
            dst_ref=y_ref.at[peer],
            send_sem=send_sem.at[peer],
            recv_sem=recv_sem.at[peer],
            device_id=(seg, peer),
            device_id_type=pl.DeviceIdType.MESH,
        )

    def send(d, carry):
        outgoing(lax.rem(me + d, count)).start()
        return carry

    lax.fori_loop(1, count, send, 0)

    def finish(d, carry):
        outgoing(lax.rem(me + d, count)).wait_send()
        incoming(lax.rem(me + count - d, count)).wait_recv()
        return carry

    lax.fori_loop(1, count, finish, 0)
    own.wait()


def exchange(x, count, collective_id):
    spread = count // x.shape[0]
    return pl.pallas_call(
        functools.partial(exchange_kernel, count, spread),
        out_shape=jax.ShapeDtypeStruct((count,) + x.shape[1:], x.dtype),
        in_specs=[pl.BlockSpec(memory_space=pl.ANY)],
        out_specs=pl.BlockSpec(memory_space=pl.ANY),
        scratch_shapes=[
            pltpu.SemaphoreType.DMA((count,)),
            pltpu.SemaphoreType.DMA((count,)),
            pltpu.SemaphoreType.DMA,
        ],
        compiler_params=pltpu.CompilerParams(collective_id=collective_id, has_side_effects=True),
    )(x)


def ffn_kernel(x_ref, g_ref, u_ref, d_ref, o_ref, acc_g, acc_u):
    k = pl.program_id(0)

    @pl.when(k == 0)
    def _():
        acc_g[...] = jnp.zeros_like(acc_g)
        acc_u[...] = jnp.zeros_like(acc_u)

    for c in range(x_ref.shape[1]):
        xc = x_ref[:, c, :]
        acc_g[c] += jnp.dot(xc, g_ref[...], preferred_element_type=jnp.float32)
        acc_u[c] += jnp.dot(xc, u_ref[...], preferred_element_type=jnp.float32)

    @pl.when(k == pl.num_programs(0) - 1)
    def _():
        for c in range(x_ref.shape[1]):
            g = acc_g[c]
            inner = (g / (1.0 + jnp.exp(-g)) * acc_u[c]).astype(jnp.bfloat16)
            o_ref[:, c, :] = jnp.dot(
                inner, d_ref[...], preferred_element_type=jnp.float32
            ).astype(o_ref.dtype)


def expert_ffn(x, gate_mat, up_mat, down_mat):
    sources, slots, model_dim = x.shape
    hidden = gate_mat.shape[1]
    chunk = 1024
    rows = sources * slots
    return pl.pallas_call(
        ffn_kernel,
        grid=(model_dim // chunk,),
        in_specs=[
            pl.BlockSpec((sources, slots, chunk), lambda k: (0, 0, k)),
            pl.BlockSpec((chunk, hidden), lambda k: (k, 0)),
            pl.BlockSpec((chunk, hidden), lambda k: (k, 0)),
            pl.BlockSpec((hidden, model_dim), lambda k: (0, 0)),
        ],
        out_specs=pl.BlockSpec((sources, slots, model_dim), lambda k: (0, 0, 0)),
        out_shape=jax.ShapeDtypeStruct(x.shape, jnp.bfloat16),
        scratch_shapes=[
            pltpu.VMEM((slots, sources, hidden), jnp.float32),
            pltpu.VMEM((slots, sources, hidden), jnp.float32),
        ],
        cost_estimate=pl.CostEstimate(
            flops=6 * rows * model_dim * hidden,
            transcendentals=rows * hidden,
            bytes_accessed=3 * model_dim * hidden * 2 + 2 * rows * model_dim * 2,
        ),
    )(x, gate_mat, up_mat, down_mat)


def shifted(value, axis, steps):
    count = lax.axis_size(axis)
    pairs = [(source, (source + steps) % count) for source in range(count)]
    return lax.ppermute(value, axis, pairs)


def on_device(states, routing, route_weight, norm_gain, gate_proj, up_proj, down_proj):
    owners = lax.axis_size("expert")
    experts = owners // GROUP
    passes_count = routing.shape[1]
    row_dev = states.shape[1]
    capacity = 2
    gain_row = norm_gain[0]
    gate_mat = gate_proj[0]
    up_mat = up_proj[0]
    down_mat = down_proj[0]
    expert_ids = jnp.arange(experts, dtype=jnp.int32)
    slot_ids = jnp.arange(capacity, dtype=jnp.int32)
    owner_expert = jnp.arange(owners, dtype=jnp.int32) // GROUP

    current = states[0]
    for step_no in range(passes_count):
        chosen = routing[0, step_no]
        weights_now = route_weight[0, step_no]
        picked = chosen[:, :, None] == expert_ids[None, None, :]
        member = jnp.any(picked, axis=1)
        dense_weight = jnp.sum(
            jnp.where(picked, weights_now[:, :, None].astype(jnp.float32), jnp.float32(0.0)), axis=1
        )
        slot_rank = jnp.cumsum(member.astype(jnp.int32), axis=0) - 1
        placer = member.T[:, None, :] & (slot_rank.T[:, None, :] == slot_ids[None, :, None])
        placer_f = placer.astype(jnp.bfloat16)

        current_f = current.astype(jnp.float32)
        inv_rms = lax.rsqrt(jnp.mean(current_f * current_f, axis=1, keepdims=True) + 1e-06)
        normed = (current_f * inv_rms * gain_row).astype(jnp.bfloat16)

        packed = jnp.einsum(
            "jcr,rd->jcd", placer_f, normed, preferred_element_type=jnp.float32
        ).astype(jnp.bfloat16)
        packed_weight = jnp.sum(
            jnp.where(placer, dense_weight.T[:, None, :], jnp.float32(0.0)), axis=2
        )
        got = exchange(packed, owners, 0)
        terms = expert_ffn(got, gate_mat, up_mat, down_mat)

        back = exchange(terms, owners, 1)
        slot_weight = jnp.where(placer, packed_weight[:, :, None], jnp.float32(0.0))
        back_weight = slot_weight[owner_expert].astype(jnp.bfloat16)
        summed = jnp.einsum(
            "ocr,ocd->rd", back_weight, back, preferred_element_type=jnp.float32
        )
        updated = (current_f + summed).astype(jnp.bfloat16)
        current = shifted(updated, "segment", 1)
    return current[None]


def solution(mesh):
    return jax.shard_map(
        on_device,
        mesh=mesh,
        in_specs=(
            P("segment", "expert", None),
            P("segment", None, "expert", None),
            P("segment", None, "expert", None),
            P("segment", None),
            P("segment", None, "expert"),
            P("segment", None, "expert"),
            P("segment", "expert", None),
        ),
        out_specs=P("segment", "expert", None),
        check_vma=False,
    )
```

```python
import functools

import jax
import jax.numpy as jnp
from jax import lax
from jax.experimental import pallas as pl
from jax.experimental.pallas import tpu as pltpu
from jax.sharding import PartitionSpec as P

GROUP = 4


def exchange_kernel(count, spread, x_ref, y_ref, send_sem, recv_sem, own_sem):
    me = lax.axis_index("expert")
    seg = lax.axis_index("segment")

    barrier = pltpu.get_barrier_semaphore()

    def greet(d, carry):
        peer = lax.rem(me + d, count)
        pl.semaphore_signal(
            barrier, inc=1, device_id=(seg, peer), device_id_type=pl.DeviceIdType.MESH
        )
        return carry

    lax.fori_loop(1, count, greet, 0)
    pl.semaphore_wait(barrier, count - 1)

    own = pltpu.make_async_copy(x_ref.at[me // spread], y_ref.at[me], own_sem)
    own.start()

    def outgoing(peer):
        return pltpu.make_async_remote_copy(
            src_ref=x_ref.at[peer // spread],
            dst_ref=y_ref.at[me],
            send_sem=send_sem.at[peer],
            recv_sem=recv_sem.at[me],
            device_id=(seg, peer),
            device_id_type=pl.DeviceIdType.MESH,
        )

    def incoming(peer):
        return pltpu.make_async_remote_copy(
            src_ref=x_ref.at[me // spread],
            dst_ref=y_ref.at[peer],
            send_sem=send_sem.at[peer],
            recv_sem=recv_sem.at[peer],
            device_id=(seg, peer),
            device_id_type=pl.DeviceIdType.MESH,
        )

    def send(d, carry):
        outgoing(lax.rem(me + d, count)).start()
        return carry

    lax.fori_loop(1, count, send, 0)

    def finish(d, carry):
        outgoing(lax.rem(me + d, count)).wait_send()
        incoming(lax.rem(me + count - d, count)).wait_recv()
        return carry

    lax.fori_loop(1, count, finish, 0)
    own.wait()


def exchange(x, count, collective_id):
    spread = count // x.shape[0]
    return pl.pallas_call(
        functools.partial(exchange_kernel, count, spread),
        out_shape=jax.ShapeDtypeStruct((count,) + x.shape[1:], x.dtype),
        in_specs=[pl.BlockSpec(memory_space=pl.ANY)],
        out_specs=pl.BlockSpec(memory_space=pl.ANY),
        scratch_shapes=[
            pltpu.SemaphoreType.DMA((count,)),
            pltpu.SemaphoreType.DMA((count,)),
            pltpu.SemaphoreType.DMA,
        ],
        compiler_params=pltpu.CompilerParams(collective_id=collective_id, has_side_effects=True),
    )(x)


def ffn_kernel(steps, x_ref, g_ref, u_ref, d_ref, o_ref, acc_g, acc_u, inner):
    k = pl.program_id(0)
    slots = x_ref.shape[1]

    @pl.when(k == 0)
    def _():
        acc_g[...] = jnp.zeros_like(acc_g)
        acc_u[...] = jnp.zeros_like(acc_u)

    @pl.when(k < steps)
    def _():
        for c in range(slots):
            xc = x_ref[:, c, :]
            acc_g[c] += jnp.dot(xc, g_ref[...], preferred_element_type=jnp.float32)
            acc_u[c] += jnp.dot(xc, u_ref[...], preferred_element_type=jnp.float32)

    @pl.when(k == steps)
    def _():
        for c in range(slots):
            g = acc_g[c]
            inner[c] = (g / (1.0 + jnp.exp(-g)) * acc_u[c]).astype(jnp.bfloat16)

    @pl.when(k >= steps)
    def _():
        for c in range(slots):
            o_ref[:, c, :] = jnp.dot(
                inner[c], d_ref[...], preferred_element_type=jnp.float32
            ).astype(o_ref.dtype)


def expert_ffn(x, gate_mat, up_mat, down_mat):
    sources, slots, model_dim = x.shape
    hidden = gate_mat.shape[1]
    chunk = 1024
    steps = model_dim // chunk
    rows = sources * slots

    def first(k):
        return jnp.minimum(k, steps - 1)

    def second(k):
        return jnp.maximum(k - steps, 0)

    return pl.pallas_call(
        functools.partial(ffn_kernel, steps),
        grid=(2 * steps,),
        in_specs=[
            pl.BlockSpec((sources, slots, chunk), lambda k: (0, 0, first(k))),
            pl.BlockSpec((chunk, hidden), lambda k: (first(k), 0)),
            pl.BlockSpec((chunk, hidden), lambda k: (first(k), 0)),
            pl.BlockSpec((hidden, chunk), lambda k: (0, second(k))),
        ],
        out_specs=pl.BlockSpec((sources, slots, chunk), lambda k: (0, 0, second(k))),
        out_shape=jax.ShapeDtypeStruct(x.shape, jnp.bfloat16),
        scratch_shapes=[
            pltpu.VMEM((slots, sources, hidden), jnp.float32),
            pltpu.VMEM((slots, sources, hidden), jnp.float32),
            pltpu.VMEM((slots, sources, hidden), jnp.bfloat16),
        ],
        cost_estimate=pl.CostEstimate(
            flops=6 * rows * model_dim * hidden,
            transcendentals=rows * hidden,
            bytes_accessed=3 * model_dim * hidden * 2 + 2 * rows * model_dim * 2,
        ),
    )(x, gate_mat, up_mat, down_mat)


def shifted(value, axis, steps):
    count = lax.axis_size(axis)
    pairs = [(source, (source + steps) % count) for source in range(count)]
    return lax.ppermute(value, axis, pairs)


def on_device(states, routing, route_weight, norm_gain, gate_proj, up_proj, down_proj):
    owners = lax.axis_size("expert")
    experts = owners // GROUP
    passes_count = routing.shape[1]
    row_dev = states.shape[1]
    capacity = 2
    gain_row = norm_gain[0]
    gate_mat = gate_proj[0]
    up_mat = up_proj[0]
    down_mat = down_proj[0]
    expert_ids = jnp.arange(experts, dtype=jnp.int32)
    slot_ids = jnp.arange(capacity, dtype=jnp.int32)
    owner_expert = jnp.arange(owners, dtype=jnp.int32) // GROUP

    current = states[0]
    for step_no in range(passes_count):
        chosen = routing[0, step_no]
        weights_now = route_weight[0, step_no]
        picked = chosen[:, :, None] == expert_ids[None, None, :]
        member = jnp.any(picked, axis=1)
        dense_weight = jnp.sum(
            jnp.where(picked, weights_now[:, :, None].astype(jnp.float32), jnp.float32(0.0)), axis=1
        )
        slot_rank = jnp.cumsum(member.astype(jnp.int32), axis=0) - 1
        placer = member.T[:, None, :] & (slot_rank.T[:, None, :] == slot_ids[None, :, None])
        placer_f = placer.astype(jnp.bfloat16)

        current_f = current.astype(jnp.float32)
        inv_rms = lax.rsqrt(jnp.mean(current_f * current_f, axis=1, keepdims=True) + 1e-06)
        normed = (current_f * inv_rms * gain_row).astype(jnp.bfloat16)

        packed = jnp.einsum(
            "jcr,rd->jcd", placer_f, normed, preferred_element_type=jnp.float32
        ).astype(jnp.bfloat16)
        packed_weight = jnp.sum(
            jnp.where(placer, dense_weight.T[:, None, :], jnp.float32(0.0)), axis=2
        )
        got = exchange(packed, owners, 0)
        terms = expert_ffn(got, gate_mat, up_mat, down_mat)

        back = exchange(terms, owners, 1)
        slot_weight = jnp.where(placer, packed_weight[:, :, None], jnp.float32(0.0))
        back_weight = slot_weight[owner_expert].astype(jnp.bfloat16)
        summed = jnp.einsum(
            "ocr,ocd->rd", back_weight, back, preferred_element_type=jnp.float32
        )
        updated = (current_f + summed).astype(jnp.bfloat16)
        current = shifted(updated, "segment", 1)
    return current[None]


def solution(mesh):
    return jax.shard_map(
        on_device,
        mesh=mesh,
        in_specs=(
            P("segment", "expert", None),
            P("segment", None, "expert", None),
            P("segment", None, "expert", None),
            P("segment", None),
            P("segment", None, "expert"),
            P("segment", None, "expert"),
            P("segment", "expert", None),
        ),
        out_specs=P("segment", "expert", None),
        check_vma=False,
    )
```

```python
import functools

import jax
import jax.numpy as jnp
from jax import lax
from jax.experimental import pallas as pl
from jax.experimental.pallas import tpu as pltpu
from jax.sharding import PartitionSpec as P

GROUP = 4


def signed_step(index):
    odd = index % 2
    return odd * ((index + 1) // 2) - (1 - odd) * (index // 2)


def exchange_kernel(count, spread, x_ref, y_ref, send_sem, recv_sem, own_sem):
    me = lax.axis_index("expert")
    seg = lax.axis_index("segment")
    ring_z = 8
    ring_y = count // ring_z
    my_y = me // ring_z
    my_z = me % ring_z

    def peer_at(d, sign):
        step_z = signed_step(d % ring_z) * sign
        step_y = signed_step(d // ring_z) * sign
        return ((my_y + step_y + ring_y) % ring_y) * ring_z + (my_z + step_z + ring_z) % ring_z

    barrier = pltpu.get_barrier_semaphore()

    def greet(d, carry):
        pl.semaphore_signal(
            barrier, inc=1, device_id=(seg, peer_at(d, 1)), device_id_type=pl.DeviceIdType.MESH
        )
        return carry

    lax.fori_loop(1, count, greet, 0)
    pl.semaphore_wait(barrier, count - 1)

    own = pltpu.make_async_copy(x_ref.at[me // spread], y_ref.at[me], own_sem)
    own.start()

    def outgoing(peer):
        return pltpu.make_async_remote_copy(
            src_ref=x_ref.at[peer // spread],
            dst_ref=y_ref.at[me],
            send_sem=send_sem.at[peer],
            recv_sem=recv_sem.at[me],
            device_id=(seg, peer),
            device_id_type=pl.DeviceIdType.MESH,
        )

    def incoming(peer):
        return pltpu.make_async_remote_copy(
            src_ref=x_ref.at[me // spread],
            dst_ref=y_ref.at[peer],
            send_sem=send_sem.at[peer],
            recv_sem=recv_sem.at[peer],
            device_id=(seg, peer),
            device_id_type=pl.DeviceIdType.MESH,
        )

    def send(d, carry):
        outgoing(peer_at(d, 1)).start()
        return carry

    lax.fori_loop(1, count, send, 0)

    def finish(d, carry):
        outgoing(peer_at(d, 1)).wait_send()
        incoming(peer_at(d, -1)).wait_recv()
        return carry

    lax.fori_loop(1, count, finish, 0)
    own.wait()


def exchange(x, count, collective_id):
    spread = count // x.shape[0]
    return pl.pallas_call(
        functools.partial(exchange_kernel, count, spread),
        out_shape=jax.ShapeDtypeStruct((count,) + x.shape[1:], x.dtype),
        in_specs=[pl.BlockSpec(memory_space=pl.ANY)],
        out_specs=pl.BlockSpec(memory_space=pl.ANY),
        scratch_shapes=[
            pltpu.SemaphoreType.DMA((count,)),
            pltpu.SemaphoreType.DMA((count,)),
            pltpu.SemaphoreType.DMA,
        ],
        compiler_params=pltpu.CompilerParams(collective_id=collective_id, has_side_effects=True),
    )(x)


def ffn_kernel(x_ref, g_ref, u_ref, d_ref, o_ref, acc_g, acc_u):
    k = pl.program_id(0)

    @pl.when(k == 0)
    def _():
        acc_g[...] = jnp.zeros_like(acc_g)
        acc_u[...] = jnp.zeros_like(acc_u)

    for c in range(x_ref.shape[1]):
        xc = x_ref[:, c, :]
        acc_g[c] += jnp.dot(xc, g_ref[...], preferred_element_type=jnp.float32)
        acc_u[c] += jnp.dot(xc, u_ref[...], preferred_element_type=jnp.float32)

    @pl.when(k == pl.num_programs(0) - 1)
    def _():
        for c in range(x_ref.shape[1]):
            g = acc_g[c]
            inner = (g / (1.0 + jnp.exp(-g)) * acc_u[c]).astype(jnp.bfloat16)
            o_ref[:, c, :] = jnp.dot(
                inner, d_ref[...], preferred_element_type=jnp.float32
            ).astype(o_ref.dtype)


def expert_ffn(x, gate_mat, up_mat, down_mat):
    sources, slots, model_dim = x.shape
    hidden = gate_mat.shape[1]
    chunk = 1024
    rows = sources * slots
    return pl.pallas_call(
        ffn_kernel,
        grid=(model_dim // chunk,),
        in_specs=[
            pl.BlockSpec((sources, slots, chunk), lambda k: (0, 0, k)),
            pl.BlockSpec((chunk, hidden), lambda k: (k, 0)),
            pl.BlockSpec((chunk, hidden), lambda k: (k, 0)),
            pl.BlockSpec((hidden, model_dim), lambda k: (0, 0)),
        ],
        out_specs=pl.BlockSpec((sources, slots, model_dim), lambda k: (0, 0, 0)),
        out_shape=jax.ShapeDtypeStruct(x.shape, jnp.bfloat16),
        scratch_shapes=[
            pltpu.VMEM((slots, sources, hidden), jnp.float32),
            pltpu.VMEM((slots, sources, hidden), jnp.float32),
        ],
        cost_estimate=pl.CostEstimate(
            flops=6 * rows * model_dim * hidden,
            transcendentals=rows * hidden,
            bytes_accessed=3 * model_dim * hidden * 2 + 2 * rows * model_dim * 2,
        ),
    )(x, gate_mat, up_mat, down_mat)


def shifted(value, axis, steps):
    count = lax.axis_size(axis)
    pairs = [(source, (source + steps) % count) for source in range(count)]
    return lax.ppermute(value, axis, pairs)


def on_device(states, routing, route_weight, norm_gain, gate_proj, up_proj, down_proj):
    owners = lax.axis_size("expert")
    experts = owners // GROUP
    passes_count = routing.shape[1]
    row_dev = states.shape[1]
    capacity = 2
    gain_row = norm_gain[0]
    gate_mat = gate_proj[0]
    up_mat = up_proj[0]
    down_mat = down_proj[0]
    expert_ids = jnp.arange(experts, dtype=jnp.int32)
    slot_ids = jnp.arange(capacity, dtype=jnp.int32)
    owner_expert = jnp.arange(owners, dtype=jnp.int32) // GROUP

    current = states[0]
    for step_no in range(passes_count):
        chosen = routing[0, step_no]
        weights_now = route_weight[0, step_no]
        picked = chosen[:, :, None] == expert_ids[None, None, :]
        member = jnp.any(picked, axis=1)
        dense_weight = jnp.sum(
            jnp.where(picked, weights_now[:, :, None].astype(jnp.float32), jnp.float32(0.0)), axis=1
        )
        slot_rank = jnp.cumsum(member.astype(jnp.int32), axis=0) - 1
        placer = member.T[:, None, :] & (slot_rank.T[:, None, :] == slot_ids[None, :, None])
        placer_f = placer.astype(jnp.bfloat16)

        current_f = current.astype(jnp.float32)
        inv_rms = lax.rsqrt(jnp.mean(current_f * current_f, axis=1, keepdims=True) + 1e-06)
        normed = (current_f * inv_rms * gain_row).astype(jnp.bfloat16)

        packed = jnp.einsum(
            "jcr,rd->jcd", placer_f, normed, preferred_element_type=jnp.float32
        ).astype(jnp.bfloat16)
        packed_weight = jnp.sum(
            jnp.where(placer, dense_weight.T[:, None, :], jnp.float32(0.0)), axis=2
        )
        got = exchange(packed, owners, 0)
        terms = expert_ffn(got, gate_mat, up_mat, down_mat)

        back = exchange(terms, owners, 1)
        slot_weight = jnp.where(placer, packed_weight[:, :, None], jnp.float32(0.0))
        back_weight = slot_weight[owner_expert].astype(jnp.bfloat16)
        summed = jnp.einsum(
            "ocr,ocd->rd", back_weight, back, preferred_element_type=jnp.float32
        )
        updated = (current_f + summed).astype(jnp.bfloat16)
        current = shifted(updated, "segment", 1)
    return current[None]


def solution(mesh):
    return jax.shard_map(
        on_device,
        mesh=mesh,
        in_specs=(
            P("segment", "expert", None),
            P("segment", None, "expert", None),
            P("segment", None, "expert", None),
            P("segment", None),
            P("segment", None, "expert"),
            P("segment", None, "expert"),
            P("segment", "expert", None),
        ),
        out_specs=P("segment", "expert", None),
        check_vma=False,
    )
```

```python
import functools

import jax
import jax.numpy as jnp
from jax import lax
from jax.experimental import pallas as pl
from jax.experimental.pallas import tpu as pltpu
from jax.sharding import PartitionSpec as P

GROUP = 4


def exchange_kernel(count, spread, x_ref, y_ref, send_sem, recv_sem, own_sem):
    me = lax.axis_index("expert")
    seg = lax.axis_index("segment")

    barrier = pltpu.get_barrier_semaphore()

    def greet(d, carry):
        peer = lax.rem(me + d, count)
        pl.semaphore_signal(
            barrier, inc=1, device_id=(seg, peer), device_id_type=pl.DeviceIdType.MESH
        )
        return carry

    lax.fori_loop(1, count, greet, 0)
    pl.semaphore_wait(barrier, count - 1)

    own = pltpu.make_async_copy(x_ref.at[me // spread], y_ref.at[me], own_sem)
    own.start()

    def outgoing(peer):
        return pltpu.make_async_remote_copy(
            src_ref=x_ref.at[peer // spread],
            dst_ref=y_ref.at[me],
            send_sem=send_sem.at[peer],
            recv_sem=recv_sem.at[me],
            device_id=(seg, peer),
            device_id_type=pl.DeviceIdType.MESH,
        )

    def incoming(peer):
        return pltpu.make_async_remote_copy(
            src_ref=x_ref.at[me // spread],
            dst_ref=y_ref.at[peer],
            send_sem=send_sem.at[peer],
            recv_sem=recv_sem.at[peer],
            device_id=(seg, peer),
            device_id_type=pl.DeviceIdType.MESH,
        )

    def send(d, carry):
        outgoing(lax.rem(me + d, count)).start()
        return carry

    lax.fori_loop(1, count, send, 0)

    def finish(d, carry):
        outgoing(lax.rem(me + d, count)).wait_send()
        incoming(lax.rem(me + count - d, count)).wait_recv()
        return carry

    lax.fori_loop(1, count, finish, 0)
    own.wait()


def exchange(x, count, collective_id):
    spread = count // x.shape[0]
    return pl.pallas_call(
        functools.partial(exchange_kernel, count, spread),
        out_shape=jax.ShapeDtypeStruct((count,) + x.shape[1:], x.dtype),
        in_specs=[pl.BlockSpec(memory_space=pl.ANY)],
        out_specs=pl.BlockSpec(memory_space=pl.ANY),
        scratch_shapes=[
            pltpu.SemaphoreType.DMA((count,)),
            pltpu.SemaphoreType.DMA((count,)),
            pltpu.SemaphoreType.DMA,
        ],
        compiler_params=pltpu.CompilerParams(collective_id=collective_id, has_side_effects=True),
    )(x)


def entry_z(z_from, half, line):
    ring = 2 * line
    inside = (z_from // line) == half
    r = z_from % line
    low = (z_from - 1 - r + ring) % ring
    high = (z_from + line - r) % ring
    return jnp.where(inside, z_from, jnp.where(r < line // 2, low, high))


def dispatch_kernel(count, x_ref, y_ref, send_sem, recv_sem, right_sem, left_sem, own_sem):
    me = lax.axis_index("expert")
    seg = lax.axis_index("segment")
    line = GROUP
    ring_z = 2 * line
    my_y = me // ring_z
    my_z = me % ring_z
    my_half = my_z // line
    pos = my_z % line
    group = me // GROUP
    groups = count // GROUP

    barrier = pltpu.get_barrier_semaphore()

    def greet(d, carry):
        pl.semaphore_signal(
            barrier, inc=1, device_id=(seg, lax.rem(me + d, count)),
            device_id_type=pl.DeviceIdType.MESH,
        )
        return carry

    lax.fori_loop(1, count, greet, 0)
    pl.semaphore_wait(barrier, count - 1)

    own = pltpu.make_async_copy(x_ref.at[group], y_ref.at[me], own_sem)
    own.start()

    def first_hop(g):
        target = (g // 2) * ring_z + entry_z(my_z, g % 2, line)
        return pltpu.make_async_remote_copy(
            src_ref=x_ref.at[g],
            dst_ref=y_ref.at[me],
            send_sem=send_sem.at[g],
            recv_sem=recv_sem.at[me],
            device_id=(seg, target),
            device_id_type=pl.DeviceIdType.MESH,
        )

    def send(i, carry):
        g = lax.rem(group + i, groups)
        first_hop(g).start()
        return carry

    lax.fori_loop(1, groups, send, 0)

    def relay(p, step, sem):
        source = x_ref.at[group] if p is None else y_ref.at[p]
        slot = me if p is None else p
        return pltpu.make_async_remote_copy(
            src_ref=source,
            dst_ref=y_ref.at[slot],
            send_sem=sem.at[slot],
            recv_sem=recv_sem.at[slot],
            device_id=(seg, me + step),
            device_id_type=pl.DeviceIdType.MESH,
        )

    def arrival(p):
        return pltpu.make_async_remote_copy(
            src_ref=x_ref.at[group],
            dst_ref=y_ref.at[p],
            send_sem=send_sem.at[0],
            recv_sem=recv_sem.at[p],
            device_id=(seg, p),
            device_id_type=pl.DeviceIdType.MESH,
        )

    def entry_pos(p):
        return entry_z(p % ring_z, my_half, line) % line

    @pl.when(pos < line - 1)
    def _():
        relay(None, 1, right_sem).start()

    @pl.when(pos > 0)
    def _():
        relay(None, -1, left_sem).start()

    for delta in range(line):
        def forward(i, carry):
            p = lax.rem(me + i, count)
            e = entry_pos(p)
            far = jnp.abs(e - pos)

            @pl.when(far == delta)
            def _():
                arrival(p).wait_recv()

                @pl.when((e <= pos) & (pos < line - 1))
                def _():
                    relay(p, 1, right_sem).start()

                @pl.when((e >= pos) & (pos > 0))
                def _():
                    relay(p, -1, left_sem).start()

            return carry

        lax.fori_loop(1, count, forward, 0)

    def drain(i, carry):
        p = lax.rem(me + i, count)
        e = entry_pos(p)

        @pl.when((e <= pos) & (pos < line - 1))
        def _():
            relay(p, 1, right_sem).wait_send()

        @pl.when((e >= pos) & (pos > 0))
        def _():
            relay(p, -1, left_sem).wait_send()

        return carry

    lax.fori_loop(1, count, drain, 0)

    @pl.when(pos < line - 1)
    def _():
        relay(None, 1, right_sem).wait_send()

    @pl.when(pos > 0)
    def _():
        relay(None, -1, left_sem).wait_send()

    def sent(i, carry):
        first_hop(lax.rem(group + i, groups)).wait_send()
        return carry

    lax.fori_loop(1, groups, sent, 0)
    own.wait()


def dispatch(x, count, collective_id):
    return pl.pallas_call(
        functools.partial(dispatch_kernel, count),
        out_shape=jax.ShapeDtypeStruct((count,) + x.shape[1:], x.dtype),
        in_specs=[pl.BlockSpec(memory_space=pl.ANY)],
        out_specs=pl.BlockSpec(memory_space=pl.ANY),
        scratch_shapes=[
            pltpu.SemaphoreType.DMA((x.shape[0],)),
            pltpu.SemaphoreType.DMA((count,)),
            pltpu.SemaphoreType.DMA((count,)),
            pltpu.SemaphoreType.DMA((count,)),
            pltpu.SemaphoreType.DMA,
        ],
        compiler_params=pltpu.CompilerParams(collective_id=collective_id, has_side_effects=True),
    )(x)


def ffn_kernel(x_ref, g_ref, u_ref, d_ref, o_ref, acc_g, acc_u):
    k = pl.program_id(0)

    @pl.when(k == 0)
    def _():
        acc_g[...] = jnp.zeros_like(acc_g)
        acc_u[...] = jnp.zeros_like(acc_u)

    for c in range(x_ref.shape[1]):
        xc = x_ref[:, c, :]
        acc_g[c] += jnp.dot(xc, g_ref[...], preferred_element_type=jnp.float32)
        acc_u[c] += jnp.dot(xc, u_ref[...], preferred_element_type=jnp.float32)

    @pl.when(k == pl.num_programs(0) - 1)
    def _():
        for c in range(x_ref.shape[1]):
            g = acc_g[c]
            inner = (g / (1.0 + jnp.exp(-g)) * acc_u[c]).astype(jnp.bfloat16)
            o_ref[:, c, :] = jnp.dot(
                inner, d_ref[...], preferred_element_type=jnp.float32
            ).astype(o_ref.dtype)


def expert_ffn(x, gate_mat, up_mat, down_mat):
    sources, slots, model_dim = x.shape
    hidden = gate_mat.shape[1]
    chunk = 1024
    rows = sources * slots
    return pl.pallas_call(
        ffn_kernel,
        grid=(model_dim // chunk,),
        in_specs=[
            pl.BlockSpec((sources, slots, chunk), lambda k: (0, 0, k)),
            pl.BlockSpec((chunk, hidden), lambda k: (k, 0)),
            pl.BlockSpec((chunk, hidden), lambda k: (k, 0)),
            pl.BlockSpec((hidden, model_dim), lambda k: (0, 0)),
        ],
        out_specs=pl.BlockSpec((sources, slots, model_dim), lambda k: (0, 0, 0)),
        out_shape=jax.ShapeDtypeStruct(x.shape, jnp.bfloat16),
        scratch_shapes=[
            pltpu.VMEM((slots, sources, hidden), jnp.float32),
            pltpu.VMEM((slots, sources, hidden), jnp.float32),
        ],
        cost_estimate=pl.CostEstimate(
            flops=6 * rows * model_dim * hidden,
            transcendentals=rows * hidden,
            bytes_accessed=3 * model_dim * hidden * 2 + 2 * rows * model_dim * 2,
        ),
    )(x, gate_mat, up_mat, down_mat)


def shifted(value, axis, steps):
    count = lax.axis_size(axis)
    pairs = [(source, (source + steps) % count) for source in range(count)]
    return lax.ppermute(value, axis, pairs)


def on_device(states, routing, route_weight, norm_gain, gate_proj, up_proj, down_proj):
    owners = lax.axis_size("expert")
    experts = owners // GROUP
    passes_count = routing.shape[1]
    row_dev = states.shape[1]
    capacity = 2
    gain_row = norm_gain[0]
    gate_mat = gate_proj[0]
    up_mat = up_proj[0]
    down_mat = down_proj[0]
    expert_ids = jnp.arange(experts, dtype=jnp.int32)
    slot_ids = jnp.arange(capacity, dtype=jnp.int32)
    owner_expert = jnp.arange(owners, dtype=jnp.int32) // GROUP

    current = states[0]
    for step_no in range(passes_count):
        chosen = routing[0, step_no]
        weights_now = route_weight[0, step_no]
        picked = chosen[:, :, None] == expert_ids[None, None, :]
        member = jnp.any(picked, axis=1)
        dense_weight = jnp.sum(
            jnp.where(picked, weights_now[:, :, None].astype(jnp.float32), jnp.float32(0.0)), axis=1
        )
        slot_rank = jnp.cumsum(member.astype(jnp.int32), axis=0) - 1
        placer = member.T[:, None, :] & (slot_rank.T[:, None, :] == slot_ids[None, :, None])
        placer_f = placer.astype(jnp.bfloat16)

        current_f = current.astype(jnp.float32)
        inv_rms = lax.rsqrt(jnp.mean(current_f * current_f, axis=1, keepdims=True) + 1e-06)
        normed = (current_f * inv_rms * gain_row).astype(jnp.bfloat16)

        packed = jnp.einsum(
            "jcr,rd->jcd", placer_f, normed, preferred_element_type=jnp.float32
        ).astype(jnp.bfloat16)
        packed_weight = jnp.sum(
            jnp.where(placer, dense_weight.T[:, None, :], jnp.float32(0.0)), axis=2
        )
        got = dispatch(packed, owners, 2)
        terms = expert_ffn(got, gate_mat, up_mat, down_mat)

        back = exchange(terms, owners, 1)
        slot_weight = jnp.where(placer, packed_weight[:, :, None], jnp.float32(0.0))
        back_weight = slot_weight[owner_expert].astype(jnp.bfloat16)
        summed = jnp.einsum(
            "ocr,ocd->rd", back_weight, back, preferred_element_type=jnp.float32
        )
        updated = (current_f + summed).astype(jnp.bfloat16)
        current = shifted(updated, "segment", 1)
    return current[None]


def solution(mesh):
    return jax.shard_map(
        on_device,
        mesh=mesh,
        in_specs=(
            P("segment", "expert", None),
            P("segment", None, "expert", None),
            P("segment", None, "expert", None),
            P("segment", None),
            P("segment", None, "expert"),
            P("segment", None, "expert"),
            P("segment", "expert", None),
        ),
        out_specs=P("segment", "expert", None),
        check_vma=False,
    )
```

```python
import functools

import jax
import jax.numpy as jnp
from jax import lax
from jax.experimental import pallas as pl
from jax.experimental.pallas import tpu as pltpu
from jax.sharding import PartitionSpec as P

GROUP = 4


def exchange_kernel(count, spread, x_ref, y_ref, send_sem, recv_sem, own_sem):
    me = lax.axis_index("expert")
    seg = lax.axis_index("segment")

    barrier = pltpu.get_barrier_semaphore()

    def greet(d, carry):
        peer = lax.rem(me + d, count)
        pl.semaphore_signal(
            barrier, inc=1, device_id=(seg, peer), device_id_type=pl.DeviceIdType.MESH
        )
        return carry

    lax.fori_loop(1, count, greet, 0)
    pl.semaphore_wait(barrier, count - 1)

    own = pltpu.make_async_copy(x_ref.at[me // spread], y_ref.at[me], own_sem)
    own.start()

    def outgoing(peer):
        return pltpu.make_async_remote_copy(
            src_ref=x_ref.at[peer // spread],
            dst_ref=y_ref.at[me],
            send_sem=send_sem.at[peer],
            recv_sem=recv_sem.at[me],
            device_id=(seg, peer),
            device_id_type=pl.DeviceIdType.MESH,
        )

    def incoming(peer):
        return pltpu.make_async_remote_copy(
            src_ref=x_ref.at[me // spread],
            dst_ref=y_ref.at[peer],
            send_sem=send_sem.at[peer],
            recv_sem=recv_sem.at[peer],
            device_id=(seg, peer),
            device_id_type=pl.DeviceIdType.MESH,
        )

    def send(d, carry):
        outgoing(lax.rem(me + d, count)).start()
        return carry

    lax.fori_loop(1, count, send, 0)

    def finish(d, carry):
        outgoing(lax.rem(me + d, count)).wait_send()
        incoming(lax.rem(me + count - d, count)).wait_recv()
        return carry

    lax.fori_loop(1, count, finish, 0)
    own.wait()


def exchange(x, count, collective_id):
    spread = count // x.shape[0]
    return pl.pallas_call(
        functools.partial(exchange_kernel, count, spread),
        out_shape=jax.ShapeDtypeStruct((count,) + x.shape[1:], x.dtype),
        in_specs=[pl.BlockSpec(memory_space=pl.ANY)],
        out_specs=pl.BlockSpec(memory_space=pl.ANY),
        scratch_shapes=[
            pltpu.SemaphoreType.DMA((count,)),
            pltpu.SemaphoreType.DMA((count,)),
            pltpu.SemaphoreType.DMA,
        ],
        compiler_params=pltpu.CompilerParams(collective_id=collective_id, has_side_effects=True),
    )(x)


def ffn_kernel(x_ref, g_ref, u_ref, d_ref, o_ref, acc_g, acc_u):
    k = pl.program_id(0)

    @pl.when(k == 0)
    def _():
        acc_g[...] = jnp.zeros_like(acc_g)
        acc_u[...] = jnp.zeros_like(acc_u)

    for c in range(x_ref.shape[1]):
        xc = x_ref[:, c, :]
        acc_g[c] += jnp.dot(xc, g_ref[...], preferred_element_type=jnp.float32)
        acc_u[c] += jnp.dot(xc, u_ref[...], preferred_element_type=jnp.float32)

    @pl.when(k == pl.num_programs(0) - 1)
    def _():
        for c in range(x_ref.shape[1]):
            g = acc_g[c]
            inner = (g / (1.0 + jnp.exp(-g)) * acc_u[c]).astype(jnp.bfloat16)
            o_ref[:, c, :] = jnp.dot(
                inner, d_ref[...], preferred_element_type=jnp.float32
            ).astype(o_ref.dtype)


def expert_ffn(x, gate_mat, up_mat, down_mat):
    sources, slots, model_dim = x.shape
    hidden = gate_mat.shape[1]
    chunk = 1024
    rows = sources * slots
    return pl.pallas_call(
        ffn_kernel,
        grid=(model_dim // chunk,),
        in_specs=[
            pl.BlockSpec((sources, slots, chunk), lambda k: (0, 0, k)),
            pl.BlockSpec((chunk, hidden), lambda k: (k, 0)),
            pl.BlockSpec((chunk, hidden), lambda k: (k, 0)),
            pl.BlockSpec((hidden, model_dim), lambda k: (0, 0)),
        ],
        out_specs=pl.BlockSpec((sources, slots, model_dim), lambda k: (0, 0, 0)),
        out_shape=jax.ShapeDtypeStruct(x.shape, jnp.bfloat16),
        scratch_shapes=[
            pltpu.VMEM((slots, sources, hidden), jnp.float32),
            pltpu.VMEM((slots, sources, hidden), jnp.float32),
        ],
        cost_estimate=pl.CostEstimate(
            flops=6 * rows * model_dim * hidden,
            transcendentals=rows * hidden,
            bytes_accessed=3 * model_dim * hidden * 2 + 2 * rows * model_dim * 2,
        ),
    )(x, gate_mat, up_mat, down_mat)


def ffn_combine_kernel(count, steps, chunk, x_hbm, g_hbm, u_hbm, d_hbm, y_ref, terms_ref,
                       acc_g, acc_u, inner, send_sem, recv_sem, own_sem):
    me = lax.axis_index("expert")
    seg = lax.axis_index("segment")
    sources, slots = x_hbm.shape[0], x_hbm.shape[1]
    hidden = g_hbm.shape[1]
    model_dim = x_hbm.shape[2]

    barrier = pltpu.get_barrier_semaphore()

    def greet(d, carry):
        pl.semaphore_signal(
            barrier, inc=1, device_id=(seg, lax.rem(me + d, count)),
            device_id_type=pl.DeviceIdType.MESH,
        )
        return carry

    lax.fori_loop(1, count, greet, 0)

    acc_g[...] = jnp.zeros_like(acc_g)
    acc_u[...] = jnp.zeros_like(acc_u)

    def gate_up(x_v, g_v, u_v):
        for c in range(slots):
            xc = x_v[:, c, :]
            acc_g[c] += jnp.dot(xc, g_v[...], preferred_element_type=jnp.float32)
            acc_u[c] += jnp.dot(xc, u_v[...], preferred_element_type=jnp.float32)

    pltpu.emit_pipeline(
        gate_up,
        grid=(steps,),
        in_specs=[
            pl.BlockSpec((sources, slots, chunk), lambda k: (0, 0, k)),
            pl.BlockSpec((chunk, hidden), lambda k: (k, 0)),
            pl.BlockSpec((chunk, hidden), lambda k: (k, 0)),
        ],
    )(x_hbm, g_hbm, u_hbm)

    for c in range(slots):
        g = acc_g[c]
        inner[c] = (g / (1.0 + jnp.exp(-g)) * acc_u[c]).astype(jnp.bfloat16)

    def down(d_v, o_v):
        for c in range(slots):
            o_v[:, c, :] = jnp.dot(
                inner[c], d_v[...], preferred_element_type=jnp.float32
            ).astype(o_v.dtype)

    pltpu.emit_pipeline(
        down,
        grid=(1,),
        in_specs=[pl.BlockSpec((hidden, model_dim), lambda k: (0, 0))],
        out_specs=[pl.BlockSpec((sources, slots, model_dim), lambda k: (0, 0, 0))],
    )(d_hbm, terms_ref)

    pl.semaphore_wait(barrier, count - 1)

    own = pltpu.make_async_copy(terms_ref.at[me], y_ref.at[me], own_sem)
    own.start()

    def outgoing(peer):
        return pltpu.make_async_remote_copy(
            src_ref=terms_ref.at[peer],
            dst_ref=y_ref.at[me],
            send_sem=send_sem.at[peer],
            recv_sem=recv_sem.at[me],
            device_id=(seg, peer),
            device_id_type=pl.DeviceIdType.MESH,
        )

    def incoming(peer):
        return pltpu.make_async_remote_copy(
            src_ref=terms_ref.at[me],
            dst_ref=y_ref.at[peer],
            send_sem=send_sem.at[peer],
            recv_sem=recv_sem.at[peer],
            device_id=(seg, peer),
            device_id_type=pl.DeviceIdType.MESH,
        )

    def send(d, carry):
        outgoing(lax.rem(me + d, count)).start()
        return carry

    lax.fori_loop(1, count, send, 0)

    def finish(d, carry):
        outgoing(lax.rem(me + d, count)).wait_send()
        incoming(lax.rem(me + count - d, count)).wait_recv()
        return carry

    lax.fori_loop(1, count, finish, 0)
    own.wait()


def ffn_combine(x, gate_mat, up_mat, down_mat, collective_id):
    count, slots, model_dim = x.shape
    hidden = gate_mat.shape[1]
    chunk = 1024
    steps = model_dim // chunk
    back, _ = pl.pallas_call(
        functools.partial(ffn_combine_kernel, count, steps, chunk),
        out_shape=(
            jax.ShapeDtypeStruct(x.shape, jnp.bfloat16),
            jax.ShapeDtypeStruct(x.shape, jnp.bfloat16),
        ),
        in_specs=[pl.BlockSpec(memory_space=pl.ANY)] * 4,
        out_specs=(pl.BlockSpec(memory_space=pl.ANY), pl.BlockSpec(memory_space=pl.ANY)),
        scratch_shapes=[
            pltpu.VMEM((slots, count, hidden), jnp.float32),
            pltpu.VMEM((slots, count, hidden), jnp.float32),
            pltpu.VMEM((slots, count, hidden), jnp.bfloat16),
            pltpu.SemaphoreType.DMA((count,)),
            pltpu.SemaphoreType.DMA((count,)),
            pltpu.SemaphoreType.DMA,
        ],
        compiler_params=pltpu.CompilerParams(collective_id=collective_id, has_side_effects=True),
    )(x, gate_mat, up_mat, down_mat)
    return back


def shifted(value, axis, steps):
    count = lax.axis_size(axis)
    pairs = [(source, (source + steps) % count) for source in range(count)]
    return lax.ppermute(value, axis, pairs)


def on_device(states, routing, route_weight, norm_gain, gate_proj, up_proj, down_proj):
    owners = lax.axis_size("expert")
    experts = owners // GROUP
    passes_count = routing.shape[1]
    row_dev = states.shape[1]
    capacity = 2
    gain_row = norm_gain[0]
    gate_mat = gate_proj[0]
    up_mat = up_proj[0]
    down_mat = down_proj[0]
    expert_ids = jnp.arange(experts, dtype=jnp.int32)
    slot_ids = jnp.arange(capacity, dtype=jnp.int32)
    owner_expert = jnp.arange(owners, dtype=jnp.int32) // GROUP

    current = states[0]
    for step_no in range(passes_count):
        chosen = routing[0, step_no]
        weights_now = route_weight[0, step_no]
        picked = chosen[:, :, None] == expert_ids[None, None, :]
        member = jnp.any(picked, axis=1)
        dense_weight = jnp.sum(
            jnp.where(picked, weights_now[:, :, None].astype(jnp.float32), jnp.float32(0.0)), axis=1
        )
        slot_rank = jnp.cumsum(member.astype(jnp.int32), axis=0) - 1
        placer = member.T[:, None, :] & (slot_rank.T[:, None, :] == slot_ids[None, :, None])
        placer_f = placer.astype(jnp.bfloat16)

        current_f = current.astype(jnp.float32)
        inv_rms = lax.rsqrt(jnp.mean(current_f * current_f, axis=1, keepdims=True) + 1e-06)
        normed = (current_f * inv_rms * gain_row).astype(jnp.bfloat16)

        packed = jnp.einsum(
            "jcr,rd->jcd", placer_f, normed, preferred_element_type=jnp.float32
        ).astype(jnp.bfloat16)
        packed_weight = jnp.sum(
            jnp.where(placer, dense_weight.T[:, None, :], jnp.float32(0.0)), axis=2
        )
        got = exchange(packed, owners, 0)
        back = ffn_combine(got, gate_mat, up_mat, down_mat, 1)
        slot_weight = jnp.where(placer, packed_weight[:, :, None], jnp.float32(0.0))
        back_weight = slot_weight[owner_expert].astype(jnp.bfloat16)
        summed = jnp.einsum(
            "ocr,ocd->rd", back_weight, back, preferred_element_type=jnp.float32
        )
        updated = (current_f + summed).astype(jnp.bfloat16)
        current = shifted(updated, "segment", 1)
    return current[None]


def solution(mesh):
    return jax.shard_map(
        on_device,
        mesh=mesh,
        in_specs=(
            P("segment", "expert", None),
            P("segment", None, "expert", None),
            P("segment", None, "expert", None),
            P("segment", None),
            P("segment", None, "expert"),
            P("segment", None, "expert"),
            P("segment", "expert", None),
        ),
        out_specs=P("segment", "expert", None),
        check_vma=False,
    )
```

```python
import functools

import jax
import jax.numpy as jnp
from jax import lax
from jax.experimental import pallas as pl
from jax.experimental.pallas import tpu as pltpu
from jax.sharding import PartitionSpec as P

GROUP = 4


def exchange_kernel(count, spread, x_ref, y_ref, send_sem, recv_sem, own_sem):
    me = lax.axis_index("expert")
    seg = lax.axis_index("segment")

    barrier = pltpu.get_barrier_semaphore()

    def greet(d, carry):
        peer = lax.rem(me + d, count)
        pl.semaphore_signal(
            barrier, inc=1, device_id=(seg, peer), device_id_type=pl.DeviceIdType.MESH
        )
        return carry

    lax.fori_loop(1, count, greet, 0)
    pl.semaphore_wait(barrier, count - 1)

    own = pltpu.make_async_copy(x_ref.at[me // spread], y_ref.at[me], own_sem)
    own.start()

    def outgoing(peer):
        return pltpu.make_async_remote_copy(
            src_ref=x_ref.at[peer // spread],
            dst_ref=y_ref.at[me],
            send_sem=send_sem.at[peer],
            recv_sem=recv_sem.at[me],
            device_id=(seg, peer),
            device_id_type=pl.DeviceIdType.MESH,
        )

    def incoming(peer):
        return pltpu.make_async_remote_copy(
            src_ref=x_ref.at[me // spread],
            dst_ref=y_ref.at[peer],
            send_sem=send_sem.at[peer],
            recv_sem=recv_sem.at[peer],
            device_id=(seg, peer),
            device_id_type=pl.DeviceIdType.MESH,
        )

    def send(d, carry):
        outgoing(lax.rem(me + d, count)).start()
        return carry

    lax.fori_loop(1, count, send, 0)

    def finish(d, carry):
        outgoing(lax.rem(me + d, count)).wait_send()
        incoming(lax.rem(me + count - d, count)).wait_recv()
        return carry

    lax.fori_loop(1, count, finish, 0)
    own.wait()


def exchange(x, count, collective_id):
    spread = count // x.shape[0]
    return pl.pallas_call(
        functools.partial(exchange_kernel, count, spread),
        out_shape=jax.ShapeDtypeStruct((count,) + x.shape[1:], x.dtype),
        in_specs=[pl.BlockSpec(memory_space=pl.ANY)],
        out_specs=pl.BlockSpec(memory_space=pl.ANY),
        scratch_shapes=[
            pltpu.SemaphoreType.DMA((count,)),
            pltpu.SemaphoreType.DMA((count,)),
            pltpu.SemaphoreType.DMA,
        ],
        compiler_params=pltpu.CompilerParams(collective_id=collective_id, has_side_effects=True),
    )(x)


def ffn_kernel(x_ref, g_ref, u_ref, d_ref, o_ref, acc_g, acc_u):
    k = pl.program_id(0)

    @pl.when(k == 0)
    def _():
        acc_g[...] = jnp.zeros_like(acc_g)
        acc_u[...] = jnp.zeros_like(acc_u)

    for c in range(x_ref.shape[1]):
        xc = x_ref[:, c, :]
        acc_g[c] += jnp.dot(xc, g_ref[...], preferred_element_type=jnp.float32)
        acc_u[c] += jnp.dot(xc, u_ref[...], preferred_element_type=jnp.float32)

    @pl.when(k == pl.num_programs(0) - 1)
    def _():
        for c in range(x_ref.shape[1]):
            g = acc_g[c]
            inner = (g / (1.0 + jnp.exp(-g)) * acc_u[c]).astype(jnp.bfloat16)
            o_ref[:, c, :] = jnp.dot(
                inner, d_ref[...], preferred_element_type=jnp.float32
            ).astype(o_ref.dtype)


def expert_ffn(x, gate_mat, up_mat, down_mat):
    sources, slots, model_dim = x.shape
    hidden = gate_mat.shape[1]
    chunk = 1024
    rows = sources * slots
    return pl.pallas_call(
        ffn_kernel,
        grid=(model_dim // chunk,),
        in_specs=[
            pl.BlockSpec((sources, slots, chunk), lambda k: (0, 0, k)),
            pl.BlockSpec((chunk, hidden), lambda k: (k, 0)),
            pl.BlockSpec((chunk, hidden), lambda k: (k, 0)),
            pl.BlockSpec((hidden, model_dim), lambda k: (0, 0)),
        ],
        out_specs=pl.BlockSpec((sources, slots, model_dim), lambda k: (0, 0, 0)),
        out_shape=jax.ShapeDtypeStruct(x.shape, jnp.bfloat16),
        scratch_shapes=[
            pltpu.VMEM((slots, sources, hidden), jnp.float32),
            pltpu.VMEM((slots, sources, hidden), jnp.float32),
        ],
        cost_estimate=pl.CostEstimate(
            flops=6 * rows * model_dim * hidden,
            transcendentals=rows * hidden,
            bytes_accessed=3 * model_dim * hidden * 2 + 2 * rows * model_dim * 2,
        ),
    )(x, gate_mat, up_mat, down_mat)


def pack_dispatch_kernel(count, normed_ref, placer_ref, y_ref, send_buf, send_sem, recv_sem, own_sem):
    me = lax.axis_index("expert")
    seg = lax.axis_index("segment")
    slots = y_ref.shape[1]

    barrier = pltpu.get_barrier_semaphore()

    def greet(d, carry):
        pl.semaphore_signal(
            barrier, inc=1, device_id=(seg, lax.rem(me + d, count)),
            device_id_type=pl.DeviceIdType.MESH,
        )
        return carry

    lax.fori_loop(1, count, greet, 0)

    send_buf[...] = jnp.dot(
        placer_ref[...], normed_ref[...], preferred_element_type=jnp.float32
    ).astype(send_buf.dtype)

    pl.semaphore_wait(barrier, count - 1)

    def rows_of(peer):
        return send_buf.at[pl.ds((peer // GROUP) * slots, slots)]

    own = pltpu.make_async_copy(rows_of(me), y_ref.at[me], own_sem)
    own.start()

    def outgoing(peer):
        return pltpu.make_async_remote_copy(
            src_ref=rows_of(peer),
            dst_ref=y_ref.at[me],
            send_sem=send_sem.at[peer],
            recv_sem=recv_sem.at[me],
            device_id=(seg, peer),
            device_id_type=pl.DeviceIdType.MESH,
        )

    def incoming(peer):
        return pltpu.make_async_remote_copy(
            src_ref=rows_of(me),
            dst_ref=y_ref.at[peer],
            send_sem=send_sem.at[peer],
            recv_sem=recv_sem.at[peer],
            device_id=(seg, peer),
            device_id_type=pl.DeviceIdType.MESH,
        )

    def send(d, carry):
        outgoing(lax.rem(me + d, count)).start()
        return carry

    lax.fori_loop(1, count, send, 0)

    def finish(d, carry):
        outgoing(lax.rem(me + d, count)).wait_send()
        incoming(lax.rem(me + count - d, count)).wait_recv()
        return carry

    lax.fori_loop(1, count, finish, 0)
    own.wait()


def pack_dispatch(normed, placer_rows, count, slots, collective_id):
    model_dim = normed.shape[1]
    return pl.pallas_call(
        functools.partial(pack_dispatch_kernel, count),
        out_shape=jax.ShapeDtypeStruct((count, slots, model_dim), normed.dtype),
        in_specs=[
            pl.BlockSpec(memory_space=pltpu.VMEM),
            pl.BlockSpec(memory_space=pltpu.VMEM),
        ],
        out_specs=pl.BlockSpec(memory_space=pl.ANY),
        scratch_shapes=[
            pltpu.VMEM((placer_rows.shape[0], model_dim), normed.dtype),
            pltpu.SemaphoreType.DMA((count,)),
            pltpu.SemaphoreType.DMA((count,)),
            pltpu.SemaphoreType.DMA,
        ],
        compiler_params=pltpu.CompilerParams(collective_id=collective_id, has_side_effects=True),
    )(normed, placer_rows)


def ffn_combine_kernel(count, steps, chunk, x_hbm, g_hbm, u_hbm, d_hbm, y_ref, terms_ref,
                       acc_g, acc_u, inner, send_sem, recv_sem, own_sem):
    me = lax.axis_index("expert")
    seg = lax.axis_index("segment")
    sources, slots = x_hbm.shape[0], x_hbm.shape[1]
    hidden = g_hbm.shape[1]
    model_dim = x_hbm.shape[2]

    barrier = pltpu.get_barrier_semaphore()

    def greet(d, carry):
        pl.semaphore_signal(
            barrier, inc=1, device_id=(seg, lax.rem(me + d, count)),
            device_id_type=pl.DeviceIdType.MESH,
        )
        return carry

    lax.fori_loop(1, count, greet, 0)

    acc_g[...] = jnp.zeros_like(acc_g)
    acc_u[...] = jnp.zeros_like(acc_u)

    def gate_up(x_v, g_v, u_v):
        for c in range(slots):
            xc = x_v[:, c, :]
            acc_g[c] += jnp.dot(xc, g_v[...], preferred_element_type=jnp.float32)
            acc_u[c] += jnp.dot(xc, u_v[...], preferred_element_type=jnp.float32)

    pltpu.emit_pipeline(
        gate_up,
        grid=(steps,),
        in_specs=[
            pl.BlockSpec((sources, slots, chunk), lambda k: (0, 0, k)),
            pl.BlockSpec((chunk, hidden), lambda k: (k, 0)),
            pl.BlockSpec((chunk, hidden), lambda k: (k, 0)),
        ],
    )(x_hbm, g_hbm, u_hbm)

    for c in range(slots):
        g = acc_g[c]
        inner[c] = (g / (1.0 + jnp.exp(-g)) * acc_u[c]).astype(jnp.bfloat16)

    def down(d_v, o_v):
        for c in range(slots):
            o_v[:, c, :] = jnp.dot(
                inner[c], d_v[...], preferred_element_type=jnp.float32
            ).astype(o_v.dtype)

    pltpu.emit_pipeline(
        down,
        grid=(1,),
        in_specs=[pl.BlockSpec((hidden, model_dim), lambda k: (0, 0))],
        out_specs=[pl.BlockSpec((sources, slots, model_dim), lambda k: (0, 0, 0))],
    )(d_hbm, terms_ref)

    pl.semaphore_wait(barrier, count - 1)

    own = pltpu.make_async_copy(terms_ref.at[me], y_ref.at[me], own_sem)
    own.start()

    def outgoing(peer):
        return pltpu.make_async_remote_copy(
            src_ref=terms_ref.at[peer],
            dst_ref=y_ref.at[me],
            send_sem=send_sem.at[peer],
            recv_sem=recv_sem.at[me],
            device_id=(seg, peer),
            device_id_type=pl.DeviceIdType.MESH,
        )

    def incoming(peer):
        return pltpu.make_async_remote_copy(
            src_ref=terms_ref.at[me],
            dst_ref=y_ref.at[peer],
            send_sem=send_sem.at[peer],
            recv_sem=recv_sem.at[peer],
            device_id=(seg, peer),
            device_id_type=pl.DeviceIdType.MESH,
        )

    def send(d, carry):
        outgoing(lax.rem(me + d, count)).start()
        return carry

    lax.fori_loop(1, count, send, 0)

    def finish(d, carry):
        outgoing(lax.rem(me + d, count)).wait_send()
        incoming(lax.rem(me + count - d, count)).wait_recv()
        return carry

    lax.fori_loop(1, count, finish, 0)
    own.wait()


def ffn_combine(x, gate_mat, up_mat, down_mat, collective_id):
    count, slots, model_dim = x.shape
    hidden = gate_mat.shape[1]
    chunk = 1024
    steps = model_dim // chunk
    back, _ = pl.pallas_call(
        functools.partial(ffn_combine_kernel, count, steps, chunk),
        out_shape=(
            jax.ShapeDtypeStruct(x.shape, jnp.bfloat16),
            jax.ShapeDtypeStruct(x.shape, jnp.bfloat16),
        ),
        in_specs=[pl.BlockSpec(memory_space=pl.ANY)] * 4,
        out_specs=(pl.BlockSpec(memory_space=pl.ANY), pl.BlockSpec(memory_space=pl.ANY)),
        scratch_shapes=[
            pltpu.VMEM((slots, count, hidden), jnp.float32),
            pltpu.VMEM((slots, count, hidden), jnp.float32),
            pltpu.VMEM((slots, count, hidden), jnp.bfloat16),
            pltpu.SemaphoreType.DMA((count,)),
            pltpu.SemaphoreType.DMA((count,)),
            pltpu.SemaphoreType.DMA,
        ],
        compiler_params=pltpu.CompilerParams(collective_id=collective_id, has_side_effects=True),
    )(x, gate_mat, up_mat, down_mat)
    return back


def shifted(value, axis, steps):
    count = lax.axis_size(axis)
    pairs = [(source, (source + steps) % count) for source in range(count)]
    return lax.ppermute(value, axis, pairs)


def on_device(states, routing, route_weight, norm_gain, gate_proj, up_proj, down_proj):
    owners = lax.axis_size("expert")
    experts = owners // GROUP
    passes_count = routing.shape[1]
    row_dev = states.shape[1]
    capacity = 2
    gain_row = norm_gain[0]
    gate_mat = gate_proj[0]
    up_mat = up_proj[0]
    down_mat = down_proj[0]
    expert_ids = jnp.arange(experts, dtype=jnp.int32)
    slot_ids = jnp.arange(capacity, dtype=jnp.int32)
    owner_expert = jnp.arange(owners, dtype=jnp.int32) // GROUP

    current = states[0]
    for step_no in range(passes_count):
        chosen = routing[0, step_no]
        weights_now = route_weight[0, step_no]
        picked = chosen[:, :, None] == expert_ids[None, None, :]
        member = jnp.any(picked, axis=1)
        dense_weight = jnp.sum(
            jnp.where(picked, weights_now[:, :, None].astype(jnp.float32), jnp.float32(0.0)), axis=1
        )
        slot_rank = jnp.cumsum(member.astype(jnp.int32), axis=0) - 1
        placer = member.T[:, None, :] & (slot_rank.T[:, None, :] == slot_ids[None, :, None])
        placer_f = placer.astype(jnp.bfloat16)

        current_f = current.astype(jnp.float32)
        inv_rms = lax.rsqrt(jnp.mean(current_f * current_f, axis=1, keepdims=True) + 1e-06)
        normed = (current_f * inv_rms * gain_row).astype(jnp.bfloat16)

        packed_weight = jnp.sum(
            jnp.where(placer, dense_weight.T[:, None, :], jnp.float32(0.0)), axis=2
        )
        got = pack_dispatch(normed, placer_f.reshape(experts * capacity, -1), owners, capacity, 0)
        back = ffn_combine(got, gate_mat, up_mat, down_mat, 1)
        slot_weight = jnp.where(placer, packed_weight[:, :, None], jnp.float32(0.0))
        back_weight = slot_weight[owner_expert].astype(jnp.bfloat16)
        summed = jnp.einsum(
            "ocr,ocd->rd", back_weight, back, preferred_element_type=jnp.float32
        )
        updated = (current_f + summed).astype(jnp.bfloat16)
        current = shifted(updated, "segment", 1)
    return current[None]


def solution(mesh):
    return jax.shard_map(
        on_device,
        mesh=mesh,
        in_specs=(
            P("segment", "expert", None),
            P("segment", None, "expert", None),
            P("segment", None, "expert", None),
            P("segment", None),
            P("segment", None, "expert"),
            P("segment", None, "expert"),
            P("segment", "expert", None),
        ),
        out_specs=P("segment", "expert", None),
        check_vma=False,
    )
```

```python
import functools

import jax
import jax.numpy as jnp
from jax import lax
from jax.experimental import pallas as pl
from jax.experimental.pallas import tpu as pltpu
from jax.sharding import PartitionSpec as P

GROUP = 4


def exchange_kernel(count, spread, x_ref, y_ref, send_sem, recv_sem, own_sem):
    me = lax.axis_index("expert")
    seg = lax.axis_index("segment")

    barrier = pltpu.get_barrier_semaphore()

    def greet(d, carry):
        peer = lax.rem(me + d, count)
        pl.semaphore_signal(
            barrier, inc=1, device_id=(seg, peer), device_id_type=pl.DeviceIdType.MESH
        )
        return carry

    lax.fori_loop(1, count, greet, 0)
    pl.semaphore_wait(barrier, count - 1)

    own = pltpu.make_async_copy(x_ref.at[me // spread], y_ref.at[me], own_sem)
    own.start()

    def outgoing(peer):
        return pltpu.make_async_remote_copy(
            src_ref=x_ref.at[peer // spread],
            dst_ref=y_ref.at[me],
            send_sem=send_sem.at[peer],
            recv_sem=recv_sem.at[me],
            device_id=(seg, peer),
            device_id_type=pl.DeviceIdType.MESH,
        )

    def incoming(peer):
        return pltpu.make_async_remote_copy(
            src_ref=x_ref.at[me // spread],
            dst_ref=y_ref.at[peer],
            send_sem=send_sem.at[peer],
            recv_sem=recv_sem.at[peer],
            device_id=(seg, peer),
            device_id_type=pl.DeviceIdType.MESH,
        )

    def send(d, carry):
        outgoing(lax.rem(me + d, count)).start()
        return carry

    lax.fori_loop(1, count, send, 0)

    def finish(d, carry):
        outgoing(lax.rem(me + d, count)).wait_send()
        incoming(lax.rem(me + count - d, count)).wait_recv()
        return carry

    lax.fori_loop(1, count, finish, 0)
    own.wait()


def exchange(x, count, collective_id):
    spread = count // x.shape[0]
    return pl.pallas_call(
        functools.partial(exchange_kernel, count, spread),
        out_shape=jax.ShapeDtypeStruct((count,) + x.shape[1:], x.dtype),
        in_specs=[pl.BlockSpec(memory_space=pl.ANY)],
        out_specs=pl.BlockSpec(memory_space=pl.ANY),
        scratch_shapes=[
            pltpu.SemaphoreType.DMA((count,)),
            pltpu.SemaphoreType.DMA((count,)),
            pltpu.SemaphoreType.DMA,
        ],
        compiler_params=pltpu.CompilerParams(collective_id=collective_id, has_side_effects=True),
    )(x)


def ffn_kernel(x_ref, g_ref, u_ref, d_ref, o_ref, acc_g, acc_u):
    k = pl.program_id(0)

    @pl.when(k == 0)
    def _():
        acc_g[...] = jnp.zeros_like(acc_g)
        acc_u[...] = jnp.zeros_like(acc_u)

    for c in range(x_ref.shape[1]):
        xc = x_ref[:, c, :]
        acc_g[c] += jnp.dot(xc, g_ref[...], preferred_element_type=jnp.float32)
        acc_u[c] += jnp.dot(xc, u_ref[...], preferred_element_type=jnp.float32)

    @pl.when(k == pl.num_programs(0) - 1)
    def _():
        for c in range(x_ref.shape[1]):
            g = acc_g[c]
            inner = (g / (1.0 + jnp.exp(-g)) * acc_u[c]).astype(jnp.bfloat16)
            o_ref[:, c, :] = jnp.dot(
                inner, d_ref[...], preferred_element_type=jnp.float32
            ).astype(o_ref.dtype)


def expert_ffn(x, gate_mat, up_mat, down_mat):
    sources, slots, model_dim = x.shape
    hidden = gate_mat.shape[1]
    chunk = 1024
    rows = sources * slots
    return pl.pallas_call(
        ffn_kernel,
        grid=(model_dim // chunk,),
        in_specs=[
            pl.BlockSpec((sources, slots, chunk), lambda k: (0, 0, k)),
            pl.BlockSpec((chunk, hidden), lambda k: (k, 0)),
            pl.BlockSpec((chunk, hidden), lambda k: (k, 0)),
            pl.BlockSpec((hidden, model_dim), lambda k: (0, 0)),
        ],
        out_specs=pl.BlockSpec((sources, slots, model_dim), lambda k: (0, 0, 0)),
        out_shape=jax.ShapeDtypeStruct(x.shape, jnp.bfloat16),
        scratch_shapes=[
            pltpu.VMEM((slots, sources, hidden), jnp.float32),
            pltpu.VMEM((slots, sources, hidden), jnp.float32),
        ],
        cost_estimate=pl.CostEstimate(
            flops=6 * rows * model_dim * hidden,
            transcendentals=rows * hidden,
            bytes_accessed=3 * model_dim * hidden * 2 + 2 * rows * model_dim * 2,
        ),
    )(x, gate_mat, up_mat, down_mat)


def ffn_combine_kernel(count, steps, chunk, x_hbm, g_hbm, u_hbm, d_hbm, y_ref, terms_ref,
                       acc_g, acc_u, inner, down_v, send_sem, recv_sem, own_sem, down_sem):
    me = lax.axis_index("expert")
    seg = lax.axis_index("segment")
    sources, slots = x_hbm.shape[0], x_hbm.shape[1]
    hidden = g_hbm.shape[1]
    model_dim = x_hbm.shape[2]

    barrier = pltpu.get_barrier_semaphore()

    def greet(d, carry):
        pl.semaphore_signal(
            barrier, inc=1, device_id=(seg, lax.rem(me + d, count)),
            device_id_type=pl.DeviceIdType.MESH,
        )
        return carry

    lax.fori_loop(1, count, greet, 0)

    down_copy = pltpu.make_async_copy(d_hbm, down_v, down_sem)
    down_copy.start()

    acc_g[...] = jnp.zeros_like(acc_g)
    acc_u[...] = jnp.zeros_like(acc_u)

    def gate_up(x_v, g_v, u_v):
        for c in range(slots):
            xc = x_v[:, c, :]
            acc_g[c] += jnp.dot(xc, g_v[...], preferred_element_type=jnp.float32)
            acc_u[c] += jnp.dot(xc, u_v[...], preferred_element_type=jnp.float32)

    pltpu.emit_pipeline(
        gate_up,
        grid=(steps,),
        in_specs=[
            pl.BlockSpec((sources, slots, chunk), lambda k: (0, 0, k)),
            pl.BlockSpec((chunk, hidden), lambda k: (k, 0)),
            pl.BlockSpec((chunk, hidden), lambda k: (k, 0)),
        ],
    )(x_hbm, g_hbm, u_hbm)

    for c in range(slots):
        g = acc_g[c]
        inner[c] = (g / (1.0 + jnp.exp(-g)) * acc_u[c]).astype(jnp.bfloat16)

    down_copy.wait()

    def down(o_v):
        for c in range(slots):
            o_v[:, c, :] = jnp.dot(
                inner[c], down_v[...], preferred_element_type=jnp.float32
            ).astype(o_v.dtype)

    pltpu.emit_pipeline(
        down,
        grid=(1,),
        out_specs=[pl.BlockSpec((sources, slots, model_dim), lambda k: (0, 0, 0))],
    )(terms_ref)

    pl.semaphore_wait(barrier, count - 1)

    own = pltpu.make_async_copy(terms_ref.at[me], y_ref.at[me], own_sem)
    own.start()

    def outgoing(peer):
        return pltpu.make_async_remote_copy(
            src_ref=terms_ref.at[peer],
            dst_ref=y_ref.at[me],
            send_sem=send_sem.at[peer],
            recv_sem=recv_sem.at[me],
            device_id=(seg, peer),
            device_id_type=pl.DeviceIdType.MESH,
        )

    def incoming(peer):
        return pltpu.make_async_remote_copy(
            src_ref=terms_ref.at[me],
            dst_ref=y_ref.at[peer],
            send_sem=send_sem.at[peer],
            recv_sem=recv_sem.at[peer],
            device_id=(seg, peer),
            device_id_type=pl.DeviceIdType.MESH,
        )

    def send(d, carry):
        outgoing(lax.rem(me + d, count)).start()
        return carry

    lax.fori_loop(1, count, send, 0)

    def finish(d, carry):
        outgoing(lax.rem(me + d, count)).wait_send()
        incoming(lax.rem(me + count - d, count)).wait_recv()
        return carry

    lax.fori_loop(1, count, finish, 0)
    own.wait()


def ffn_combine(x, gate_mat, up_mat, down_mat, collective_id):
    count, slots, model_dim = x.shape
    hidden = gate_mat.shape[1]
    chunk = 1024
    steps = model_dim // chunk
    back, _ = pl.pallas_call(
        functools.partial(ffn_combine_kernel, count, steps, chunk),
        out_shape=(
            jax.ShapeDtypeStruct(x.shape, jnp.bfloat16),
            jax.ShapeDtypeStruct(x.shape, jnp.bfloat16),
        ),
        in_specs=[pl.BlockSpec(memory_space=pl.ANY)] * 4,
        out_specs=(pl.BlockSpec(memory_space=pl.ANY), pl.BlockSpec(memory_space=pl.ANY)),
        scratch_shapes=[
            pltpu.VMEM((slots, count, hidden), jnp.float32),
            pltpu.VMEM((slots, count, hidden), jnp.float32),
            pltpu.VMEM((slots, count, hidden), jnp.bfloat16),
            pltpu.VMEM((hidden, model_dim), down_mat.dtype),
            pltpu.SemaphoreType.DMA((count,)),
            pltpu.SemaphoreType.DMA((count,)),
            pltpu.SemaphoreType.DMA,
            pltpu.SemaphoreType.DMA,
        ],
        compiler_params=pltpu.CompilerParams(collective_id=collective_id, has_side_effects=True),
    )(x, gate_mat, up_mat, down_mat)
    return back


def shifted(value, axis, steps):
    count = lax.axis_size(axis)
    pairs = [(source, (source + steps) % count) for source in range(count)]
    return lax.ppermute(value, axis, pairs)


def on_device(states, routing, route_weight, norm_gain, gate_proj, up_proj, down_proj):
    owners = lax.axis_size("expert")
    experts = owners // GROUP
    passes_count = routing.shape[1]
    row_dev = states.shape[1]
    capacity = 2
    gain_row = norm_gain[0]
    gate_mat = gate_proj[0]
    up_mat = up_proj[0]
    down_mat = down_proj[0]
    expert_ids = jnp.arange(experts, dtype=jnp.int32)
    slot_ids = jnp.arange(capacity, dtype=jnp.int32)
    owner_expert = jnp.arange(owners, dtype=jnp.int32) // GROUP

    current = states[0]
    for step_no in range(passes_count):
        chosen = routing[0, step_no]
        weights_now = route_weight[0, step_no]
        picked = chosen[:, :, None] == expert_ids[None, None, :]
        member = jnp.any(picked, axis=1)
        dense_weight = jnp.sum(
            jnp.where(picked, weights_now[:, :, None].astype(jnp.float32), jnp.float32(0.0)), axis=1
        )
        slot_rank = jnp.cumsum(member.astype(jnp.int32), axis=0) - 1
        placer = member.T[:, None, :] & (slot_rank.T[:, None, :] == slot_ids[None, :, None])
        placer_f = placer.astype(jnp.bfloat16)

        current_f = current.astype(jnp.float32)
        inv_rms = lax.rsqrt(jnp.mean(current_f * current_f, axis=1, keepdims=True) + 1e-06)
        normed = (current_f * inv_rms * gain_row).astype(jnp.bfloat16)

        packed = jnp.einsum(
            "jcr,rd->jcd", placer_f, normed, preferred_element_type=jnp.float32
        ).astype(jnp.bfloat16)
        packed_weight = jnp.sum(
            jnp.where(placer, dense_weight.T[:, None, :], jnp.float32(0.0)), axis=2
        )
        got = exchange(packed, owners, 0)
        back = ffn_combine(got, gate_mat, up_mat, down_mat, 1)
        slot_weight = jnp.where(placer, packed_weight[:, :, None], jnp.float32(0.0))
        back_weight = jnp.broadcast_to(
            slot_weight[:, None], (experts, GROUP) + slot_weight.shape[1:]
        ).reshape((owners,) + slot_weight.shape[1:]).astype(jnp.bfloat16)
        summed = jnp.einsum(
            "ocr,ocd->rd", back_weight, back, preferred_element_type=jnp.float32
        )
        updated = (current_f + summed).astype(jnp.bfloat16)
        current = shifted(updated, "segment", 1)
    return current[None]


def solution(mesh):
    return jax.shard_map(
        on_device,
        mesh=mesh,
        in_specs=(
            P("segment", "expert", None),
            P("segment", None, "expert", None),
            P("segment", None, "expert", None),
            P("segment", None),
            P("segment", None, "expert"),
            P("segment", None, "expert"),
            P("segment", "expert", None),
        ),
        out_specs=P("segment", "expert", None),
        check_vma=False,
    )
```

```python
import functools

import jax
import jax.numpy as jnp
from jax import lax
from jax.experimental import pallas as pl
from jax.experimental.pallas import tpu as pltpu
from jax.sharding import PartitionSpec as P

GROUP = 4


def exchange_kernel(count, spread, x_ref, y_ref, send_sem, recv_sem, own_sem):
    me = lax.axis_index("expert")
    seg = lax.axis_index("segment")

    barrier = pltpu.get_barrier_semaphore()

    def greet(d, carry):
        peer = lax.rem(me + d, count)
        pl.semaphore_signal(
            barrier, inc=1, device_id=(seg, peer), device_id_type=pl.DeviceIdType.MESH
        )
        return carry

    lax.fori_loop(1, count, greet, 0)
    pl.semaphore_wait(barrier, count - 1)

    own = pltpu.make_async_copy(x_ref.at[me // spread], y_ref.at[me], own_sem)
    own.start()

    def outgoing(peer):
        return pltpu.make_async_remote_copy(
            src_ref=x_ref.at[peer // spread],
            dst_ref=y_ref.at[me],
            send_sem=send_sem.at[peer],
            recv_sem=recv_sem.at[me],
            device_id=(seg, peer),
            device_id_type=pl.DeviceIdType.MESH,
        )

    def incoming(peer):
        return pltpu.make_async_remote_copy(
            src_ref=x_ref.at[me // spread],
            dst_ref=y_ref.at[peer],
            send_sem=send_sem.at[peer],
            recv_sem=recv_sem.at[peer],
            device_id=(seg, peer),
            device_id_type=pl.DeviceIdType.MESH,
        )

    def send(d, carry):
        outgoing(lax.rem(me + d, count)).start()
        return carry

    lax.fori_loop(1, count, send, 0)

    def finish(d, carry):
        outgoing(lax.rem(me + d, count)).wait_send()
        incoming(lax.rem(me + count - d, count)).wait_recv()
        return carry

    lax.fori_loop(1, count, finish, 0)
    own.wait()


def exchange(x, count, collective_id):
    spread = count // x.shape[0]
    return pl.pallas_call(
        functools.partial(exchange_kernel, count, spread),
        out_shape=jax.ShapeDtypeStruct((count,) + x.shape[1:], x.dtype),
        in_specs=[pl.BlockSpec(memory_space=pl.ANY)],
        out_specs=pl.BlockSpec(memory_space=pl.ANY),
        scratch_shapes=[
            pltpu.SemaphoreType.DMA((count,)),
            pltpu.SemaphoreType.DMA((count,)),
            pltpu.SemaphoreType.DMA,
        ],
        compiler_params=pltpu.CompilerParams(collective_id=collective_id, has_side_effects=True),
    )(x)


def ffn_kernel(x_ref, g_ref, u_ref, d_ref, o_ref, acc_g, acc_u):
    k = pl.program_id(0)

    @pl.when(k == 0)
    def _():
        acc_g[...] = jnp.zeros_like(acc_g)
        acc_u[...] = jnp.zeros_like(acc_u)

    for c in range(x_ref.shape[1]):
        xc = x_ref[:, c, :]
        acc_g[c] += jnp.dot(xc, g_ref[...], preferred_element_type=jnp.float32)
        acc_u[c] += jnp.dot(xc, u_ref[...], preferred_element_type=jnp.float32)

    @pl.when(k == pl.num_programs(0) - 1)
    def _():
        for c in range(x_ref.shape[1]):
            g = acc_g[c]
            inner = (g / (1.0 + jnp.exp(-g)) * acc_u[c]).astype(jnp.bfloat16)
            o_ref[:, c, :] = jnp.dot(
                inner, d_ref[...], preferred_element_type=jnp.float32
            ).astype(o_ref.dtype)


def expert_ffn(x, gate_mat, up_mat, down_mat):
    sources, slots, model_dim = x.shape
    hidden = gate_mat.shape[1]
    chunk = 1024
    rows = sources * slots
    return pl.pallas_call(
        ffn_kernel,
        grid=(model_dim // chunk,),
        in_specs=[
            pl.BlockSpec((sources, slots, chunk), lambda k: (0, 0, k)),
            pl.BlockSpec((chunk, hidden), lambda k: (k, 0)),
            pl.BlockSpec((chunk, hidden), lambda k: (k, 0)),
            pl.BlockSpec((hidden, model_dim), lambda k: (0, 0)),
        ],
        out_specs=pl.BlockSpec((sources, slots, model_dim), lambda k: (0, 0, 0)),
        out_shape=jax.ShapeDtypeStruct(x.shape, jnp.bfloat16),
        scratch_shapes=[
            pltpu.VMEM((slots, sources, hidden), jnp.float32),
            pltpu.VMEM((slots, sources, hidden), jnp.float32),
        ],
        cost_estimate=pl.CostEstimate(
            flops=6 * rows * model_dim * hidden,
            transcendentals=rows * hidden,
            bytes_accessed=3 * model_dim * hidden * 2 + 2 * rows * model_dim * 2,
        ),
    )(x, gate_mat, up_mat, down_mat)


def ffn_combine_kernel(count, steps, chunk, x_hbm, g_hbm, u_hbm, d_hbm, y_ref, terms_ref,
                       acc_g, acc_u, inner, down_v, send_sem, recv_sem, own_sem, down_sem):
    me = lax.axis_index("expert")
    seg = lax.axis_index("segment")
    sources, slots = x_hbm.shape[0], x_hbm.shape[1]
    hidden = g_hbm.shape[1]
    model_dim = x_hbm.shape[2]

    barrier = pltpu.get_barrier_semaphore()

    def greet(d, carry):
        pl.semaphore_signal(
            barrier, inc=1, device_id=(seg, lax.rem(me + d, count)),
            device_id_type=pl.DeviceIdType.MESH,
        )
        return carry

    lax.fori_loop(1, count, greet, 0)

    down_copy = pltpu.make_async_copy(d_hbm, down_v, down_sem)
    down_copy.start()

    acc_g[...] = jnp.zeros_like(acc_g)
    acc_u[...] = jnp.zeros_like(acc_u)

    def gate_up(x_v, g_v, u_v):
        for c in range(slots):
            xc = x_v[:, c, :]
            acc_g[c] += jnp.dot(xc, g_v[...], preferred_element_type=jnp.float32)
            acc_u[c] += jnp.dot(xc, u_v[...], preferred_element_type=jnp.float32)

    pltpu.emit_pipeline(
        gate_up,
        grid=(steps,),
        in_specs=[
            pl.BlockSpec((sources, slots, chunk), lambda k: (0, 0, k)),
            pl.BlockSpec((chunk, hidden), lambda k: (k, 0)),
            pl.BlockSpec((chunk, hidden), lambda k: (k, 0)),
        ],
    )(x_hbm, g_hbm, u_hbm)

    for c in range(slots):
        g = acc_g[c]
        inner[c] = (g / (1.0 + jnp.exp(-g)) * acc_u[c]).astype(jnp.bfloat16)

    down_copy.wait()
    pl.semaphore_wait(barrier, count - 1)

    parts = 2
    width = model_dim // parts

    def columns(part):
        return pl.ds(part * width, width)

    def outgoing(peer, part):
        return pltpu.make_async_remote_copy(
            src_ref=terms_ref.at[peer, :, columns(part)],
            dst_ref=y_ref.at[me, :, columns(part)],
            send_sem=send_sem.at[part, peer],
            recv_sem=recv_sem.at[part, me],
            device_id=(seg, peer),
            device_id_type=pl.DeviceIdType.MESH,
        )

    def incoming(peer, part):
        return pltpu.make_async_remote_copy(
            src_ref=terms_ref.at[me, :, columns(part)],
            dst_ref=y_ref.at[peer, :, columns(part)],
            send_sem=send_sem.at[part, peer],
            recv_sem=recv_sem.at[part, peer],
            device_id=(seg, peer),
            device_id_type=pl.DeviceIdType.MESH,
        )

    for part in range(parts):
        def down(o_v, part=part):
            for c in range(slots):
                o_v[:, c, :] = jnp.dot(
                    inner[c], down_v[:, columns(part)], preferred_element_type=jnp.float32
                ).astype(o_v.dtype)

        pltpu.emit_pipeline(
            down,
            grid=(1,),
            out_specs=[pl.BlockSpec((sources, slots, width), lambda k, part=part: (0, 0, part))],
        )(terms_ref)

        def send(d, carry, part=part):
            outgoing(lax.rem(me + d, count), part).start()
            return carry

        lax.fori_loop(1, count, send, 0)

    own = pltpu.make_async_copy(terms_ref.at[me], y_ref.at[me], own_sem)
    own.start()

    for part in range(parts):
        def finish(d, carry, part=part):
            outgoing(lax.rem(me + d, count), part).wait_send()
            incoming(lax.rem(me + count - d, count), part).wait_recv()
            return carry

        lax.fori_loop(1, count, finish, 0)
    own.wait()


def ffn_combine(x, gate_mat, up_mat, down_mat, collective_id):
    count, slots, model_dim = x.shape
    hidden = gate_mat.shape[1]
    chunk = 1024
    steps = model_dim // chunk
    back, _ = pl.pallas_call(
        functools.partial(ffn_combine_kernel, count, steps, chunk),
        out_shape=(
            jax.ShapeDtypeStruct(x.shape, jnp.bfloat16),
            jax.ShapeDtypeStruct(x.shape, jnp.bfloat16),
        ),
        in_specs=[pl.BlockSpec(memory_space=pl.ANY)] * 4,
        out_specs=(pl.BlockSpec(memory_space=pl.ANY), pl.BlockSpec(memory_space=pl.ANY)),
        scratch_shapes=[
            pltpu.VMEM((slots, count, hidden), jnp.float32),
            pltpu.VMEM((slots, count, hidden), jnp.float32),
            pltpu.VMEM((slots, count, hidden), jnp.bfloat16),
            pltpu.VMEM((hidden, model_dim), down_mat.dtype),
            pltpu.SemaphoreType.DMA((2, count)),
            pltpu.SemaphoreType.DMA((2, count)),
            pltpu.SemaphoreType.DMA,
            pltpu.SemaphoreType.DMA,
        ],
        compiler_params=pltpu.CompilerParams(collective_id=collective_id, has_side_effects=True),
    )(x, gate_mat, up_mat, down_mat)
    return back


def shifted(value, axis, steps):
    count = lax.axis_size(axis)
    pairs = [(source, (source + steps) % count) for source in range(count)]
    return lax.ppermute(value, axis, pairs)


def on_device(states, routing, route_weight, norm_gain, gate_proj, up_proj, down_proj):
    owners = lax.axis_size("expert")
    experts = owners // GROUP
    passes_count = routing.shape[1]
    row_dev = states.shape[1]
    capacity = 2
    gain_row = norm_gain[0]
    gate_mat = gate_proj[0]
    up_mat = up_proj[0]
    down_mat = down_proj[0]
    expert_ids = jnp.arange(experts, dtype=jnp.int32)
    slot_ids = jnp.arange(capacity, dtype=jnp.int32)
    owner_expert = jnp.arange(owners, dtype=jnp.int32) // GROUP

    current = states[0]
    for step_no in range(passes_count):
        chosen = routing[0, step_no]
        weights_now = route_weight[0, step_no]
        picked = chosen[:, :, None] == expert_ids[None, None, :]
        member = jnp.any(picked, axis=1)
        dense_weight = jnp.sum(
            jnp.where(picked, weights_now[:, :, None].astype(jnp.float32), jnp.float32(0.0)), axis=1
        )
        slot_rank = jnp.cumsum(member.astype(jnp.int32), axis=0) - 1
        placer = member.T[:, None, :] & (slot_rank.T[:, None, :] == slot_ids[None, :, None])
        placer_f = placer.astype(jnp.bfloat16)

        current_f = current.astype(jnp.float32)
        inv_rms = lax.rsqrt(jnp.mean(current_f * current_f, axis=1, keepdims=True) + 1e-06)
        normed = (current_f * inv_rms * gain_row).astype(jnp.bfloat16)

        packed = jnp.einsum(
            "jcr,rd->jcd", placer_f, normed, preferred_element_type=jnp.float32
        ).astype(jnp.bfloat16)
        packed_weight = jnp.sum(
            jnp.where(placer, dense_weight.T[:, None, :], jnp.float32(0.0)), axis=2
        )
        got = exchange(packed, owners, 0)
        back = ffn_combine(got, gate_mat, up_mat, down_mat, 1)
        slot_weight = jnp.where(placer, packed_weight[:, :, None], jnp.float32(0.0))
        back_weight = jnp.broadcast_to(
            slot_weight[:, None], (experts, GROUP) + slot_weight.shape[1:]
        ).reshape((owners,) + slot_weight.shape[1:]).astype(jnp.bfloat16)
        summed = jnp.einsum(
            "ocr,ocd->rd", back_weight, back, preferred_element_type=jnp.float32
        )
        updated = (current_f + summed).astype(jnp.bfloat16)
        current = shifted(updated, "segment", 1)
    return current[None]


def solution(mesh):
    return jax.shard_map(
        on_device,
        mesh=mesh,
        in_specs=(
            P("segment", "expert", None),
            P("segment", None, "expert", None),
            P("segment", None, "expert", None),
            P("segment", None),
            P("segment", None, "expert"),
            P("segment", None, "expert"),
            P("segment", "expert", None),
        ),
        out_specs=P("segment", "expert", None),
        check_vma=False,
    )
```

```python
import functools

import jax
import jax.numpy as jnp
from jax import lax
from jax.experimental import pallas as pl
from jax.experimental.pallas import tpu as pltpu
from jax.sharding import PartitionSpec as P

GROUP = 4


def exchange_kernel(count, spread, x_ref, y_ref, send_sem, recv_sem, own_sem):
    me = lax.axis_index("expert")
    seg = lax.axis_index("segment")

    barrier = pltpu.get_barrier_semaphore()

    def greet(d, carry):
        peer = lax.rem(me + d, count)
        pl.semaphore_signal(
            barrier, inc=1, device_id=(seg, peer), device_id_type=pl.DeviceIdType.MESH
        )
        return carry

    lax.fori_loop(1, count, greet, 0)
    pl.semaphore_wait(barrier, count - 1)

    own = pltpu.make_async_copy(x_ref.at[me // spread], y_ref.at[me], own_sem)
    own.start()

    def outgoing(peer):
        return pltpu.make_async_remote_copy(
            src_ref=x_ref.at[peer // spread],
            dst_ref=y_ref.at[me],
            send_sem=send_sem.at[peer],
            recv_sem=recv_sem.at[me],
            device_id=(seg, peer),
            device_id_type=pl.DeviceIdType.MESH,
        )

    def incoming(peer):
        return pltpu.make_async_remote_copy(
            src_ref=x_ref.at[me // spread],
            dst_ref=y_ref.at[peer],
            send_sem=send_sem.at[peer],
            recv_sem=recv_sem.at[peer],
            device_id=(seg, peer),
            device_id_type=pl.DeviceIdType.MESH,
        )

    def send(d, carry):
        outgoing(lax.rem(me + d, count)).start()
        return carry

    lax.fori_loop(1, count, send, 0)

    def finish(d, carry):
        outgoing(lax.rem(me + d, count)).wait_send()
        incoming(lax.rem(me + count - d, count)).wait_recv()
        return carry

    lax.fori_loop(1, count, finish, 0)
    own.wait()


def exchange(x, count, collective_id):
    spread = count // x.shape[0]
    return pl.pallas_call(
        functools.partial(exchange_kernel, count, spread),
        out_shape=jax.ShapeDtypeStruct((count,) + x.shape[1:], x.dtype),
        in_specs=[pl.BlockSpec(memory_space=pl.ANY)],
        out_specs=pl.BlockSpec(memory_space=pl.ANY),
        scratch_shapes=[
            pltpu.SemaphoreType.DMA((count,)),
            pltpu.SemaphoreType.DMA((count,)),
            pltpu.SemaphoreType.DMA,
        ],
        compiler_params=pltpu.CompilerParams(collective_id=collective_id, has_side_effects=True),
    )(x)


def ffn_kernel(x_ref, g_ref, u_ref, d_ref, o_ref, acc_g, acc_u):
    k = pl.program_id(0)

    @pl.when(k == 0)
    def _():
        acc_g[...] = jnp.zeros_like(acc_g)
        acc_u[...] = jnp.zeros_like(acc_u)

    for c in range(x_ref.shape[1]):
        xc = x_ref[:, c, :]
        acc_g[c] += jnp.dot(xc, g_ref[...], preferred_element_type=jnp.float32)
        acc_u[c] += jnp.dot(xc, u_ref[...], preferred_element_type=jnp.float32)

    @pl.when(k == pl.num_programs(0) - 1)
    def _():
        for c in range(x_ref.shape[1]):
            g = acc_g[c]
            inner = (g / (1.0 + jnp.exp(-g)) * acc_u[c]).astype(jnp.bfloat16)
            o_ref[:, c, :] = jnp.dot(
                inner, d_ref[...], preferred_element_type=jnp.float32
            ).astype(o_ref.dtype)


def expert_ffn(x, gate_mat, up_mat, down_mat):
    sources, slots, model_dim = x.shape
    hidden = gate_mat.shape[1]
    chunk = 1024
    rows = sources * slots
    return pl.pallas_call(
        ffn_kernel,
        grid=(model_dim // chunk,),
        in_specs=[
            pl.BlockSpec((sources, slots, chunk), lambda k: (0, 0, k)),
            pl.BlockSpec((chunk, hidden), lambda k: (k, 0)),
            pl.BlockSpec((chunk, hidden), lambda k: (k, 0)),
            pl.BlockSpec((hidden, model_dim), lambda k: (0, 0)),
        ],
        out_specs=pl.BlockSpec((sources, slots, model_dim), lambda k: (0, 0, 0)),
        out_shape=jax.ShapeDtypeStruct(x.shape, jnp.bfloat16),
        scratch_shapes=[
            pltpu.VMEM((slots, sources, hidden), jnp.float32),
            pltpu.VMEM((slots, sources, hidden), jnp.float32),
        ],
        cost_estimate=pl.CostEstimate(
            flops=6 * rows * model_dim * hidden,
            transcendentals=rows * hidden,
            bytes_accessed=3 * model_dim * hidden * 2 + 2 * rows * model_dim * 2,
        ),
    )(x, gate_mat, up_mat, down_mat)


def ffn_combine_kernel(count, steps, chunk, x_hbm, g_hbm, u_hbm, d_hbm, h_ref, w_ref,
                       y_ref, terms_ref, next_ref, stage_ref,
                       acc_g, acc_u, inner, down_v, y_v, h_v,
                       send_sem, recv_sem, own_sem, down_sem, y_sem, stage_sem, h_send_sem, h_recv_sem):
    me = lax.axis_index("expert")
    seg = lax.axis_index("segment")
    sections = lax.axis_size("segment")
    ahead = lax.rem(seg + 1, sections)
    behind = lax.rem(seg + sections - 1, sections)
    sources, slots = x_hbm.shape[0], x_hbm.shape[1]
    hidden = g_hbm.shape[1]
    model_dim = x_hbm.shape[2]

    barrier = pltpu.get_barrier_semaphore()

    def greet(d, carry):
        pl.semaphore_signal(
            barrier, inc=1, device_id=(seg, lax.rem(me + d, count)),
            device_id_type=pl.DeviceIdType.MESH,
        )
        return carry

    lax.fori_loop(1, count, greet, 0)
    for section in (ahead, behind):
        pl.semaphore_signal(
            barrier, inc=1, device_id=(section, me), device_id_type=pl.DeviceIdType.MESH
        )

    down_copy = pltpu.make_async_copy(d_hbm, down_v, down_sem)
    down_copy.start()

    acc_g[...] = jnp.zeros_like(acc_g)
    acc_u[...] = jnp.zeros_like(acc_u)

    def gate_up(x_v, g_v, u_v):
        for c in range(slots):
            xc = x_v[:, c, :]
            acc_g[c] += jnp.dot(xc, g_v[...], preferred_element_type=jnp.float32)
            acc_u[c] += jnp.dot(xc, u_v[...], preferred_element_type=jnp.float32)

    pltpu.emit_pipeline(
        gate_up,
        grid=(steps,),
        in_specs=[
            pl.BlockSpec((sources, slots, chunk), lambda k: (0, 0, k)),
            pl.BlockSpec((chunk, hidden), lambda k: (k, 0)),
            pl.BlockSpec((chunk, hidden), lambda k: (k, 0)),
        ],
    )(x_hbm, g_hbm, u_hbm)

    for c in range(slots):
        g = acc_g[c]
        inner[c] = (g / (1.0 + jnp.exp(-g)) * acc_u[c]).astype(jnp.bfloat16)

    down_copy.wait()

    def down(o_v):
        for c in range(slots):
            o_v[:, c, :] = jnp.dot(
                inner[c], down_v[...], preferred_element_type=jnp.float32
            ).astype(o_v.dtype)

    pltpu.emit_pipeline(
        down,
        grid=(1,),
        out_specs=[pl.BlockSpec((sources, slots, model_dim), lambda k: (0, 0, 0))],
    )(terms_ref)

    pl.semaphore_wait(barrier, count + 1)

    own = pltpu.make_async_copy(terms_ref.at[me], y_ref.at[me], own_sem)
    own.start()

    def outgoing(peer):
        return pltpu.make_async_remote_copy(
            src_ref=terms_ref.at[peer],
            dst_ref=y_ref.at[me],
            send_sem=send_sem.at[peer],
            recv_sem=recv_sem.at[me],
            device_id=(seg, peer),
            device_id_type=pl.DeviceIdType.MESH,
        )

    def incoming(peer):
        return pltpu.make_async_remote_copy(
            src_ref=terms_ref.at[me],
            dst_ref=y_ref.at[peer],
            send_sem=send_sem.at[peer],
            recv_sem=recv_sem.at[peer],
            device_id=(seg, peer),
            device_id_type=pl.DeviceIdType.MESH,
        )

    def send(d, carry):
        outgoing(lax.rem(me + d, count)).start()
        return carry

    lax.fori_loop(1, count, send, 0)

    def finish(d, carry):
        outgoing(lax.rem(me + d, count)).wait_send()
        incoming(lax.rem(me + count - d, count)).wait_recv()
        return carry

    lax.fori_loop(1, count, finish, 0)
    own.wait()

    y_copy = pltpu.make_async_copy(y_ref, y_v, y_sem)
    y_copy.start()
    y_copy.wait()
    for k in range(steps):
        cols = pl.ds(k * chunk, chunk)
        total = h_ref[:, cols].astype(jnp.float32)
        for c in range(slots):
            total = total + jnp.dot(w_ref[c], y_v[:, c, cols], preferred_element_type=jnp.float32)
        h_v[:, cols] = total.astype(h_v.dtype)

    stage = pltpu.make_async_copy(h_v, stage_ref, stage_sem)
    stage.start()
    stage.wait()
    moved = pltpu.make_async_remote_copy(
        src_ref=stage_ref,
        dst_ref=next_ref,
        send_sem=h_send_sem,
        recv_sem=h_recv_sem,
        device_id=(ahead, me),
        device_id_type=pl.DeviceIdType.MESH,
    )
    moved.start()
    moved.wait_send()
    arrived = pltpu.make_async_remote_copy(
        src_ref=stage_ref,
        dst_ref=next_ref,
        send_sem=h_send_sem,
        recv_sem=h_recv_sem,
        device_id=(behind, me),
        device_id_type=pl.DeviceIdType.MESH,
    )
    arrived.wait_recv()


def ffn_combine(x, gate_mat, up_mat, down_mat, h, weights, collective_id):
    count, slots, model_dim = x.shape
    hidden = gate_mat.shape[1]
    chunk = 1024
    steps = model_dim // chunk
    _, _, moved, _ = pl.pallas_call(
        functools.partial(ffn_combine_kernel, count, steps, chunk),
        out_shape=(
            jax.ShapeDtypeStruct(x.shape, jnp.bfloat16),
            jax.ShapeDtypeStruct(x.shape, jnp.bfloat16),
            jax.ShapeDtypeStruct(h.shape, h.dtype),
            jax.ShapeDtypeStruct(h.shape, h.dtype),
        ),
        in_specs=[pl.BlockSpec(memory_space=pl.ANY)] * 4
        + [pl.BlockSpec(memory_space=pltpu.VMEM)] * 2,
        out_specs=tuple(pl.BlockSpec(memory_space=pl.ANY) for _ in range(4)),
        scratch_shapes=[
            pltpu.VMEM((slots, count, hidden), jnp.float32),
            pltpu.VMEM((slots, count, hidden), jnp.float32),
            pltpu.VMEM((slots, count, hidden), jnp.bfloat16),
            pltpu.VMEM((hidden, model_dim), down_mat.dtype),
            pltpu.VMEM(x.shape, jnp.bfloat16),
            pltpu.VMEM(h.shape, h.dtype),
            pltpu.SemaphoreType.DMA((count,)),
            pltpu.SemaphoreType.DMA((count,)),
            pltpu.SemaphoreType.DMA,
            pltpu.SemaphoreType.DMA,
            pltpu.SemaphoreType.DMA,
            pltpu.SemaphoreType.DMA,
            pltpu.SemaphoreType.DMA,
            pltpu.SemaphoreType.DMA,
        ],
        compiler_params=pltpu.CompilerParams(collective_id=collective_id, has_side_effects=True),
    )(x, gate_mat, up_mat, down_mat, h, weights)
    return moved

def shifted(value, axis, steps):
    count = lax.axis_size(axis)
    pairs = [(source, (source + steps) % count) for source in range(count)]
    return lax.ppermute(value, axis, pairs)


def on_device(states, routing, route_weight, norm_gain, gate_proj, up_proj, down_proj):
    owners = lax.axis_size("expert")
    experts = owners // GROUP
    passes_count = routing.shape[1]
    row_dev = states.shape[1]
    capacity = 2
    gain_row = norm_gain[0]
    gate_mat = gate_proj[0]
    up_mat = up_proj[0]
    down_mat = down_proj[0]
    expert_ids = jnp.arange(experts, dtype=jnp.int32)
    slot_ids = jnp.arange(capacity, dtype=jnp.int32)
    owner_expert = jnp.arange(owners, dtype=jnp.int32) // GROUP

    current = states[0]
    for step_no in range(passes_count):
        chosen = routing[0, step_no]
        weights_now = route_weight[0, step_no]
        picked = chosen[:, :, None] == expert_ids[None, None, :]
        member = jnp.any(picked, axis=1)
        dense_weight = jnp.sum(
            jnp.where(picked, weights_now[:, :, None].astype(jnp.float32), jnp.float32(0.0)), axis=1
        )
        slot_rank = jnp.cumsum(member.astype(jnp.int32), axis=0) - 1
        placer = member.T[:, None, :] & (slot_rank.T[:, None, :] == slot_ids[None, :, None])
        placer_f = placer.astype(jnp.bfloat16)

        current_f = current.astype(jnp.float32)
        inv_rms = lax.rsqrt(jnp.mean(current_f * current_f, axis=1, keepdims=True) + 1e-06)
        normed = (current_f * inv_rms * gain_row).astype(jnp.bfloat16)

        packed = jnp.einsum(
            "jcr,rd->jcd", placer_f, normed, preferred_element_type=jnp.float32
        ).astype(jnp.bfloat16)
        packed_weight = jnp.sum(
            jnp.where(placer, dense_weight.T[:, None, :], jnp.float32(0.0)), axis=2
        )
        got = exchange(packed, owners, 0)
        slot_weight = jnp.where(placer, packed_weight[:, :, None], jnp.float32(0.0))
        weights = jnp.broadcast_to(
            slot_weight.transpose(1, 2, 0)[:, :, :, None], (capacity, row_dev, experts, GROUP)
        ).reshape(capacity, row_dev, owners).astype(jnp.bfloat16)
        current = ffn_combine(got, gate_mat, up_mat, down_mat, current, weights, 1 + step_no)
    return current[None]


def solution(mesh):
    return jax.shard_map(
        on_device,
        mesh=mesh,
        in_specs=(
            P("segment", "expert", None),
            P("segment", None, "expert", None),
            P("segment", None, "expert", None),
            P("segment", None),
            P("segment", None, "expert"),
            P("segment", None, "expert"),
            P("segment", "expert", None),
        ),
        out_specs=P("segment", "expert", None),
        check_vma=False,
    )
```

```python
import functools

import jax
import jax.numpy as jnp
from jax import lax
from jax.experimental import pallas as pl
from jax.experimental.pallas import tpu as pltpu
from jax.sharding import PartitionSpec as P

GROUP = 4


def exchange_kernel(count, spread, x_ref, y_ref, send_sem, recv_sem, own_sem):
    me = lax.axis_index("expert")
    seg = lax.axis_index("segment")

    barrier = pltpu.get_barrier_semaphore()

    def greet(d, carry):
        peer = lax.rem(me + d, count)
        pl.semaphore_signal(
            barrier, inc=1, device_id=(seg, peer), device_id_type=pl.DeviceIdType.MESH
        )
        return carry

    lax.fori_loop(1, count, greet, 0)
    pl.semaphore_wait(barrier, count - 1)

    own = pltpu.make_async_copy(x_ref.at[me // spread], y_ref.at[me], own_sem)
    own.start()

    def outgoing(peer):
        return pltpu.make_async_remote_copy(
            src_ref=x_ref.at[peer // spread],
            dst_ref=y_ref.at[me],
            send_sem=send_sem.at[peer],
            recv_sem=recv_sem.at[me],
            device_id=(seg, peer),
            device_id_type=pl.DeviceIdType.MESH,
        )

    def incoming(peer):
        return pltpu.make_async_remote_copy(
            src_ref=x_ref.at[me // spread],
            dst_ref=y_ref.at[peer],
            send_sem=send_sem.at[peer],
            recv_sem=recv_sem.at[peer],
            device_id=(seg, peer),
            device_id_type=pl.DeviceIdType.MESH,
        )

    def send(d, carry):
        outgoing(lax.rem(me + d, count)).start()
        return carry

    lax.fori_loop(1, count, send, 0)

    def finish(d, carry):
        outgoing(lax.rem(me + d, count)).wait_send()
        incoming(lax.rem(me + count - d, count)).wait_recv()
        return carry

    lax.fori_loop(1, count, finish, 0)
    own.wait()


def exchange(x, count, collective_id):
    spread = count // x.shape[0]
    return pl.pallas_call(
        functools.partial(exchange_kernel, count, spread),
        out_shape=jax.ShapeDtypeStruct((count,) + x.shape[1:], x.dtype),
        in_specs=[pl.BlockSpec(memory_space=pl.ANY)],
        out_specs=pl.BlockSpec(memory_space=pl.ANY),
        scratch_shapes=[
            pltpu.SemaphoreType.DMA((count,)),
            pltpu.SemaphoreType.DMA((count,)),
            pltpu.SemaphoreType.DMA,
        ],
        compiler_params=pltpu.CompilerParams(collective_id=collective_id, has_side_effects=True),
    )(x)


def ffn_kernel(x_ref, g_ref, u_ref, d_ref, o_ref, acc_g, acc_u):
    k = pl.program_id(0)

    @pl.when(k == 0)
    def _():
        acc_g[...] = jnp.zeros_like(acc_g)
        acc_u[...] = jnp.zeros_like(acc_u)

    for c in range(x_ref.shape[1]):
        xc = x_ref[:, c, :]
        acc_g[c] += jnp.dot(xc, g_ref[...], preferred_element_type=jnp.float32)
        acc_u[c] += jnp.dot(xc, u_ref[...], preferred_element_type=jnp.float32)

    @pl.when(k == pl.num_programs(0) - 1)
    def _():
        for c in range(x_ref.shape[1]):
            g = acc_g[c]
            inner = (g / (1.0 + jnp.exp(-g)) * acc_u[c]).astype(jnp.bfloat16)
            o_ref[:, c, :] = jnp.dot(
                inner, d_ref[...], preferred_element_type=jnp.float32
            ).astype(o_ref.dtype)


def expert_ffn(x, gate_mat, up_mat, down_mat):
    sources, slots, model_dim = x.shape
    hidden = gate_mat.shape[1]
    chunk = 1024
    rows = sources * slots
    return pl.pallas_call(
        ffn_kernel,
        grid=(model_dim // chunk,),
        in_specs=[
            pl.BlockSpec((sources, slots, chunk), lambda k: (0, 0, k)),
            pl.BlockSpec((chunk, hidden), lambda k: (k, 0)),
            pl.BlockSpec((chunk, hidden), lambda k: (k, 0)),
            pl.BlockSpec((hidden, model_dim), lambda k: (0, 0)),
        ],
        out_specs=pl.BlockSpec((sources, slots, model_dim), lambda k: (0, 0, 0)),
        out_shape=jax.ShapeDtypeStruct(x.shape, jnp.bfloat16),
        scratch_shapes=[
            pltpu.VMEM((slots, sources, hidden), jnp.float32),
            pltpu.VMEM((slots, sources, hidden), jnp.float32),
        ],
        cost_estimate=pl.CostEstimate(
            flops=6 * rows * model_dim * hidden,
            transcendentals=rows * hidden,
            bytes_accessed=3 * model_dim * hidden * 2 + 2 * rows * model_dim * 2,
        ),
    )(x, gate_mat, up_mat, down_mat)


def ffn_combine_kernel(count, steps, chunk, x_hbm, g_hbm, u_hbm, d_hbm, y_ref, terms_ref,
                       acc_g, acc_u, inner, down_v, send_sem, recv_sem, own_sem, down_sem):
    me = lax.axis_index("expert")
    seg = lax.axis_index("segment")
    sources, slots = x_hbm.shape[0], x_hbm.shape[1]
    hidden = g_hbm.shape[1]
    model_dim = x_hbm.shape[2]

    barrier = pltpu.get_barrier_semaphore()

    def greet(d, carry):
        pl.semaphore_signal(
            barrier, inc=1, device_id=(seg, lax.rem(me + d, count)),
            device_id_type=pl.DeviceIdType.MESH,
        )
        return carry

    lax.fori_loop(1, count, greet, 0)

    down_copy = pltpu.make_async_copy(d_hbm, down_v, down_sem)
    down_copy.start()

    acc_g[...] = jnp.zeros_like(acc_g)
    acc_u[...] = jnp.zeros_like(acc_u)

    def gate_up(x_v, g_v, u_v):
        for c in range(slots):
            xc = x_v[:, c, :]
            acc_g[c] += jnp.dot(xc, g_v[...], preferred_element_type=jnp.float32)
            acc_u[c] += jnp.dot(xc, u_v[...], preferred_element_type=jnp.float32)

    pltpu.emit_pipeline(
        gate_up,
        grid=(steps,),
        in_specs=[
            pl.BlockSpec((sources, slots, chunk), lambda k: (0, 0, k)),
            pl.BlockSpec((chunk, hidden), lambda k: (k, 0)),
            pl.BlockSpec((chunk, hidden), lambda k: (k, 0)),
        ],
    )(x_hbm, g_hbm, u_hbm)

    for c in range(slots):
        g = acc_g[c]
        inner[c] = (g / (1.0 + jnp.exp(-g)) * acc_u[c]).astype(jnp.bfloat16)

    down_copy.wait()

    def down(o_v):
        for c in range(slots):
            o_v[:, c, :] = jnp.dot(
                inner[c], down_v[...], preferred_element_type=jnp.float32
            ).astype(o_v.dtype)

    pltpu.emit_pipeline(
        down,
        grid=(1,),
        out_specs=[pl.BlockSpec((sources, slots, model_dim), lambda k: (0, 0, 0))],
    )(terms_ref)

    pl.semaphore_wait(barrier, count - 1)

    own = pltpu.make_async_copy(terms_ref.at[me], y_ref.at[me], own_sem)
    own.start()

    def outgoing(peer):
        return pltpu.make_async_remote_copy(
            src_ref=terms_ref.at[peer],
            dst_ref=y_ref.at[me],
            send_sem=send_sem.at[peer],
            recv_sem=recv_sem.at[me],
            device_id=(seg, peer),
            device_id_type=pl.DeviceIdType.MESH,
        )

    def incoming(peer):
        return pltpu.make_async_remote_copy(
            src_ref=terms_ref.at[me],
            dst_ref=y_ref.at[peer],
            send_sem=send_sem.at[peer],
            recv_sem=recv_sem.at[peer],
            device_id=(seg, peer),
            device_id_type=pl.DeviceIdType.MESH,
        )

    def send(d, carry):
        outgoing(lax.rem(me + d, count)).start()
        return carry

    lax.fori_loop(1, count, send, 0)

    def finish(d, carry):
        outgoing(lax.rem(me + d, count)).wait_send()
        incoming(lax.rem(me + count - d, count)).wait_recv()
        return carry

    lax.fori_loop(1, count, finish, 0)
    own.wait()


def ffn_combine(x, gate_mat, up_mat, down_mat, collective_id):
    count, slots, model_dim = x.shape
    hidden = gate_mat.shape[1]
    chunk = 1792
    steps = model_dim // chunk
    back, _ = pl.pallas_call(
        functools.partial(ffn_combine_kernel, count, steps, chunk),
        out_shape=(
            jax.ShapeDtypeStruct(x.shape, jnp.bfloat16),
            jax.ShapeDtypeStruct(x.shape, jnp.bfloat16),
        ),
        in_specs=[pl.BlockSpec(memory_space=pl.ANY)] * 4,
        out_specs=(pl.BlockSpec(memory_space=pl.ANY), pl.BlockSpec(memory_space=pl.ANY)),
        scratch_shapes=[
            pltpu.VMEM((slots, count, hidden), jnp.float32),
            pltpu.VMEM((slots, count, hidden), jnp.float32),
            pltpu.VMEM((slots, count, hidden), jnp.bfloat16),
            pltpu.VMEM((hidden, model_dim), down_mat.dtype),
            pltpu.SemaphoreType.DMA((count,)),
            pltpu.SemaphoreType.DMA((count,)),
            pltpu.SemaphoreType.DMA,
            pltpu.SemaphoreType.DMA,
        ],
        compiler_params=pltpu.CompilerParams(collective_id=collective_id, has_side_effects=True),
    )(x, gate_mat, up_mat, down_mat)
    return back


def shifted(value, axis, steps):
    count = lax.axis_size(axis)
    pairs = [(source, (source + steps) % count) for source in range(count)]
    return lax.ppermute(value, axis, pairs)


def on_device(states, routing, route_weight, norm_gain, gate_proj, up_proj, down_proj):
    owners = lax.axis_size("expert")
    experts = owners // GROUP
    passes_count = routing.shape[1]
    row_dev = states.shape[1]
    capacity = 2
    gain_row = norm_gain[0]
    gate_mat = gate_proj[0]
    up_mat = up_proj[0]
    down_mat = down_proj[0]
    expert_ids = jnp.arange(experts, dtype=jnp.int32)
    slot_ids = jnp.arange(capacity, dtype=jnp.int32)
    owner_expert = jnp.arange(owners, dtype=jnp.int32) // GROUP

    current = states[0]
    for step_no in range(passes_count):
        chosen = routing[0, step_no]
        weights_now = route_weight[0, step_no]
        picked = chosen[:, :, None] == expert_ids[None, None, :]
        member = jnp.any(picked, axis=1)
        dense_weight = jnp.sum(
            jnp.where(picked, weights_now[:, :, None].astype(jnp.float32), jnp.float32(0.0)), axis=1
        )
        slot_rank = jnp.cumsum(member.astype(jnp.int32), axis=0) - 1
        placer = member.T[:, None, :] & (slot_rank.T[:, None, :] == slot_ids[None, :, None])
        placer_f = placer.astype(jnp.bfloat16)

        current_f = current.astype(jnp.float32)
        inv_rms = lax.rsqrt(jnp.mean(current_f * current_f, axis=1, keepdims=True) + 1e-06)
        normed = (current_f * inv_rms * gain_row).astype(jnp.bfloat16)

        packed = jnp.einsum(
            "jcr,rd->jcd", placer_f, normed, preferred_element_type=jnp.float32
        ).astype(jnp.bfloat16)
        packed_weight = jnp.sum(
            jnp.where(placer, dense_weight.T[:, None, :], jnp.float32(0.0)), axis=2
        )
        got = exchange(packed, owners, 0)
        back = ffn_combine(got, gate_mat, up_mat, down_mat, 1)
        slot_weight = jnp.where(placer, packed_weight[:, :, None], jnp.float32(0.0))
        back_weight = jnp.broadcast_to(
            slot_weight[:, None], (experts, GROUP) + slot_weight.shape[1:]
        ).reshape((owners,) + slot_weight.shape[1:]).astype(jnp.bfloat16)
        summed = jnp.einsum(
            "ocr,ocd->rd", back_weight, back, preferred_element_type=jnp.float32
        )
        updated = (current_f + summed).astype(jnp.bfloat16)
        current = shifted(updated, "segment", 1)
    return current[None]


def solution(mesh):
    return jax.shard_map(
        on_device,
        mesh=mesh,
        in_specs=(
            P("segment", "expert", None),
            P("segment", None, "expert", None),
            P("segment", None, "expert", None),
            P("segment", None),
            P("segment", None, "expert"),
            P("segment", None, "expert"),
            P("segment", "expert", None),
        ),
        out_specs=P("segment", "expert", None),
        check_vma=False,
    )
```

```python
import functools

import jax
import jax.numpy as jnp
from jax import lax
from jax.experimental import pallas as pl
from jax.experimental.pallas import tpu as pltpu
from jax.sharding import PartitionSpec as P

GROUP = 4


def exchange_kernel(count, spread, x_ref, y_ref, send_sem, recv_sem, own_sem):
    me = lax.axis_index("expert")
    seg = lax.axis_index("segment")

    barrier = pltpu.get_barrier_semaphore()

    def greet(d, carry):
        peer = lax.rem(me + d, count)
        pl.semaphore_signal(
            barrier, inc=1, device_id=(seg, peer), device_id_type=pl.DeviceIdType.MESH
        )
        return carry

    lax.fori_loop(1, count, greet, 0)
    pl.semaphore_wait(barrier, count - 1)

    own = pltpu.make_async_copy(x_ref.at[me // spread], y_ref.at[me], own_sem)
    own.start()

    def outgoing(peer):
        return pltpu.make_async_remote_copy(
            src_ref=x_ref.at[peer // spread],
            dst_ref=y_ref.at[me],
            send_sem=send_sem.at[peer],
            recv_sem=recv_sem.at[me],
            device_id=(seg, peer),
            device_id_type=pl.DeviceIdType.MESH,
        )

    def incoming(peer):
        return pltpu.make_async_remote_copy(
            src_ref=x_ref.at[me // spread],
            dst_ref=y_ref.at[peer],
            send_sem=send_sem.at[peer],
            recv_sem=recv_sem.at[peer],
            device_id=(seg, peer),
            device_id_type=pl.DeviceIdType.MESH,
        )

    def send(d, carry):
        outgoing(lax.rem(me + d, count)).start()
        return carry

    lax.fori_loop(1, count, send, 0)

    def finish(d, carry):
        outgoing(lax.rem(me + d, count)).wait_send()
        incoming(lax.rem(me + count - d, count)).wait_recv()
        return carry

    lax.fori_loop(1, count, finish, 0)
    own.wait()


def exchange(x, count, collective_id):
    spread = count // x.shape[0]
    return pl.pallas_call(
        functools.partial(exchange_kernel, count, spread),
        out_shape=jax.ShapeDtypeStruct((count,) + x.shape[1:], x.dtype),
        in_specs=[pl.BlockSpec(memory_space=pl.ANY)],
        out_specs=pl.BlockSpec(memory_space=pl.ANY),
        scratch_shapes=[
            pltpu.SemaphoreType.DMA((count,)),
            pltpu.SemaphoreType.DMA((count,)),
            pltpu.SemaphoreType.DMA,
        ],
        compiler_params=pltpu.CompilerParams(collective_id=collective_id, has_side_effects=True),
    )(x)


def ffn_kernel(x_ref, g_ref, u_ref, d_ref, o_ref, acc_g, acc_u):
    k = pl.program_id(0)

    @pl.when(k == 0)
    def _():
        acc_g[...] = jnp.zeros_like(acc_g)
        acc_u[...] = jnp.zeros_like(acc_u)

    for c in range(x_ref.shape[1]):
        xc = x_ref[:, c, :]
        acc_g[c] += jnp.dot(xc, g_ref[...], preferred_element_type=jnp.float32)
        acc_u[c] += jnp.dot(xc, u_ref[...], preferred_element_type=jnp.float32)

    @pl.when(k == pl.num_programs(0) - 1)
    def _():
        for c in range(x_ref.shape[1]):
            g = acc_g[c]
            inner = (g / (1.0 + jnp.exp(-g)) * acc_u[c]).astype(jnp.bfloat16)
            o_ref[:, c, :] = jnp.dot(
                inner, d_ref[...], preferred_element_type=jnp.float32
            ).astype(o_ref.dtype)


def expert_ffn(x, gate_mat, up_mat, down_mat):
    sources, slots, model_dim = x.shape
    hidden = gate_mat.shape[1]
    chunk = 1024
    rows = sources * slots
    return pl.pallas_call(
        ffn_kernel,
        grid=(model_dim // chunk,),
        in_specs=[
            pl.BlockSpec((sources, slots, chunk), lambda k: (0, 0, k)),
            pl.BlockSpec((chunk, hidden), lambda k: (k, 0)),
            pl.BlockSpec((chunk, hidden), lambda k: (k, 0)),
            pl.BlockSpec((hidden, model_dim), lambda k: (0, 0)),
        ],
        out_specs=pl.BlockSpec((sources, slots, model_dim), lambda k: (0, 0, 0)),
        out_shape=jax.ShapeDtypeStruct(x.shape, jnp.bfloat16),
        scratch_shapes=[
            pltpu.VMEM((slots, sources, hidden), jnp.float32),
            pltpu.VMEM((slots, sources, hidden), jnp.float32),
        ],
        cost_estimate=pl.CostEstimate(
            flops=6 * rows * model_dim * hidden,
            transcendentals=rows * hidden,
            bytes_accessed=3 * model_dim * hidden * 2 + 2 * rows * model_dim * 2,
        ),
    )(x, gate_mat, up_mat, down_mat)


def ffn_combine_kernel(count, steps, chunk, x_hbm, g_hbm, u_hbm, d_hbm, y_ref, terms_ref,
                       acc_g, acc_u, inner, down_v, send_sem, recv_sem, own_sem, down_sem):
    me = lax.axis_index("expert")
    seg = lax.axis_index("segment")
    sources, slots = x_hbm.shape[0], x_hbm.shape[1]
    hidden = g_hbm.shape[1]
    model_dim = x_hbm.shape[2]

    barrier = pltpu.get_barrier_semaphore()

    def greet(d, carry):
        pl.semaphore_signal(
            barrier, inc=1, device_id=(seg, lax.rem(me + d, count)),
            device_id_type=pl.DeviceIdType.MESH,
        )
        return carry

    lax.fori_loop(1, count, greet, 0)

    down_copy = pltpu.make_async_copy(d_hbm, down_v, down_sem)
    down_copy.start()

    acc_g[...] = jnp.zeros_like(acc_g)
    acc_u[...] = jnp.zeros_like(acc_u)

    def gate_up(x_v, g_v, u_v):
        for c in range(slots):
            xc = x_v[:, c, :]
            acc_g[c] += jnp.dot(xc, g_v[...], preferred_element_type=jnp.float32)
            acc_u[c] += jnp.dot(xc, u_v[...], preferred_element_type=jnp.float32)

    pltpu.emit_pipeline(
        gate_up,
        grid=(steps,),
        in_specs=[
            pl.BlockSpec((sources, slots, chunk), lambda k: (0, 0, k)),
            pl.BlockSpec((chunk, hidden), lambda k: (k, 0)),
            pl.BlockSpec((chunk, hidden), lambda k: (k, 0)),
        ],
    )(x_hbm, g_hbm, u_hbm)

    for c in range(slots):
        g = acc_g[c]
        inner[c] = (g / (1.0 + jnp.exp(-g)) * acc_u[c]).astype(jnp.bfloat16)

    down_copy.wait()

    def down(o_v):
        for c in range(slots):
            o_v[:, c, :] = jnp.dot(
                inner[c], down_v[...], preferred_element_type=jnp.float32
            ).astype(o_v.dtype)

    pltpu.emit_pipeline(
        down,
        grid=(1,),
        out_specs=[pl.BlockSpec((sources, slots, model_dim), lambda k: (0, 0, 0))],
    )(terms_ref)

    pl.semaphore_wait(barrier, count - 1)

    own = pltpu.make_async_copy(terms_ref.at[me], y_ref.at[me], own_sem)
    own.start()

    def outgoing(peer):
        return pltpu.make_async_remote_copy(
            src_ref=terms_ref.at[peer],
            dst_ref=y_ref.at[me],
            send_sem=send_sem.at[peer],
            recv_sem=recv_sem.at[me],
            device_id=(seg, peer),
            device_id_type=pl.DeviceIdType.MESH,
        )

    def incoming(peer):
        return pltpu.make_async_remote_copy(
            src_ref=terms_ref.at[me],
            dst_ref=y_ref.at[peer],
            send_sem=send_sem.at[peer],
            recv_sem=recv_sem.at[peer],
            device_id=(seg, peer),
            device_id_type=pl.DeviceIdType.MESH,
        )

    def send(d, carry):
        outgoing(lax.rem(me + d, count)).start()
        return carry

    lax.fori_loop(1, count, send, 0)

    def finish(d, carry):
        outgoing(lax.rem(me + d, count)).wait_send()
        incoming(lax.rem(me + count - d, count)).wait_recv()
        return carry

    lax.fori_loop(1, count, finish, 0)
    own.wait()


def ffn_combine(x, gate_mat, up_mat, down_mat, collective_id):
    count, slots, model_dim = x.shape
    hidden = gate_mat.shape[1]
    chunk = 3584
    steps = model_dim // chunk
    back, _ = pl.pallas_call(
        functools.partial(ffn_combine_kernel, count, steps, chunk),
        out_shape=(
            jax.ShapeDtypeStruct(x.shape, jnp.bfloat16),
            jax.ShapeDtypeStruct(x.shape, jnp.bfloat16),
        ),
        in_specs=[pl.BlockSpec(memory_space=pl.ANY)] * 4,
        out_specs=(pl.BlockSpec(memory_space=pl.ANY), pl.BlockSpec(memory_space=pl.ANY)),
        scratch_shapes=[
            pltpu.VMEM((slots, count, hidden), jnp.float32),
            pltpu.VMEM((slots, count, hidden), jnp.float32),
            pltpu.VMEM((slots, count, hidden), jnp.bfloat16),
            pltpu.VMEM((hidden, model_dim), down_mat.dtype),
            pltpu.SemaphoreType.DMA((count,)),
            pltpu.SemaphoreType.DMA((count,)),
            pltpu.SemaphoreType.DMA,
            pltpu.SemaphoreType.DMA,
        ],
        compiler_params=pltpu.CompilerParams(collective_id=collective_id, has_side_effects=True),
    )(x, gate_mat, up_mat, down_mat)
    return back


def shifted(value, axis, steps):
    count = lax.axis_size(axis)
    pairs = [(source, (source + steps) % count) for source in range(count)]
    return lax.ppermute(value, axis, pairs)


def on_device(states, routing, route_weight, norm_gain, gate_proj, up_proj, down_proj):
    owners = lax.axis_size("expert")
    experts = owners // GROUP
    passes_count = routing.shape[1]
    row_dev = states.shape[1]
    capacity = 2
    gain_row = norm_gain[0]
    gate_mat = gate_proj[0]
    up_mat = up_proj[0]
    down_mat = down_proj[0]
    expert_ids = jnp.arange(experts, dtype=jnp.int32)
    slot_ids = jnp.arange(capacity, dtype=jnp.int32)
    owner_expert = jnp.arange(owners, dtype=jnp.int32) // GROUP

    current = states[0]
    for step_no in range(passes_count):
        chosen = routing[0, step_no]
        weights_now = route_weight[0, step_no]
        picked = chosen[:, :, None] == expert_ids[None, None, :]
        member = jnp.any(picked, axis=1)
        dense_weight = jnp.sum(
            jnp.where(picked, weights_now[:, :, None].astype(jnp.float32), jnp.float32(0.0)), axis=1
        )
        slot_rank = jnp.cumsum(member.astype(jnp.int32), axis=0) - 1
        placer = member.T[:, None, :] & (slot_rank.T[:, None, :] == slot_ids[None, :, None])
        placer_f = placer.astype(jnp.bfloat16)

        current_f = current.astype(jnp.float32)
        inv_rms = lax.rsqrt(jnp.mean(current_f * current_f, axis=1, keepdims=True) + 1e-06)
        normed = (current_f * inv_rms * gain_row).astype(jnp.bfloat16)

        packed = jnp.einsum(
            "jcr,rd->jcd", placer_f, normed, preferred_element_type=jnp.float32
        ).astype(jnp.bfloat16)
        packed_weight = jnp.sum(
            jnp.where(placer, dense_weight.T[:, None, :], jnp.float32(0.0)), axis=2
        )
        got = exchange(packed, owners, 0)
        back = ffn_combine(got, gate_mat, up_mat, down_mat, 1)
        slot_weight = jnp.where(placer, packed_weight[:, :, None], jnp.float32(0.0))
        back_weight = jnp.broadcast_to(
            slot_weight[:, None], (experts, GROUP) + slot_weight.shape[1:]
        ).reshape((owners,) + slot_weight.shape[1:]).astype(jnp.bfloat16)
        summed = jnp.einsum(
            "ocr,ocd->rd", back_weight, back, preferred_element_type=jnp.float32
        )
        updated = (current_f + summed).astype(jnp.bfloat16)
        current = shifted(updated, "segment", 1)
    return current[None]


def solution(mesh):
    return jax.shard_map(
        on_device,
        mesh=mesh,
        in_specs=(
            P("segment", "expert", None),
            P("segment", None, "expert", None),
            P("segment", None, "expert", None),
            P("segment", None),
            P("segment", None, "expert"),
            P("segment", None, "expert"),
            P("segment", "expert", None),
        ),
        out_specs=P("segment", "expert", None),
        check_vma=False,
    )
```

```python
import functools

import jax
import jax.numpy as jnp
from jax import lax
from jax.experimental import pallas as pl
from jax.experimental.pallas import tpu as pltpu
from jax.sharding import PartitionSpec as P

GROUP = 4


def exchange_kernel(count, spread, x_ref, y_ref, send_sem, recv_sem, own_sem):
    me = lax.axis_index("expert")
    seg = lax.axis_index("segment")

    barrier = pltpu.get_barrier_semaphore()

    def greet(d, carry):
        peer = lax.rem(me + d, count)
        pl.semaphore_signal(
            barrier, inc=1, device_id=(seg, peer), device_id_type=pl.DeviceIdType.MESH
        )
        return carry

    lax.fori_loop(1, count, greet, 0)
    pl.semaphore_wait(barrier, count - 1)

    own = pltpu.make_async_copy(x_ref.at[me // spread], y_ref.at[me], own_sem)
    own.start()

    def outgoing(peer):
        return pltpu.make_async_remote_copy(
            src_ref=x_ref.at[peer // spread],
            dst_ref=y_ref.at[me],
            send_sem=send_sem.at[peer],
            recv_sem=recv_sem.at[me],
            device_id=(seg, peer),
            device_id_type=pl.DeviceIdType.MESH,
        )

    def incoming(peer):
        return pltpu.make_async_remote_copy(
            src_ref=x_ref.at[me // spread],
            dst_ref=y_ref.at[peer],
            send_sem=send_sem.at[peer],
            recv_sem=recv_sem.at[peer],
            device_id=(seg, peer),
            device_id_type=pl.DeviceIdType.MESH,
        )

    def send(d, carry):
        outgoing(lax.rem(me + d, count)).start()
        return carry

    lax.fori_loop(1, count, send, 0)

    def finish(d, carry):
        outgoing(lax.rem(me + d, count)).wait_send()
        incoming(lax.rem(me + count - d, count)).wait_recv()
        return carry

    lax.fori_loop(1, count, finish, 0)
    own.wait()


def exchange(x, count, collective_id):
    spread = count // x.shape[0]
    return pl.pallas_call(
        functools.partial(exchange_kernel, count, spread),
        out_shape=jax.ShapeDtypeStruct((count,) + x.shape[1:], x.dtype),
        in_specs=[pl.BlockSpec(memory_space=pl.ANY)],
        out_specs=pl.BlockSpec(memory_space=pl.ANY),
        scratch_shapes=[
            pltpu.SemaphoreType.DMA((count,)),
            pltpu.SemaphoreType.DMA((count,)),
            pltpu.SemaphoreType.DMA,
        ],
        compiler_params=pltpu.CompilerParams(collective_id=collective_id, has_side_effects=True),
    )(x)


def ffn_kernel(x_ref, g_ref, u_ref, d_ref, o_ref, acc_g, acc_u):
    k = pl.program_id(0)

    @pl.when(k == 0)
    def _():
        acc_g[...] = jnp.zeros_like(acc_g)
        acc_u[...] = jnp.zeros_like(acc_u)

    for c in range(x_ref.shape[1]):
        xc = x_ref[:, c, :]
        acc_g[c] += jnp.dot(xc, g_ref[...], preferred_element_type=jnp.float32)
        acc_u[c] += jnp.dot(xc, u_ref[...], preferred_element_type=jnp.float32)

    @pl.when(k == pl.num_programs(0) - 1)
    def _():
        for c in range(x_ref.shape[1]):
            g = acc_g[c]
            inner = (g / (1.0 + jnp.exp(-g)) * acc_u[c]).astype(jnp.bfloat16)
            o_ref[:, c, :] = jnp.dot(
                inner, d_ref[...], preferred_element_type=jnp.float32
            ).astype(o_ref.dtype)


def expert_ffn(x, gate_mat, up_mat, down_mat):
    sources, slots, model_dim = x.shape
    hidden = gate_mat.shape[1]
    chunk = 1024
    rows = sources * slots
    return pl.pallas_call(
        ffn_kernel,
        grid=(model_dim // chunk,),
        in_specs=[
            pl.BlockSpec((sources, slots, chunk), lambda k: (0, 0, k)),
            pl.BlockSpec((chunk, hidden), lambda k: (k, 0)),
            pl.BlockSpec((chunk, hidden), lambda k: (k, 0)),
            pl.BlockSpec((hidden, model_dim), lambda k: (0, 0)),
        ],
        out_specs=pl.BlockSpec((sources, slots, model_dim), lambda k: (0, 0, 0)),
        out_shape=jax.ShapeDtypeStruct(x.shape, jnp.bfloat16),
        scratch_shapes=[
            pltpu.VMEM((slots, sources, hidden), jnp.float32),
            pltpu.VMEM((slots, sources, hidden), jnp.float32),
        ],
        cost_estimate=pl.CostEstimate(
            flops=6 * rows * model_dim * hidden,
            transcendentals=rows * hidden,
            bytes_accessed=3 * model_dim * hidden * 2 + 2 * rows * model_dim * 2,
        ),
    )(x, gate_mat, up_mat, down_mat)


def ffn_combine_kernel(count, steps, chunk, x_hbm, g_hbm, u_hbm, d_hbm, y_ref, terms_ref,
                       acc_g, acc_u, inner, down_v, x_v, g_v, u_v,
                       send_sem, recv_sem, own_sem, down_sem, in_sem):
    me = lax.axis_index("expert")
    seg = lax.axis_index("segment")
    sources, slots = x_hbm.shape[0], x_hbm.shape[1]
    hidden = g_hbm.shape[1]
    model_dim = x_hbm.shape[2]

    barrier = pltpu.get_barrier_semaphore()

    def greet(d, carry):
        pl.semaphore_signal(
            barrier, inc=1, device_id=(seg, lax.rem(me + d, count)),
            device_id_type=pl.DeviceIdType.MESH,
        )
        return carry

    lax.fori_loop(1, count, greet, 0)

    def chunk_copies(k):
        cols = pl.ds(k * chunk, chunk)
        return (
            pltpu.make_async_copy(x_hbm.at[:, :, cols], x_v.at[:, :, cols], in_sem.at[0, k]),
            pltpu.make_async_copy(g_hbm.at[cols], g_v.at[cols], in_sem.at[1, k]),
            pltpu.make_async_copy(u_hbm.at[cols], u_v.at[cols], in_sem.at[2, k]),
        )

    for k in range(steps):
        for copy in chunk_copies(k):
            copy.start()

    down_copy = pltpu.make_async_copy(d_hbm, down_v, down_sem)
    down_copy.start()

    acc_g[...] = jnp.zeros_like(acc_g)
    acc_u[...] = jnp.zeros_like(acc_u)

    for k in range(steps):
        for copy in chunk_copies(k):
            copy.wait()
        cols = pl.ds(k * chunk, chunk)
        for c in range(slots):
            xc = x_v[:, c, cols]
            acc_g[c] += jnp.dot(xc, g_v[cols, :], preferred_element_type=jnp.float32)
            acc_u[c] += jnp.dot(xc, u_v[cols, :], preferred_element_type=jnp.float32)

    for c in range(slots):
        g = acc_g[c]
        inner[c] = (g / (1.0 + jnp.exp(-g)) * acc_u[c]).astype(jnp.bfloat16)

    down_copy.wait()

    def down(o_v):
        for c in range(slots):
            o_v[:, c, :] = jnp.dot(
                inner[c], down_v[...], preferred_element_type=jnp.float32
            ).astype(o_v.dtype)

    pltpu.emit_pipeline(
        down,
        grid=(1,),
        out_specs=[pl.BlockSpec((sources, slots, model_dim), lambda k: (0, 0, 0))],
    )(terms_ref)

    pl.semaphore_wait(barrier, count - 1)

    own = pltpu.make_async_copy(terms_ref.at[me], y_ref.at[me], own_sem)
    own.start()

    def outgoing(peer):
        return pltpu.make_async_remote_copy(
            src_ref=terms_ref.at[peer],
            dst_ref=y_ref.at[me],
            send_sem=send_sem.at[peer],
            recv_sem=recv_sem.at[me],
            device_id=(seg, peer),
            device_id_type=pl.DeviceIdType.MESH,
        )

    def incoming(peer):
        return pltpu.make_async_remote_copy(
            src_ref=terms_ref.at[me],
            dst_ref=y_ref.at[peer],
            send_sem=send_sem.at[peer],
            recv_sem=recv_sem.at[peer],
            device_id=(seg, peer),
            device_id_type=pl.DeviceIdType.MESH,
        )

    def send(d, carry):
        outgoing(lax.rem(me + d, count)).start()
        return carry

    lax.fori_loop(1, count, send, 0)

    def finish(d, carry):
        outgoing(lax.rem(me + d, count)).wait_send()
        incoming(lax.rem(me + count - d, count)).wait_recv()
        return carry

    lax.fori_loop(1, count, finish, 0)
    own.wait()


def ffn_combine(x, gate_mat, up_mat, down_mat, collective_id):
    count, slots, model_dim = x.shape
    hidden = gate_mat.shape[1]
    chunk = 1792
    steps = model_dim // chunk
    back, _ = pl.pallas_call(
        functools.partial(ffn_combine_kernel, count, steps, chunk),
        out_shape=(
            jax.ShapeDtypeStruct(x.shape, jnp.bfloat16),
            jax.ShapeDtypeStruct(x.shape, jnp.bfloat16),
        ),
        in_specs=[pl.BlockSpec(memory_space=pl.ANY)] * 4,
        out_specs=(pl.BlockSpec(memory_space=pl.ANY), pl.BlockSpec(memory_space=pl.ANY)),
        scratch_shapes=[
            pltpu.VMEM((slots, count, hidden), jnp.float32),
            pltpu.VMEM((slots, count, hidden), jnp.float32),
            pltpu.VMEM((slots, count, hidden), jnp.bfloat16),
            pltpu.VMEM((hidden, model_dim), down_mat.dtype),
            pltpu.VMEM(x.shape, x.dtype),
            pltpu.VMEM(gate_mat.shape, gate_mat.dtype),
            pltpu.VMEM(up_mat.shape, up_mat.dtype),
            pltpu.SemaphoreType.DMA((count,)),
            pltpu.SemaphoreType.DMA((count,)),
            pltpu.SemaphoreType.DMA,
            pltpu.SemaphoreType.DMA,
            pltpu.SemaphoreType.DMA((3, steps)),
        ],
        compiler_params=pltpu.CompilerParams(collective_id=collective_id, has_side_effects=True),
    )(x, gate_mat, up_mat, down_mat)
    return back


def shifted(value, axis, steps):
    count = lax.axis_size(axis)
    pairs = [(source, (source + steps) % count) for source in range(count)]
    return lax.ppermute(value, axis, pairs)


def on_device(states, routing, route_weight, norm_gain, gate_proj, up_proj, down_proj):
    owners = lax.axis_size("expert")
    experts = owners // GROUP
    passes_count = routing.shape[1]
    row_dev = states.shape[1]
    capacity = 2
    gain_row = norm_gain[0]
    gate_mat = gate_proj[0]
    up_mat = up_proj[0]
    down_mat = down_proj[0]
    expert_ids = jnp.arange(experts, dtype=jnp.int32)
    slot_ids = jnp.arange(capacity, dtype=jnp.int32)
    owner_expert = jnp.arange(owners, dtype=jnp.int32) // GROUP

    current = states[0]
    for step_no in range(passes_count):
        chosen = routing[0, step_no]
        weights_now = route_weight[0, step_no]
        picked = chosen[:, :, None] == expert_ids[None, None, :]
        member = jnp.any(picked, axis=1)
        dense_weight = jnp.sum(
            jnp.where(picked, weights_now[:, :, None].astype(jnp.float32), jnp.float32(0.0)), axis=1
        )
        slot_rank = jnp.cumsum(member.astype(jnp.int32), axis=0) - 1
        placer = member.T[:, None, :] & (slot_rank.T[:, None, :] == slot_ids[None, :, None])
        placer_f = placer.astype(jnp.bfloat16)

        current_f = current.astype(jnp.float32)
        inv_rms = lax.rsqrt(jnp.mean(current_f * current_f, axis=1, keepdims=True) + 1e-06)
        normed = (current_f * inv_rms * gain_row).astype(jnp.bfloat16)

        packed = jnp.einsum(
            "jcr,rd->jcd", placer_f, normed, preferred_element_type=jnp.float32
        ).astype(jnp.bfloat16)
        packed_weight = jnp.sum(
            jnp.where(placer, dense_weight.T[:, None, :], jnp.float32(0.0)), axis=2
        )
        got = exchange(packed, owners, 0)
        back = ffn_combine(got, gate_mat, up_mat, down_mat, 1)
        slot_weight = jnp.where(placer, packed_weight[:, :, None], jnp.float32(0.0))
        back_weight = jnp.broadcast_to(
            slot_weight[:, None], (experts, GROUP) + slot_weight.shape[1:]
        ).reshape((owners,) + slot_weight.shape[1:]).astype(jnp.bfloat16)
        summed = jnp.einsum(
            "ocr,ocd->rd", back_weight, back, preferred_element_type=jnp.float32
        )
        updated = (current_f + summed).astype(jnp.bfloat16)
        current = shifted(updated, "segment", 1)
    return current[None]


def solution(mesh):
    return jax.shard_map(
        on_device,
        mesh=mesh,
        in_specs=(
            P("segment", "expert", None),
            P("segment", None, "expert", None),
            P("segment", None, "expert", None),
            P("segment", None),
            P("segment", None, "expert"),
            P("segment", None, "expert"),
            P("segment", "expert", None),
        ),
        out_specs=P("segment", "expert", None),
        check_vma=False,
    )
```

```python
import functools

import jax
import jax.numpy as jnp
from jax import lax
from jax.experimental import pallas as pl
from jax.experimental.pallas import tpu as pltpu
from jax.sharding import PartitionSpec as P

GROUP = 4


def exchange_kernel(count, spread, x_ref, y_ref, send_sem, recv_sem, own_sem):
    me = lax.axis_index("expert")
    seg = lax.axis_index("segment")

    barrier = pltpu.get_barrier_semaphore()

    def greet(d, carry):
        peer = lax.rem(me + d, count)
        pl.semaphore_signal(
            barrier, inc=1, device_id=(seg, peer), device_id_type=pl.DeviceIdType.MESH
        )
        return carry

    lax.fori_loop(1, count, greet, 0)
    pl.semaphore_wait(barrier, count - 1)

    own = pltpu.make_async_copy(x_ref.at[me // spread], y_ref.at[me], own_sem)
    own.start()

    def outgoing(peer):
        return pltpu.make_async_remote_copy(
            src_ref=x_ref.at[peer // spread],
            dst_ref=y_ref.at[me],
            send_sem=send_sem.at[peer],
            recv_sem=recv_sem.at[me],
            device_id=(seg, peer),
            device_id_type=pl.DeviceIdType.MESH,
        )

    def incoming(peer):
        return pltpu.make_async_remote_copy(
            src_ref=x_ref.at[me // spread],
            dst_ref=y_ref.at[peer],
            send_sem=send_sem.at[peer],
            recv_sem=recv_sem.at[peer],
            device_id=(seg, peer),
            device_id_type=pl.DeviceIdType.MESH,
        )

    def send(d, carry):
        outgoing(lax.rem(me + d, count)).start()
        return carry

    lax.fori_loop(1, count, send, 0)

    def finish(d, carry):
        outgoing(lax.rem(me + d, count)).wait_send()
        incoming(lax.rem(me + count - d, count)).wait_recv()
        return carry

    lax.fori_loop(1, count, finish, 0)
    own.wait()


def exchange(x, count, collective_id):
    spread = count // x.shape[0]
    return pl.pallas_call(
        functools.partial(exchange_kernel, count, spread),
        out_shape=jax.ShapeDtypeStruct((count,) + x.shape[1:], x.dtype),
        in_specs=[pl.BlockSpec(memory_space=pl.ANY)],
        out_specs=pl.BlockSpec(memory_space=pl.ANY),
        scratch_shapes=[
            pltpu.SemaphoreType.DMA((count,)),
            pltpu.SemaphoreType.DMA((count,)),
            pltpu.SemaphoreType.DMA,
        ],
        compiler_params=pltpu.CompilerParams(collective_id=collective_id, has_side_effects=True),
    )(x)


def ffn_kernel(x_ref, g_ref, u_ref, d_ref, o_ref, acc_g, acc_u):
    k = pl.program_id(0)

    @pl.when(k == 0)
    def _():
        acc_g[...] = jnp.zeros_like(acc_g)
        acc_u[...] = jnp.zeros_like(acc_u)

    for c in range(x_ref.shape[1]):
        xc = x_ref[:, c, :]
        acc_g[c] += jnp.dot(xc, g_ref[...], preferred_element_type=jnp.float32)
        acc_u[c] += jnp.dot(xc, u_ref[...], preferred_element_type=jnp.float32)

    @pl.when(k == pl.num_programs(0) - 1)
    def _():
        for c in range(x_ref.shape[1]):
            g = acc_g[c]
            inner = (g / (1.0 + jnp.exp(-g)) * acc_u[c]).astype(jnp.bfloat16)
            o_ref[:, c, :] = jnp.dot(
                inner, d_ref[...], preferred_element_type=jnp.float32
            ).astype(o_ref.dtype)


def expert_ffn(x, gate_mat, up_mat, down_mat):
    sources, slots, model_dim = x.shape
    hidden = gate_mat.shape[1]
    chunk = 1024
    rows = sources * slots
    return pl.pallas_call(
        ffn_kernel,
        grid=(model_dim // chunk,),
        in_specs=[
            pl.BlockSpec((sources, slots, chunk), lambda k: (0, 0, k)),
            pl.BlockSpec((chunk, hidden), lambda k: (k, 0)),
            pl.BlockSpec((chunk, hidden), lambda k: (k, 0)),
            pl.BlockSpec((hidden, model_dim), lambda k: (0, 0)),
        ],
        out_specs=pl.BlockSpec((sources, slots, model_dim), lambda k: (0, 0, 0)),
        out_shape=jax.ShapeDtypeStruct(x.shape, jnp.bfloat16),
        scratch_shapes=[
            pltpu.VMEM((slots, sources, hidden), jnp.float32),
            pltpu.VMEM((slots, sources, hidden), jnp.float32),
        ],
        cost_estimate=pl.CostEstimate(
            flops=6 * rows * model_dim * hidden,
            transcendentals=rows * hidden,
            bytes_accessed=3 * model_dim * hidden * 2 + 2 * rows * model_dim * 2,
        ),
    )(x, gate_mat, up_mat, down_mat)


def ffn_combine_kernel(count, steps, chunk, x_hbm, g_hbm, u_hbm, d_hbm, y_ref, terms_ref,
                       acc_g, acc_u, inner, down_v, x_v, g_v, u_v,
                       send_sem, recv_sem, own_sem, down_sem, in_sem):
    me = lax.axis_index("expert")
    seg = lax.axis_index("segment")
    sources, slots = x_hbm.shape[0], x_hbm.shape[1]
    hidden = g_hbm.shape[1]
    model_dim = x_hbm.shape[2]

    barrier = pltpu.get_barrier_semaphore()

    def greet(d, carry):
        pl.semaphore_signal(
            barrier, inc=1, device_id=(seg, lax.rem(me + d, count)),
            device_id_type=pl.DeviceIdType.MESH,
        )
        return carry

    lax.fori_loop(1, count, greet, 0)

    def chunk_copies(k):
        cols = pl.ds(k * chunk, chunk)
        return (
            pltpu.make_async_copy(x_hbm.at[:, :, cols], x_v.at[:, :, cols], in_sem.at[0, k]),
            pltpu.make_async_copy(g_hbm.at[cols], g_v.at[cols], in_sem.at[1, k]),
            pltpu.make_async_copy(u_hbm.at[cols], u_v.at[cols], in_sem.at[2, k]),
        )

    for k in range(steps):
        for copy in chunk_copies(k):
            copy.start()

    down_copy = pltpu.make_async_copy(d_hbm, down_v, down_sem)
    down_copy.start()

    acc_g[...] = jnp.zeros_like(acc_g)
    acc_u[...] = jnp.zeros_like(acc_u)

    for k in range(steps):
        for copy in chunk_copies(k):
            copy.wait()
        cols = pl.ds(k * chunk, chunk)
        for c in range(slots):
            xc = x_v[:, c, cols]
            acc_g[c] += jnp.dot(xc, g_v[cols, :], preferred_element_type=jnp.float32)
            acc_u[c] += jnp.dot(xc, u_v[cols, :], preferred_element_type=jnp.float32)

    for c in range(slots):
        g = acc_g[c]
        inner[c] = (g / (1.0 + jnp.exp(-g)) * acc_u[c]).astype(jnp.bfloat16)

    down_copy.wait()

    def down(o_v):
        for c in range(slots):
            o_v[:, c, :] = jnp.dot(
                inner[c], down_v[...], preferred_element_type=jnp.float32
            ).astype(o_v.dtype)

    pltpu.emit_pipeline(
        down,
        grid=(1,),
        out_specs=[pl.BlockSpec((sources, slots, model_dim), lambda k: (0, 0, 0))],
    )(terms_ref)

    pl.semaphore_wait(barrier, count - 1)

    own = pltpu.make_async_copy(terms_ref.at[me], y_ref.at[me], own_sem)
    own.start()

    def outgoing(peer):
        return pltpu.make_async_remote_copy(
            src_ref=terms_ref.at[peer],
            dst_ref=y_ref.at[me],
            send_sem=send_sem.at[peer],
            recv_sem=recv_sem.at[me],
            device_id=(seg, peer),
            device_id_type=pl.DeviceIdType.MESH,
        )

    def incoming(peer):
        return pltpu.make_async_remote_copy(
            src_ref=terms_ref.at[me],
            dst_ref=y_ref.at[peer],
            send_sem=send_sem.at[peer],
            recv_sem=recv_sem.at[peer],
            device_id=(seg, peer),
            device_id_type=pl.DeviceIdType.MESH,
        )

    def send(d, carry):
        outgoing(lax.rem(me + d, count)).start()
        return carry

    lax.fori_loop(1, count, send, 0)

    def finish(d, carry):
        outgoing(lax.rem(me + d, count)).wait_send()
        incoming(lax.rem(me + count - d, count)).wait_recv()
        return carry

    lax.fori_loop(1, count, finish, 0)
    own.wait()


def ffn_combine(x, gate_mat, up_mat, down_mat, collective_id):
    count, slots, model_dim = x.shape
    hidden = gate_mat.shape[1]
    chunk = 1024
    steps = model_dim // chunk
    back, _ = pl.pallas_call(
        functools.partial(ffn_combine_kernel, count, steps, chunk),
        out_shape=(
            jax.ShapeDtypeStruct(x.shape, jnp.bfloat16),
            jax.ShapeDtypeStruct(x.shape, jnp.bfloat16),
        ),
        in_specs=[pl.BlockSpec(memory_space=pl.ANY)] * 4,
        out_specs=(pl.BlockSpec(memory_space=pl.ANY), pl.BlockSpec(memory_space=pl.ANY)),
        scratch_shapes=[
            pltpu.VMEM((slots, count, hidden), jnp.float32),
            pltpu.VMEM((slots, count, hidden), jnp.float32),
            pltpu.VMEM((slots, count, hidden), jnp.bfloat16),
            pltpu.VMEM((hidden, model_dim), down_mat.dtype),
            pltpu.VMEM(x.shape, x.dtype),
            pltpu.VMEM(gate_mat.shape, gate_mat.dtype),
            pltpu.VMEM(up_mat.shape, up_mat.dtype),
            pltpu.SemaphoreType.DMA((count,)),
            pltpu.SemaphoreType.DMA((count,)),
            pltpu.SemaphoreType.DMA,
            pltpu.SemaphoreType.DMA,
            pltpu.SemaphoreType.DMA((3, steps)),
        ],
        compiler_params=pltpu.CompilerParams(collective_id=collective_id, has_side_effects=True),
    )(x, gate_mat, up_mat, down_mat)
    return back


def shifted(value, axis, steps):
    count = lax.axis_size(axis)
    pairs = [(source, (source + steps) % count) for source in range(count)]
    return lax.ppermute(value, axis, pairs)


def on_device(states, routing, route_weight, norm_gain, gate_proj, up_proj, down_proj):
    owners = lax.axis_size("expert")
    experts = owners // GROUP
    passes_count = routing.shape[1]
    row_dev = states.shape[1]
    capacity = 2
    gain_row = norm_gain[0]
    gate_mat = gate_proj[0]
    up_mat = up_proj[0]
    down_mat = down_proj[0]
    expert_ids = jnp.arange(experts, dtype=jnp.int32)
    slot_ids = jnp.arange(capacity, dtype=jnp.int32)
    owner_expert = jnp.arange(owners, dtype=jnp.int32) // GROUP

    current = states[0]
    for step_no in range(passes_count):
        chosen = routing[0, step_no]
        weights_now = route_weight[0, step_no]
        picked = chosen[:, :, None] == expert_ids[None, None, :]
        member = jnp.any(picked, axis=1)
        dense_weight = jnp.sum(
            jnp.where(picked, weights_now[:, :, None].astype(jnp.float32), jnp.float32(0.0)), axis=1
        )
        slot_rank = jnp.cumsum(member.astype(jnp.int32), axis=0) - 1
        placer = member.T[:, None, :] & (slot_rank.T[:, None, :] == slot_ids[None, :, None])
        placer_f = placer.astype(jnp.bfloat16)

        current_f = current.astype(jnp.float32)
        inv_rms = lax.rsqrt(jnp.mean(current_f * current_f, axis=1, keepdims=True) + 1e-06)
        normed = (current_f * inv_rms * gain_row).astype(jnp.bfloat16)

        packed = jnp.einsum(
            "jcr,rd->jcd", placer_f, normed, preferred_element_type=jnp.float32
        ).astype(jnp.bfloat16)
        packed_weight = jnp.sum(
            jnp.where(placer, dense_weight.T[:, None, :], jnp.float32(0.0)), axis=2
        )
        got = exchange(packed, owners, 0)
        back = ffn_combine(got, gate_mat, up_mat, down_mat, 1)
        slot_weight = jnp.where(placer, packed_weight[:, :, None], jnp.float32(0.0))
        back_weight = jnp.broadcast_to(
            slot_weight[:, None], (experts, GROUP) + slot_weight.shape[1:]
        ).reshape((owners,) + slot_weight.shape[1:]).astype(jnp.bfloat16)
        summed = jnp.einsum(
            "ocr,ocd->rd", back_weight, back, preferred_element_type=jnp.float32
        )
        updated = (current_f + summed).astype(jnp.bfloat16)
        current = shifted(updated, "segment", 1)
    return current[None]


def solution(mesh):
    return jax.shard_map(
        on_device,
        mesh=mesh,
        in_specs=(
            P("segment", "expert", None),
            P("segment", None, "expert", None),
            P("segment", None, "expert", None),
            P("segment", None),
            P("segment", None, "expert"),
            P("segment", None, "expert"),
            P("segment", "expert", None),
        ),
        out_specs=P("segment", "expert", None),
        check_vma=False,
    )
```

```python
import functools

import jax
import jax.numpy as jnp
from jax import lax
from jax.experimental import pallas as pl
from jax.experimental.pallas import tpu as pltpu
from jax.sharding import PartitionSpec as P

GROUP = 4


def exchange_kernel(count, spread, x_ref, y_ref, send_sem, recv_sem, own_sem):
    me = lax.axis_index("expert")
    seg = lax.axis_index("segment")

    barrier = pltpu.get_barrier_semaphore()

    def greet(d, carry):
        peer = lax.rem(me + d, count)
        pl.semaphore_signal(
            barrier, inc=1, device_id=(seg, peer), device_id_type=pl.DeviceIdType.MESH
        )
        return carry

    lax.fori_loop(1, count, greet, 0)
    pl.semaphore_wait(barrier, count - 1)

    own = pltpu.make_async_copy(x_ref.at[me // spread], y_ref.at[me], own_sem)
    own.start()

    def outgoing(peer):
        return pltpu.make_async_remote_copy(
            src_ref=x_ref.at[peer // spread],
            dst_ref=y_ref.at[me],
            send_sem=send_sem.at[peer],
            recv_sem=recv_sem.at[me],
            device_id=(seg, peer),
            device_id_type=pl.DeviceIdType.MESH,
        )

    def incoming(peer):
        return pltpu.make_async_remote_copy(
            src_ref=x_ref.at[me // spread],
            dst_ref=y_ref.at[peer],
            send_sem=send_sem.at[peer],
            recv_sem=recv_sem.at[peer],
            device_id=(seg, peer),
            device_id_type=pl.DeviceIdType.MESH,
        )

    def send(d, carry):
        outgoing(lax.rem(me + d, count)).start()
        return carry

    lax.fori_loop(1, count, send, 0)

    def finish(d, carry):
        outgoing(lax.rem(me + d, count)).wait_send()
        incoming(lax.rem(me + count - d, count)).wait_recv()
        return carry

    lax.fori_loop(1, count, finish, 0)
    own.wait()


def exchange(x, count, collective_id):
    spread = count // x.shape[0]
    return pl.pallas_call(
        functools.partial(exchange_kernel, count, spread),
        out_shape=jax.ShapeDtypeStruct((count,) + x.shape[1:], x.dtype),
        in_specs=[pl.BlockSpec(memory_space=pl.ANY)],
        out_specs=pl.BlockSpec(memory_space=pl.ANY),
        scratch_shapes=[
            pltpu.SemaphoreType.DMA((count,)),
            pltpu.SemaphoreType.DMA((count,)),
            pltpu.SemaphoreType.DMA,
        ],
        compiler_params=pltpu.CompilerParams(collective_id=collective_id, has_side_effects=True),
    )(x)


def ffn_kernel(x_ref, g_ref, u_ref, d_ref, o_ref, acc_g, acc_u):
    k = pl.program_id(0)

    @pl.when(k == 0)
    def _():
        acc_g[...] = jnp.zeros_like(acc_g)
        acc_u[...] = jnp.zeros_like(acc_u)

    for c in range(x_ref.shape[1]):
        xc = x_ref[:, c, :]
        acc_g[c] += jnp.dot(xc, g_ref[...], preferred_element_type=jnp.float32)
        acc_u[c] += jnp.dot(xc, u_ref[...], preferred_element_type=jnp.float32)

    @pl.when(k == pl.num_programs(0) - 1)
    def _():
        for c in range(x_ref.shape[1]):
            g = acc_g[c]
            inner = (g / (1.0 + jnp.exp(-g)) * acc_u[c]).astype(jnp.bfloat16)
            o_ref[:, c, :] = jnp.dot(
                inner, d_ref[...], preferred_element_type=jnp.float32
            ).astype(o_ref.dtype)


def expert_ffn(x, gate_mat, up_mat, down_mat):
    sources, slots, model_dim = x.shape
    hidden = gate_mat.shape[1]
    chunk = 1024
    rows = sources * slots
    return pl.pallas_call(
        ffn_kernel,
        grid=(model_dim // chunk,),
        in_specs=[
            pl.BlockSpec((sources, slots, chunk), lambda k: (0, 0, k)),
            pl.BlockSpec((chunk, hidden), lambda k: (k, 0)),
            pl.BlockSpec((chunk, hidden), lambda k: (k, 0)),
            pl.BlockSpec((hidden, model_dim), lambda k: (0, 0)),
        ],
        out_specs=pl.BlockSpec((sources, slots, model_dim), lambda k: (0, 0, 0)),
        out_shape=jax.ShapeDtypeStruct(x.shape, jnp.bfloat16),
        scratch_shapes=[
            pltpu.VMEM((slots, sources, hidden), jnp.float32),
            pltpu.VMEM((slots, sources, hidden), jnp.float32),
        ],
        cost_estimate=pl.CostEstimate(
            flops=6 * rows * model_dim * hidden,
            transcendentals=rows * hidden,
            bytes_accessed=3 * model_dim * hidden * 2 + 2 * rows * model_dim * 2,
        ),
    )(x, gate_mat, up_mat, down_mat)


def ffn_combine_kernel(count, steps, chunk, x_hbm, g_hbm, u_hbm, d_hbm, y_ref, terms_ref,
                       acc_g, acc_u, inner, down_v, x_v, g_v, u_v, t_v,
                       send_sem, recv_sem, own_sem, down_sem, in_sem):
    me = lax.axis_index("expert")
    seg = lax.axis_index("segment")
    sources, slots = x_hbm.shape[0], x_hbm.shape[1]
    hidden = g_hbm.shape[1]
    model_dim = x_hbm.shape[2]

    barrier = pltpu.get_barrier_semaphore()

    def greet(d, carry):
        pl.semaphore_signal(
            barrier, inc=1, device_id=(seg, lax.rem(me + d, count)),
            device_id_type=pl.DeviceIdType.MESH,
        )
        return carry

    lax.fori_loop(1, count, greet, 0)

    def chunk_copies(k):
        cols = pl.ds(k * chunk, chunk)
        return (
            pltpu.make_async_copy(x_hbm.at[:, :, cols], x_v.at[:, :, cols], in_sem.at[0, k]),
            pltpu.make_async_copy(g_hbm.at[cols], g_v.at[cols], in_sem.at[1, k]),
            pltpu.make_async_copy(u_hbm.at[cols], u_v.at[cols], in_sem.at[2, k]),
        )

    for k in range(steps):
        for copy in chunk_copies(k):
            copy.start()

    down_copy = pltpu.make_async_copy(d_hbm, down_v, down_sem)
    down_copy.start()

    acc_g[...] = jnp.zeros_like(acc_g)
    acc_u[...] = jnp.zeros_like(acc_u)

    for k in range(steps):
        for copy in chunk_copies(k):
            copy.wait()
        cols = pl.ds(k * chunk, chunk)
        for c in range(slots):
            xc = x_v[:, c, cols]
            acc_g[c] += jnp.dot(xc, g_v[cols, :], preferred_element_type=jnp.float32)
            acc_u[c] += jnp.dot(xc, u_v[cols, :], preferred_element_type=jnp.float32)

    for c in range(slots):
        g = acc_g[c]
        inner[c] = (g / (1.0 + jnp.exp(-g)) * acc_u[c]).astype(jnp.bfloat16)

    down_copy.wait()

    for c in range(slots):
        t_v[:, c, :] = jnp.dot(
            inner[c], down_v[...], preferred_element_type=jnp.float32
        ).astype(t_v.dtype)
    terms_out = pltpu.make_async_copy(t_v, terms_ref, down_sem)
    terms_out.start()
    terms_out.wait()

    pl.semaphore_wait(barrier, count - 1)

    own = pltpu.make_async_copy(terms_ref.at[me], y_ref.at[me], own_sem)
    own.start()

    def outgoing(peer):
        return pltpu.make_async_remote_copy(
            src_ref=terms_ref.at[peer],
            dst_ref=y_ref.at[me],
            send_sem=send_sem.at[peer],
            recv_sem=recv_sem.at[me],
            device_id=(seg, peer),
            device_id_type=pl.DeviceIdType.MESH,
        )

    def incoming(peer):
        return pltpu.make_async_remote_copy(
            src_ref=terms_ref.at[me],
            dst_ref=y_ref.at[peer],
            send_sem=send_sem.at[peer],
            recv_sem=recv_sem.at[peer],
            device_id=(seg, peer),
            device_id_type=pl.DeviceIdType.MESH,
        )

    def send(d, carry):
        outgoing(lax.rem(me + d, count)).start()
        return carry

    lax.fori_loop(1, count, send, 0)

    def finish(d, carry):
        outgoing(lax.rem(me + d, count)).wait_send()
        incoming(lax.rem(me + count - d, count)).wait_recv()
        return carry

    lax.fori_loop(1, count, finish, 0)
    own.wait()


def ffn_combine(x, gate_mat, up_mat, down_mat, collective_id):
    count, slots, model_dim = x.shape
    hidden = gate_mat.shape[1]
    chunk = 1792
    steps = model_dim // chunk
    back, _ = pl.pallas_call(
        functools.partial(ffn_combine_kernel, count, steps, chunk),
        out_shape=(
            jax.ShapeDtypeStruct(x.shape, jnp.bfloat16),
            jax.ShapeDtypeStruct(x.shape, jnp.bfloat16),
        ),
        in_specs=[pl.BlockSpec(memory_space=pl.ANY)] * 4,
        out_specs=(pl.BlockSpec(memory_space=pl.ANY), pl.BlockSpec(memory_space=pl.ANY)),
        scratch_shapes=[
            pltpu.VMEM((slots, count, hidden), jnp.float32),
            pltpu.VMEM((slots, count, hidden), jnp.float32),
            pltpu.VMEM((slots, count, hidden), jnp.bfloat16),
            pltpu.VMEM((hidden, model_dim), down_mat.dtype),
            pltpu.VMEM(x.shape, x.dtype),
            pltpu.VMEM(gate_mat.shape, gate_mat.dtype),
            pltpu.VMEM(up_mat.shape, up_mat.dtype),
            pltpu.VMEM(x.shape, jnp.bfloat16),
            pltpu.SemaphoreType.DMA((count,)),
            pltpu.SemaphoreType.DMA((count,)),
            pltpu.SemaphoreType.DMA,
            pltpu.SemaphoreType.DMA,
            pltpu.SemaphoreType.DMA((3, steps)),
        ],
        compiler_params=pltpu.CompilerParams(collective_id=collective_id, has_side_effects=True),
    )(x, gate_mat, up_mat, down_mat)
    return back


def shifted(value, axis, steps):
    count = lax.axis_size(axis)
    pairs = [(source, (source + steps) % count) for source in range(count)]
    return lax.ppermute(value, axis, pairs)


def on_device(states, routing, route_weight, norm_gain, gate_proj, up_proj, down_proj):
    owners = lax.axis_size("expert")
    experts = owners // GROUP
    passes_count = routing.shape[1]
    row_dev = states.shape[1]
    capacity = 2
    gain_row = norm_gain[0]
    gate_mat = gate_proj[0]
    up_mat = up_proj[0]
    down_mat = down_proj[0]
    expert_ids = jnp.arange(experts, dtype=jnp.int32)
    slot_ids = jnp.arange(capacity, dtype=jnp.int32)
    owner_expert = jnp.arange(owners, dtype=jnp.int32) // GROUP

    current = states[0]
    for step_no in range(passes_count):
        chosen = routing[0, step_no]
        weights_now = route_weight[0, step_no]
        picked = chosen[:, :, None] == expert_ids[None, None, :]
        member = jnp.any(picked, axis=1)
        dense_weight = jnp.sum(
            jnp.where(picked, weights_now[:, :, None].astype(jnp.float32), jnp.float32(0.0)), axis=1
        )
        slot_rank = jnp.cumsum(member.astype(jnp.int32), axis=0) - 1
        placer = member.T[:, None, :] & (slot_rank.T[:, None, :] == slot_ids[None, :, None])
        placer_f = placer.astype(jnp.bfloat16)

        current_f = current.astype(jnp.float32)
        inv_rms = lax.rsqrt(jnp.mean(current_f * current_f, axis=1, keepdims=True) + 1e-06)
        normed = (current_f * inv_rms * gain_row).astype(jnp.bfloat16)

        packed = jnp.einsum(
            "jcr,rd->jcd", placer_f, normed, preferred_element_type=jnp.float32
        ).astype(jnp.bfloat16)
        packed_weight = jnp.sum(
            jnp.where(placer, dense_weight.T[:, None, :], jnp.float32(0.0)), axis=2
        )
        got = exchange(packed, owners, 0)
        back = ffn_combine(got, gate_mat, up_mat, down_mat, 1)
        slot_weight = jnp.where(placer, packed_weight[:, :, None], jnp.float32(0.0))
        back_weight = jnp.broadcast_to(
            slot_weight[:, None], (experts, GROUP) + slot_weight.shape[1:]
        ).reshape((owners,) + slot_weight.shape[1:]).astype(jnp.bfloat16)
        summed = jnp.einsum(
            "ocr,ocd->rd", back_weight, back, preferred_element_type=jnp.float32
        )
        updated = (current_f + summed).astype(jnp.bfloat16)
        current = shifted(updated, "segment", 1)
    return current[None]


def solution(mesh):
    return jax.shard_map(
        on_device,
        mesh=mesh,
        in_specs=(
            P("segment", "expert", None),
            P("segment", None, "expert", None),
            P("segment", None, "expert", None),
            P("segment", None),
            P("segment", None, "expert"),
            P("segment", None, "expert"),
            P("segment", "expert", None),
        ),
        out_specs=P("segment", "expert", None),
        check_vma=False,
    )
```
